32 devices in a mesh: rows: 4 (over x, core), cols: 8 (over z, y).
Axes of the slice: x: 2, y: 2, z: 4, core: 2. Of those that a mesh axis runs over, the one named last changes fastest.
Arguments:
- features: bfloat16 [1024, 512], P(('rows', 'cols')), may hold values from -0.59765625 to 0.59765625
- positions: float32 [3, 1024], P(None, ('rows', 'cols')), may hold values from 0 to 1, as said below
- cell_lengths: float32 [3], replicated, may hold values from 30 to 60
- block_lists: int32 [32, 8], P(('rows', 'cols')), may hold values from 0 to 31, as said below
- image_offsets: int32 [3, 32, 8], P(None, ('rows', 'cols')), may hold values from -1 to 1
- block_valid: int32 [32, 8], P(('rows', 'cols')), may hold values from 0 to 1, as said below
- norm_gain: float32 [512], replicated, may hold values from 0.1 to 1.9
- w_qkv: bfloat16 [512, 1536], replicated, may hold values from -1 to 1
- w_out: bfloat16 [512, 512], replicated, may hold values from -0.25 to 0.25
- rbf_weight: float32 [16, 64], replicated, may hold values from -5 to 5
- rbf_offset: float32 [64], replicated, may hold values from -4 to 4
- pair_weight: float32 [64, 16], replicated, may hold values from -30 to 30
- cosine_scale: float32 [16], replicated, may hold values from -80 to 80, as said below
Outputs:
- updated: bfloat16 [1024, 512], P(('rows', 'cols'))
The draws below stay inside these ranges and needn't reach their ends.
Inputs may be any that keep to these rules, and one draw needn't show every extreme that they name: `block_lists`: block b lies at grid row b // 8 and column b % 8. Every entry names a block whose row and column each differ from b's by at most one, counted around the grid; the first entry is b itself and the entries of a block differ. `block_valid`: the first entry of every block is 1 and a block's ones come before its zeros; some block has all 8 entries 1. `positions`: atoms of block b have their first coordinate within [r, r + 1] / 4 and their second within [c, c + 1] / 8, with r = b // 8 and c = b % 8. `cosine_scale`: every magnitude is 0.3 or more.
All inputs are finite; a program needn't handle non-finite values.
Results may differ from the reference program's by a relative error of at most 0.012.
The reference program's roundings to bfloat16 on the way (of `normed`, `packed`, `local_out`, `global_out` and `combined`) count: a program that leaves them out, or rounds other values in their place, can miss the bound.
Values may be sent and summed in bfloat16 or wider, within the bound.
No kernel may reach another device: no remote copies, remote signals or barrier semaphores. Data moves between devices by JAX's collectives and lax.ppermute only.
A program may use at most 64 MiB of HBM per device.

```python
import math
import jax
import jax.numpy as jnp
import numpy as np
from jax import lax

D = 512
H = 16
PAIR = 64
NRBF = 16
LIST = 8
ATOM_DEV = 32
GROWS = 4
GCOLS = 8
BLOCKS = 32
ATOMS = 1024


neighbour_moves = np.array([[-1, -1], [-1, 0], [-1, 1], [0, -1], [0, 1], [1, -1], [1, 0], [1, 1]], dtype=np.int32)


def draw_positions(key, part):
    fraction = jax.random.uniform(key, (3, ATOMS), jnp.float32)
    block_ids = jnp.arange(ATOMS, dtype=jnp.int32) // ATOM_DEV
    row_of = (block_ids // GCOLS).astype(jnp.float32)
    col_of = (block_ids % GCOLS).astype(jnp.float32)
    return jnp.stack([(row_of + fraction[0]) / GROWS, (col_of + fraction[1]) / GCOLS, fraction[2]])


def draw_block_lists(key, part):
    scores = jax.random.randint(key, (BLOCKS, 8), 0, 1 << 20) * 8 + jnp.arange(8, dtype=jnp.int32)[None, :]
    picked = jnp.argsort(scores, axis=1, stable=True)[:, :LIST - 1]
    moves = jnp.asarray(neighbour_moves)[picked]
    block_ids = jnp.arange(BLOCKS, dtype=jnp.int32)
    row_of = block_ids // GCOLS
    col_of = block_ids % GCOLS
    listed = (row_of[:, None] + moves[:, :, 0]) % GROWS * GCOLS + (col_of[:, None] + moves[:, :, 1]) % GCOLS
    return jnp.concatenate([block_ids[:, None], listed], axis=1).astype(jnp.int32)


def draw_block_valid(key, part):
    extra = jax.random.randint(key, (BLOCKS,), 2, LIST)
    extra = jnp.where(jnp.arange(BLOCKS) == 0, LIST - 1, extra)
    return (jnp.arange(LIST, dtype=jnp.int32)[None, :] <= extra[:, None]).astype(jnp.int32)


def draw_w_qkv(key, part):
    columns = jnp.arange(3 * D, dtype=jnp.int32)
    spread = jnp.where(columns < 2 * D, 2.3, 1.0).astype(jnp.float32) / math.sqrt(D)
    base = jnp.clip(jax.random.normal(jax.random.fold_in(key, 5), (D, 3 * D), jnp.float32), -4.0, 4.0)
    return jnp.clip(base * spread[None, :], -1.0, 1.0).astype(jnp.bfloat16)


def draw_pair_weight(key, part):
    base = jnp.clip(jax.random.normal(jax.random.fold_in(key, 1), (PAIR, H), jnp.float32), -4.0, 4.0) / math.sqrt(PAIR)
    upper = 3.0
    scales = jnp.exp(jax.random.uniform(jax.random.fold_in(key, 2), (H,), jnp.float32, math.log(0.5), math.log(upper)))
    return jnp.clip(base * scales[None, :], -30.0, 30.0)


def draw_cosine_scale(key, part):
    upper = 24.0
    magnitude = jnp.exp(jax.random.uniform(jax.random.fold_in(key, 3), (H,), jnp.float32, math.log(0.3), math.log(upper)))
    order = jax.random.permutation(jax.random.fold_in(key, 4), H)
    signs = jnp.where(order < H // 2, -1.0, 1.0).astype(jnp.float32)
    return magnitude * signs


def with_ends(values, stream_key, smallest, high):
    dims = values.shape
    place = [jax.random.randint(jax.random.fold_in(stream_key, axis), (), 0, dims[axis]) for axis in range(len(dims))]
    values = values.at[tuple(place)].set(smallest)
    longest = dims.index(max(dims))
    place[longest] = (place[longest] + 1) % dims[longest]
    return values.at[tuple(place)].set(high)


def shard_levels(rng, extent, shards, low, largest):
    loudness, own = 1.0, jax.random.fold_in(rng, 6)
    for axis_at, parts in shards:
        steps = jnp.exp(jax.random.uniform(jax.random.fold_in(own, axis_at), (parts,), jnp.float32, low / len(shards), largest / len(shards)))
        loudness = loudness * jnp.repeat(steps, extent[axis_at] // parts).reshape([-1 if axis == axis_at else 1 for axis in range(len(extent))])
    return loudness


def centred(rng, extent, scale, bound, shards=(), kind=jnp.bfloat16):
    loudness = shard_levels(rng, extent, shards, -0.22, 0.18) if shards else 1.0
    values = jax.random.normal(rng, extent, jnp.float32) * scale * loudness
    return jnp.minimum(jnp.maximum(values, -bound), bound).astype(kind)


def setup_inputs(seed: int = 0) -> dict:
    splits = jax.random.split(jax.random.key(seed), 14)
    features = centred(splits[0], (ATOMS, D), 0.1, 0.59765625, ((0, 32),))
    positions = draw_positions(jax.random.fold_in(splits[13], 71), 0)
    cell_lengths = jnp.clip(jnp.exp(jax.random.uniform(splits[2], (3,), jnp.float32, math.log(30.0), math.log(60.0))), 30.0, 60.0)
    block_lists = draw_block_lists(jax.random.fold_in(splits[13], 71), 0)
    image_offsets = with_ends(jax.random.randint(splits[4], (3, BLOCKS, LIST), -1, 2), jax.random.fold_in(splits[4], 1), -1, 1).astype(jnp.int32)
    block_valid = draw_block_valid(jax.random.fold_in(splits[13], 71), 0)
    norm_gain = jnp.clip(1.0 + 0.18 * jax.random.normal(splits[6], (D,), jnp.float32), 0.1, 1.9)
    w_qkv = draw_w_qkv(jax.random.fold_in(splits[13], 71), 0)
    w_out = centred(splits[8], (D, D), D ** -0.5, 0.25)
    rbf_weight = centred(splits[9], (NRBF, PAIR), 1.0, 5.0, (), jnp.float32)
    rbf_offset = centred(splits[10], (PAIR,), 1.0, 4.0, (), jnp.float32)
    pair_weight = draw_pair_weight(jax.random.fold_in(splits[13], 71), 0)
    cosine_scale = draw_cosine_scale(jax.random.fold_in(splits[13], 71), 0)
    return {"features": features, "positions": positions, "cell_lengths": cell_lengths, "block_lists": block_lists, "image_offsets": image_offsets, "block_valid": block_valid, "norm_gain": norm_gain, "w_qkv": w_qkv, "w_out": w_out, "rbf_weight": rbf_weight, "rbf_offset": rbf_offset, "pair_weight": pair_weight, "cosine_scale": cosine_scale}


rbf_step = 2.0
rbf_width = 2.0
two_pi = 2.0 * math.pi
highest = lax.Precision.HIGHEST

def rounded(value):
    return lax.optimization_barrier(value.astype(jnp.bfloat16))

def rms_rows(values, norm_gain):
    floats = values.astype(jnp.float32)
    spread = lax.optimization_barrier(jnp.mean(floats * floats, axis=-1, keepdims=True))
    return rounded(floats * lax.rsqrt(spread + 1e-06) * norm_gain)

def near_attention(query_rows, own_pos, keys, key_pos, shifts, live, cell_lengths, rbf_weight, rbf_offset, pair_weight):
    entries, block_len = (keys.shape[0], keys.shape[1])
    model_dim = query_rows.shape[1]
    head_count = pair_weight.shape[1]
    head_dim = model_dim // head_count
    key_coords = key_pos.transpose(1, 0, 2) + shifts.astype(jnp.float32)[:, :, None]
    key_coords = key_coords.reshape(3, entries * block_len)
    displace = (key_coords[:, None, :] - own_pos[:, :, None]) * cell_lengths[:, None, None]
    distance = jnp.sqrt(lax.optimization_barrier(jnp.sum(displace * displace, axis=0)) + 0.25)
    centers = jnp.arange(rbf_weight.shape[0], dtype=jnp.float32) * rbf_step
    radial = jnp.exp(-(distance[None] - centers[:, None, None]) ** 2 * (0.5 / rbf_width ** 2))
    radial = radial.reshape(rbf_weight.shape[0], -1)
    hidden = jax.nn.silu(jnp.dot(rbf_weight.T, radial, precision=highest) + rbf_offset[:, None])
    pair_bias = jnp.dot(pair_weight.T, hidden, precision=highest).reshape(head_count, query_rows.shape[0], entries * block_len)
    query_heads = query_rows.reshape(-1, head_count, head_dim).astype(jnp.float32)
    key_heads = keys[:, :, :model_dim].reshape(entries * block_len, head_count, head_dim).astype(jnp.float32)
    value_heads = keys[:, :, model_dim:].reshape(entries * block_len, head_count, head_dim).astype(jnp.float32)
    scores = jnp.einsum('ahd,khd->hak', query_heads, key_heads, precision=highest) * head_dim ** (-0.5) + pair_bias
    allowed = jnp.repeat(live > 0, block_len)
    scores = jnp.where(allowed[None, None, :], scores, -1e+30)
    row_max = lax.optimization_barrier(jnp.max(scores, axis=-1, keepdims=True))
    weights = jnp.exp(scores - row_max)
    row_sum = lax.optimization_barrier(jnp.sum(weights, axis=-1, keepdims=True))
    prob_bf = rounded(weights).astype(jnp.float32)
    attended = jnp.einsum('hak,khd->ahd', prob_bf, value_heads, precision=highest) / row_sum.transpose(1, 0, 2)
    return rounded(attended.reshape(-1, model_dim))

def reference(features, positions, cell_lengths, block_lists, image_offsets, block_valid, norm_gain, w_qkv, w_out, rbf_weight, rbf_offset, pair_weight, cosine_scale):
    model_dim = features.shape[1]
    head_count = pair_weight.shape[1]
    head_dim = model_dim // head_count
    normed = rms_rows(features, norm_gain)
    packed = rounded(jnp.dot(normed, w_qkv, preferred_element_type=jnp.float32))
    kv_blocks = packed[:, model_dim:].reshape(BLOCKS, ATOM_DEV, 2 * model_dim)
    query_blocks = packed[:, :model_dim].reshape(BLOCKS, ATOM_DEV, model_dim)
    pos_blocks = positions.reshape(3, BLOCKS, ATOM_DEV).transpose(1, 0, 2)
    shift_blocks = image_offsets.transpose(1, 0, 2)

    def one_block(inputs):
        query_rows, own_pos, listed, shifts, live = inputs
        return near_attention(query_rows, own_pos, kv_blocks[listed], pos_blocks[listed], shifts, live, cell_lengths, rbf_weight, rbf_offset, pair_weight)
    local_out = lax.map(one_block, (query_blocks, pos_blocks, block_lists, shift_blocks, block_valid)).reshape(ATOMS, model_dim)
    angles = two_pi * positions
    coord_feats = jnp.concatenate([jnp.cos(angles), jnp.sin(angles)], axis=0)
    heads_first = packed.reshape(ATOMS, 3, head_count, head_dim).transpose(1, 2, 0, 3)
    query_len = ATOM_DEV * GCOLS

    def one_head(inputs):
        query_all, key_all, value_all, strength = inputs
        key_f = key_all.astype(jnp.float32)
        value_f = value_all.astype(jnp.float32)

        def one_rows(block_in):
            query_rows, query_feats = block_in
            scores = jnp.dot(query_rows.astype(jnp.float32), key_f.T, precision=highest) * head_dim ** (-0.5)
            scores = scores + strength * jnp.dot(query_feats.T, coord_feats, precision=highest)
            row_max = lax.optimization_barrier(jnp.max(scores, axis=-1, keepdims=True))
            weights = jnp.exp(scores - row_max)
            row_sum = lax.optimization_barrier(jnp.sum(weights, axis=-1))
            prob_bf = rounded(weights).astype(jnp.float32)
            return rounded(jnp.dot(prob_bf, value_f, precision=highest) / row_sum[:, None])
        query_split = query_all.reshape(ATOMS // query_len, query_len, head_dim)
        feat_split = coord_feats.reshape(6, ATOMS // query_len, query_len).transpose(1, 0, 2)
        return lax.map(one_rows, (query_split, feat_split)).reshape(ATOMS, head_dim)
    global_heads = lax.map(one_head, (heads_first[0], heads_first[1], heads_first[2], cosine_scale))
    global_out = global_heads.transpose(1, 0, 2).reshape(ATOMS, model_dim)
    combined = rounded(local_out.astype(jnp.float32) + global_out.astype(jnp.float32))
    updated = features.astype(jnp.float32) + jnp.dot(combined, w_out, preferred_element_type=jnp.float32)
    return updated.astype(jnp.bfloat16)
```

```python
import functools
import math

import jax
import jax.numpy as jnp
from jax import lax
from jax.experimental import pallas as pl
from jax.experimental.pallas import tpu as pltpu
from jax.sharding import PartitionSpec as P

rbf_step = 2.0
rbf_width = 2.0
two_pi = 2.0 * math.pi
highest = lax.Precision.HIGHEST


def with_halo(cells, sides, width):
    for axis, dim in sides:
        count = lax.axis_size(axis)
        head = lax.slice_in_dim(cells, 0, width, axis=dim)
        tail = lax.slice_in_dim(cells, cells.shape[dim] - width, cells.shape[dim], axis=dim)
        cells = jnp.concatenate(
            [
                lax.ppermute(tail, axis, [(i, (i + 1) % count) for i in range(count)]),
                cells,
                lax.ppermute(head, axis, [((i + 1) % count, i) for i in range(count)]),
            ],
            axis=dim,
        )
    return cells


def rms_rows(values, norm_gain):
    floats = values.astype(jnp.float32)
    spread = jnp.mean(floats * floats, axis=-1, keepdims=True)
    return (floats * lax.rsqrt(spread + 1e-06) * norm_gain).astype(jnp.bfloat16)


def near_attention(
    query_rows,
    own_pos,
    keys,
    key_pos,
    shifts,
    live,
    cell_lengths,
    rbf_weight,
    rbf_offset,
    pair_weight,
):
    entries, block_len = (keys.shape[0], keys.shape[1])
    model_dim = query_rows.shape[1]
    head_count = pair_weight.shape[1]
    head_dim = model_dim // head_count
    key_coords = key_pos.transpose(1, 0, 2) + shifts.astype(jnp.float32)[:, :, None]
    key_coords = key_coords.reshape(3, entries * block_len)
    displace = (key_coords[:, None, :] - own_pos[:, :, None]) * cell_lengths[:, None, None]
    distance = jnp.sqrt(jnp.sum(displace * displace, axis=0) + 0.25)
    centers = jnp.arange(rbf_weight.shape[0], dtype=jnp.float32) * rbf_step
    radial = jnp.exp(-((distance[None] - centers[:, None, None]) ** 2) * (0.5 / rbf_width**2))
    radial = radial.reshape(rbf_weight.shape[0], -1)
    hidden = jax.nn.silu(jnp.dot(rbf_weight.T, radial, precision=highest) + rbf_offset[:, None])
    pair_bias = jnp.dot(pair_weight.T, hidden, precision=highest).reshape(
        head_count, query_rows.shape[0], entries * block_len
    )
    query_heads = query_rows.reshape(-1, head_count, head_dim)
    key_heads = keys[:, :, :model_dim].reshape(entries * block_len, head_count, head_dim)
    value_heads = keys[:, :, model_dim:].reshape(entries * block_len, head_count, head_dim)
    scores = (
        jnp.einsum("ahd,khd->hak", query_heads, key_heads, preferred_element_type=jnp.float32)
        * head_dim ** (-0.5)
        + pair_bias
    )
    allowed = jnp.repeat(live > 0, block_len)
    scores = jnp.where(allowed[None, None, :], scores, -1e30)
    row_max = jnp.max(scores, axis=-1, keepdims=True)
    weights = jnp.exp(scores - row_max)
    row_sum = jnp.sum(weights, axis=-1, keepdims=True)
    prob_bf = weights.astype(jnp.bfloat16)
    attended = jnp.einsum(
        "hak,khd->ahd", prob_bf, value_heads, preferred_element_type=jnp.float32
    ) / row_sum.transpose(1, 0, 2)
    return attended.reshape(-1, model_dim).astype(jnp.bfloat16)


def on_device(
    features,
    positions,
    cell_lengths,
    block_lists,
    image_offsets,
    block_valid,
    norm_gain,
    w_qkv,
    w_out,
    rbf_weight,
    rbf_offset,
    pair_weight,
    cosine_scale,
):
    atom_count, model_dim = features.shape
    head_count = pair_weight.shape[1]
    head_dim = model_dim // head_count
    row_count = lax.axis_size("rows")
    col_count = lax.axis_size("cols")
    row_index = lax.axis_index("rows")
    col_index = lax.axis_index("cols")
    per_dev = head_count // row_count
    normed = rms_rows(features, norm_gain)
    packed = jnp.dot(normed, w_qkv, preferred_element_type=jnp.float32).astype(jnp.bfloat16)
    every_pos = lax.all_gather(positions, ("rows", "cols"), axis=1, tiled=True)
    near_rows = with_halo(normed[None, None], (("rows", 0), ("cols", 1)), 1)
    near_kv = jnp.dot(
        near_rows.reshape(9 * atom_count, model_dim),
        w_qkv[:, model_dim:],
        preferred_element_type=jnp.float32,
    )
    near_kv = near_kv.astype(jnp.bfloat16).reshape(9, atom_count, 2 * model_dim)
    listed = block_lists[0]
    list_row = listed // col_count
    list_col = listed % col_count
    slots = (list_row - row_index + 1) % row_count * 3 + (list_col - col_index + 1) % col_count
    keys = jnp.take(near_kv, slots, axis=0)
    block_pos = every_pos.reshape(3, row_count * col_count, atom_count)
    key_pos = jnp.take(block_pos, listed, axis=1).transpose(1, 0, 2)
    local_out = near_attention(
        packed[:, :model_dim],
        positions,
        keys,
        key_pos,
        image_offsets[:, 0, :],
        block_valid[0],
        cell_lengths,
        rbf_weight,
        rbf_offset,
        pair_weight,
    )
    grouped = (
        packed.reshape(atom_count, 3, head_count, head_dim)
        .transpose(1, 2, 0, 3)
        .reshape(3, head_count, atom_count * head_dim)
    )
    regrouped = lax.all_to_all(grouped, "rows", split_axis=1, concat_axis=2, tiled=True)
    query_count = row_count * atom_count
    queries = regrouped[0].reshape(per_dev, query_count, head_dim)
    key_vals = regrouped[1:]
    cycle_pos = (
        every_pos.reshape(3, row_count, col_count, atom_count).transpose(0, 2, 1, 3).reshape(3, -1)
    )
    query_pos = lax.dynamic_slice_in_dim(cycle_pos, col_index * query_count, query_count, 1)
    cycle_feats = jnp.concatenate(
        [jnp.cos(two_pi * cycle_pos), jnp.sin(two_pi * cycle_pos)], axis=0
    )
    query_feats = jnp.concatenate(
        [jnp.cos(two_pi * query_pos), jnp.sin(two_pi * query_pos)], axis=0
    )
    strengths = lax.dynamic_slice_in_dim(cosine_scale, row_index * per_dev, per_dev)
    scale = head_dim ** (-0.5)

    def update(state, kv_block, key_start, block_len):
        run_max, run_sum, accum = state
        scores = (
            jnp.einsum("hqd,hkd->hqk", queries, kv_block[0], preferred_element_type=jnp.float32)
            * scale
        )
        coords = lax.dynamic_slice_in_dim(cycle_feats, key_start, block_len, 1)
        cos_bias = jnp.dot(query_feats.T, coords, precision=highest)
        scores = scores + strengths[:, None, None] * cos_bias[None]
        new_max = jnp.maximum(run_max, jnp.max(scores, axis=-1))
        keep_part = jnp.exp(run_max - new_max)
        weights = jnp.exp(scores - new_max[:, :, None])
        run_sum = run_sum * keep_part + jnp.sum(weights, axis=-1)
        prob_bf = weights.astype(jnp.bfloat16)
        accum = accum * keep_part[:, None, :] + jnp.einsum(
            "hqk,hkd->hdq", prob_bf, kv_block[1], preferred_element_type=jnp.float32
        )
        return (new_max, run_sum, accum)

    initial = (
        jnp.full((per_dev, query_count), -1e30, jnp.float32),
        jnp.zeros((per_dev, query_count), jnp.float32),
        jnp.zeros((per_dev, head_dim, query_count), jnp.float32),
    )
    piece = lax.all_gather(key_vals, "cols", axis=2, tiled=True)
    key_total = piece.shape[2] // head_dim
    if key_total > 1024 and key_total % 1024 == 0:
        block_len = 1024
    else:
        block_len = key_total
    block_count = key_total // block_len
    kv_blocks = piece.reshape(2, per_dev, block_count, block_len, head_dim).transpose(2, 0, 1, 3, 4)
    block_starts = jnp.arange(block_count, dtype=jnp.int32) * block_len

    def one_block(state, block_in):
        kv_block, key_start = block_in
        return (update(state, kv_block, key_start, block_len), None)

    state, _ = lax.scan(one_block, initial, (kv_blocks, block_starts))
    run_max, run_sum, accum = state
    head_out = (
        (accum / run_sum[:, None, :])
        .transpose(0, 2, 1)
        .astype(jnp.bfloat16)
        .reshape(per_dev, query_count * head_dim)
    )
    returned = lax.all_to_all(head_out, "rows", split_axis=1, concat_axis=0, tiled=True)
    global_out = (
        returned.reshape(head_count, atom_count, head_dim)
        .transpose(1, 0, 2)
        .reshape(atom_count, model_dim)
    )
    combined = (local_out.astype(jnp.float32) + global_out.astype(jnp.float32)).astype(jnp.bfloat16)
    updated = features.astype(jnp.float32) + jnp.dot(
        combined, w_out, preferred_element_type=jnp.float32
    )
    return updated.astype(jnp.bfloat16)


def mm(a, b, dims):
    return lax.dot_general(a, b, (dims, ((), ())), preferred_element_type=jnp.float32)


def parts_of(value, count):
    out = []
    for _ in range(count):
        part = value.astype(jnp.bfloat16)
        out.append(part)
        value = value - part.astype(jnp.float32)
    return out


def unit(rows, cols, dtype):
    r = lax.broadcasted_iota(jnp.int32, (rows, cols), 0)
    c = lax.broadcasted_iota(jnp.int32, (rows, cols), 1)
    return (r == c).astype(dtype)


def to_column(row):
    count = row.shape[1]
    r = lax.broadcasted_iota(jnp.int32, (count, count), 0)
    c = lax.broadcasted_iota(jnp.int32, (count, count), 1)
    return jnp.sum(jnp.where(r == c, jnp.broadcast_to(row, (count, count)), 0.0), axis=1, keepdims=True)


def pack_kernel(feat_ref, gain_ref, pos_ref, mate_ref, out_ref, tmp_ref):
    atoms, dim = feat_ref.shape
    floats = feat_ref[...].astype(jnp.float32)
    spread = jnp.mean(floats * floats, axis=-1, keepdims=True)
    normed = floats * lax.rsqrt(spread + 1e-06) * gain_ref[...]
    out_ref[:, :dim] = normed.astype(jnp.bfloat16)
    tmp_ref[...] = jnp.zeros(tmp_ref.shape, jnp.float32)
    own = parts_of(pos_ref[...], 3)
    mate = parts_of(mate_ref[...], 3)
    for p in range(3):
        tmp_ref[8 * p : 8 * p + 3, :] = own[p].astype(jnp.float32)
        tmp_ref[8 * p + 3 : 8 * p + 6, :] = mate[p].astype(jnp.float32)
    eye = unit(atoms, atoms, jnp.bfloat16)
    turned = mm(eye, tmp_ref[...].astype(jnp.bfloat16), ((1,), (1,)))
    out_ref[:, dim:] = turned.astype(jnp.bfloat16)


def query_kernel(
    head_dim,
    pack_ref,
    wqkv_ref,
    rw_ref,
    ro_ref,
    pw_ref,
    qexp_ref,
    w1_ref,
    w2_ref,
    off_ref,
):
    atoms = pack_ref.shape[0]
    dim = wqkv_ref.shape[0]
    groups, rows, width = qexp_ref.shape
    per = rows // atoms
    q = mm(pack_ref[:, :dim], wqkv_ref[:, :dim], ((1,), (0,)))
    q = q.astype(jnp.bfloat16).astype(jnp.float32)
    lane = lax.broadcasted_iota(jnp.int32, (per, width), 1) // head_dim
    sub = lax.broadcasted_iota(jnp.int32, (per, width), 0)
    keep = (lane == sub)[None]
    for g in range(groups):
        part = q[:, g * width : (g + 1) * width]
        spread = jnp.broadcast_to(part[:, None, :], (atoms, per, width))
        spread = jnp.where(keep, spread, 0.0).reshape(rows, width)
        qexp_ref[g] = spread.astype(jnp.bfloat16)
    h, m, l = parts_of(rw_ref[...], 3)
    stack = jnp.concatenate([h, h, m, h, l, m], axis=0)
    hidden = rw_ref.shape[1]
    w1_ref[...] = mm(unit(hidden, hidden, jnp.bfloat16), stack, ((1,), (1,))).astype(jnp.bfloat16)
    h, l = parts_of(pw_ref[...], 2)
    stack = jnp.concatenate([h, h, l], axis=0)
    heads = pw_ref.shape[1]
    w2_ref[...] = mm(unit(heads, heads, jnp.bfloat16), stack, ((1,), (1,))).astype(jnp.bfloat16)
    off_ref[...] = jnp.broadcast_to(to_column(ro_ref[...]), off_ref.shape)


def chosen(scalars, lane):
    out = jnp.full(lane.shape, scalars[0])
    for e in range(1, len(scalars)):
        out = jnp.where(lane == e, scalars[e], out)
    return out


def turned_positions(rows_bf):
    r = lax.broadcasted_iota(jnp.int32, (8, 128), 0)
    c = lax.broadcasted_iota(jnp.int32, (8, 128), 1)
    pick = ((c % 8 == r) & (c < 24) & (r < 6)).astype(jnp.bfloat16)
    return mm(pick, rows_bf, ((1,), (1,)))


def own_columns(rows_bf):
    rows = rows_bf.astype(jnp.float32)
    return [rows[:, c : c + 1] + rows[:, c + 8 : c + 9] + rows[:, c + 16 : c + 17] for c in range(3)]


def wave_feats(pos8):
    angle = two_pi * pos8
    return jnp.cos(angle), jnp.sin(angle)


def cosine_rows(own_cols, feats):
    cos_k, sin_k = feats
    total = None
    for c in range(3):
        angle = two_pi * own_cols[c]
        term = jnp.cos(angle) * cos_k[c : c + 1] + jnp.sin(angle) * sin_k[c : c + 1]
        total = term if total is None else total + term
    return total


def attend(qexp, keys, vals, scale, bias3):
    rows = qexp.shape[0]
    count = keys.shape[0]
    atoms, per, _ = bias3.shape
    s = mm(qexp, keys, ((1,), (1,))).reshape(atoms, per, count) * scale + bias3
    top = jnp.max(s, axis=-1, keepdims=True)
    p = jnp.exp(s - top)
    total = jnp.sum(p, axis=-1, keepdims=True)
    o = mm(p.astype(jnp.bfloat16).reshape(rows, count), vals, ((1,), (0,)))
    return top, total, o.reshape(atoms, per, vals.shape[1])


def early_kernel(
    head_dim,
    slot_ref,
    mate_ref,
    shift_ref,
    cell_ref,
    pack_ref,
    wqkv_ref,
    qexp_ref,
    w1_ref,
    w2_ref,
    off_ref,
    str_ref,
    kv_ref,
    acc_ref,
    top_ref,
    sum_ref,
    bias_ref,
    feat_ref,
    loc_ref,
):
    dim = wqkv_ref.shape[0]
    atoms = acc_ref.shape[1]
    groups, rows, width = qexp_ref.shape
    per = rows // atoms
    kv = mm(pack_ref[:, :dim], wqkv_ref[:, dim:], ((1,), (0,)))
    kv_ref[...] = kv.astype(jnp.bfloat16)
    own = own_columns(pack_ref[:atoms, dim:])
    pos8 = turned_positions(pack_ref[:, dim:])
    cos8, sin8 = wave_feats(pos8)
    feat_ref[0] = cos8
    feat_ref[1] = sin8
    waves = cosine_rows(own, (cos8, sin8))
    strength = to_column(str_ref[...])
    scale = head_dim ** (-0.5)
    for g in range(groups):
        low, high = g * width, (g + 1) * width
        bias3 = strength[g * per : (g + 1) * per][None] * waves[:, None, :]
        top, total, o = attend(
            qexp_ref[g], kv_ref[:, low:high], kv_ref[:, dim + low : dim + high], scale, bias3
        )
        acc_ref[g] = o
        top_ref[g] = jnp.broadcast_to(top, top_ref.shape[1:])
        sum_ref[g] = jnp.broadcast_to(total, sum_ref.shape[1:])
    entries = slot_ref.shape[0]
    for e in range(entries):
        start = pl.multiple_of(slot_ref[e] * atoms, atoms)
        loc_ref[e * atoms : (e + 1) * atoms, :] = pack_ref[pl.ds(start, atoms), dim:]
    near = turned_positions(loc_ref[...])
    listed = entries * atoms
    lane = lax.broadcasted_iota(jnp.int32, (1, listed), 1) // atoms
    from_mate = chosen([mate_ref[e] for e in range(entries)], lane) > 0
    square = None
    for c in range(3):
        at = jnp.where(from_mate, near[c + 3 : c + 4], near[c : c + 1])
        at = at + chosen([shift_ref[c, e] for e in range(entries)], lane).astype(jnp.float32)
        gap = (at - own[c]) * cell_ref[c]
        square = gap * gap if square is None else square + gap * gap
    dist = jnp.sqrt(square + 0.25)
    nrbf = w1_ref.shape[1] // 6
    centers = lax.broadcasted_iota(jnp.int32, (nrbf, 1), 0).astype(jnp.float32) * rbf_step
    offset = off_ref[:, :1]
    step = 4
    for i in range(0, atoms, step):
        radial = jnp.concatenate(
            [
                jnp.exp(-((dist[j : j + 1] - centers) ** 2) * (0.5 / rbf_width**2))
                for j in range(i, i + step)
            ],
            axis=1,
        )
        h, m, l = parts_of(radial, 3)
        stack = jnp.concatenate([h, m, h, l, h, m], axis=0)
        u = mm(w1_ref[...], stack, ((1,), (0,))) + offset
        u = u / (1.0 + jnp.exp(-u))
        h, l = parts_of(u, 2)
        pair = mm(w2_ref[...], jnp.concatenate([h, l, h], axis=0), ((1,), (0,)))
        for j in range(step):
            for g in range(groups):
                bias_ref[g, i + j] = pair[
                    g * per : (g + 1) * per, j * listed : (j + 1) * listed
                ]


def late_kernel(
    head_dim,
    slot_ref,
    valid_ref,
    pack_ref,
    feat_ref,
    wqkv_ref,
    wout_ref,
    qexp_ref,
    str_ref,
    own_ref,
    kv_ref,
    acc_ref,
    top_ref,
    sum_ref,
    bias_ref,
    in_ref,
    out_ref,
    kv2_ref,
    near_ref,
):
    dim = wqkv_ref.shape[0]
    atoms = acc_ref.shape[1]
    groups, rows, width = qexp_ref.shape
    per = rows // atoms
    half = kv_ref.shape[0]
    kv2 = mm(pack_ref[:, :dim], wqkv_ref[:, dim:], ((1,), (0,)))
    kv2_ref[half:, :] = kv2.astype(jnp.bfloat16)
    kv2_ref[:half, :] = kv_ref[...]
    entries = slot_ref.shape[0]
    for e in range(entries):
        start = pl.multiple_of(slot_ref[e] * atoms, atoms)
        near_ref[e * atoms : (e + 1) * atoms, :] = kv2_ref[pl.ds(start, atoms), :]
    own = own_columns(own_ref[:, dim:])
    waves = cosine_rows(own, (feat_ref[0, 3:6], feat_ref[1, 3:6]))
    strength = to_column(str_ref[...])
    scale = head_dim ** (-0.5)
    listed = entries * atoms
    lane = lax.broadcasted_iota(jnp.int32, (1, 1, listed), 2) // atoms
    live = chosen([valid_ref[e] for e in range(entries)], lane) > 0
    block = lax.broadcasted_iota(jnp.int32, (1, per, width), 2) // head_dim
    keep = block == lax.broadcasted_iota(jnp.int32, (1, per, width), 1)
    pieces = []
    for g in range(groups):
        low, high = g * width, (g + 1) * width
        bias3 = strength[g * per : (g + 1) * per][None] * waves[:, None, :]
        top, total, o = attend(
            qexp_ref[g],
            kv2_ref[half:, low:high],
            kv2_ref[half:, dim + low : dim + high],
            scale,
            bias3,
        )
        top1 = top_ref[g][:, :, :1]
        best = jnp.maximum(top, top1)
        a, b = jnp.exp(top1 - best), jnp.exp(top - best)
        denom = a * sum_ref[g][:, :, :1] + b * total
        far = (a / denom) * acc_ref[g] + (b / denom) * o
        far = jnp.sum(jnp.where(keep, far, 0.0), axis=1).astype(jnp.bfloat16)
        s = mm(qexp_ref[g], near_ref[:, low:high], ((1,), (1,)))
        s = s.reshape(atoms, per, listed) * scale + bias_ref[g]
        s = jnp.where(live, s, -1e30)
        p = jnp.exp(s - jnp.max(s, axis=-1, keepdims=True))
        total = jnp.sum(p, axis=-1, keepdims=True)
        o = mm(
            p.astype(jnp.bfloat16).reshape(rows, listed),
            near_ref[:, dim + low : dim + high],
            ((1,), (0,)),
        )
        o = o.reshape(atoms, per, width) / total
        close = jnp.sum(jnp.where(keep, o, 0.0), axis=1).astype(jnp.bfloat16)
        pieces.append((close.astype(jnp.float32) + far.astype(jnp.float32)).astype(jnp.bfloat16))
    combined = jnp.concatenate(pieces, axis=1)
    moved = mm(combined, wout_ref[...], ((1,), (0,)))
    out_ref[...] = (in_ref[...].astype(jnp.float32) + moved).astype(jnp.bfloat16)


def call(kernel, outs, scratch, smem, args):
    specs = [pl.BlockSpec(memory_space=pltpu.SMEM)] * smem
    specs += [pl.BlockSpec(memory_space=pltpu.VMEM)] * (len(args) - smem)
    many = isinstance(outs, list)
    vmem = pl.BlockSpec(memory_space=pltpu.VMEM)
    return pl.pallas_call(
        kernel,
        out_shape=outs,
        in_specs=specs,
        out_specs=[vmem] * len(outs) if many else vmem,
        scratch_shapes=scratch,
    )(*args)


def xor_phases(row_count, col_count):
    col_bits = col_count.bit_length() - 1
    row_bits = row_count.bit_length() - 1
    first = list(range(1, col_bits))
    second = [0] + list(range(col_bits + 1, col_bits + row_bits))
    return first, second, [col_bits]


def spread_bits(number, bits):
    return sum(((number >> k) & 1) << bit for k, bit in enumerate(bits))


def on_device_small(
    features,
    positions,
    cell_lengths,
    block_lists,
    image_offsets,
    block_valid,
    norm_gain,
    w_qkv,
    w_out,
    rbf_weight,
    rbf_offset,
    pair_weight,
    cosine_scale,
):
    atoms, dim = features.shape
    heads = pair_weight.shape[1]
    hidden = pair_weight.shape[0]
    nrbf = rbf_weight.shape[0]
    head_dim = dim // heads
    row_count = lax.axis_size("rows")
    col_count = lax.axis_size("cols")
    total = row_count * col_count
    axes = ("rows", "cols")
    me = lax.axis_index("rows") * col_count + lax.axis_index("cols")
    phases = xor_phases(row_count, col_count)
    entries = block_lists.shape[1]
    width = 256
    per = width // head_dim
    groups = heads // per
    rows = atoms * per
    half = total // 2 * atoms
    f32, bf16 = jnp.float32, jnp.bfloat16
    shape = jax.ShapeDtypeStruct

    def swap(array, mask):
        return lax.ppermute(array, axes, [(i, i ^ mask) for i in range(total)])

    def gathered(array, bits):
        got = [swap(array, spread_bits(d, bits)) for d in range(1, 1 << len(bits))]
        return jnp.concatenate([array] + got, axis=0)

    rel = block_lists[0] ^ me
    slot = jnp.zeros_like(rel)
    stride = 1
    for bits in phases[:2]:
        for bit in bits:
            slot = slot + ((rel >> bit) & 1) * stride
            stride = stride * 2
    from_mate = (rel >> phases[2][0]) & 1
    full_slot = slot + from_mate * stride
    mate = swap(positions, 1 << phases[2][0])
    pack = call(
        pack_kernel,
        shape((atoms, dim + 128), bf16),
        [pltpu.VMEM((128, atoms), f32)],
        0,
        (features, norm_gain[None], positions, mate),
    )
    near = gathered(pack, phases[0])
    qexp, w1, w2, off = call(
        functools.partial(query_kernel, head_dim),
        [
            shape((groups, rows, width), bf16),
            shape((hidden, 6 * nrbf), bf16),
            shape((heads, 3 * hidden), bf16),
            shape((hidden, 128), f32),
        ],
        [],
        0,
        (pack, w_qkv, rbf_weight, rbf_offset[None], pair_weight),
    )
    mine = gathered(near, phases[1])
    other = swap(mine, 1 << phases[2][0])
    kv, acc, top, summed, bias, feats = call(
        functools.partial(early_kernel, head_dim),
        [
            shape((half, 2 * dim), bf16),
            shape((groups, atoms, per, width), f32),
            shape((groups, atoms, per, 128), f32),
            shape((groups, atoms, per, 128), f32),
            shape((groups, atoms, per, entries * atoms), f32),
            shape((2, 8, half), f32),
        ],
        [pltpu.VMEM((entries * atoms, 128), bf16)],
        4,
        (
            slot,
            from_mate,
            image_offsets[:, 0, :],
            cell_lengths,
            mine,
            w_qkv,
            qexp,
            w1,
            w2,
            off,
            cosine_scale[None],
        ),
    )
    return call(
        functools.partial(late_kernel, head_dim),
        shape((atoms, dim), bf16),
        [
            pltpu.VMEM((2 * half, 2 * dim), bf16),
            pltpu.VMEM((entries * atoms, 2 * dim), bf16),
        ],
        2,
        (
            full_slot,
            block_valid[0],
            other,
            feats,
            w_qkv,
            w_out,
            qexp,
            cosine_scale[None],
            pack,
            kv,
            acc,
            top,
            summed,
            bias,
            features,
        ),
    )


def solution(mesh):
    row_count, col_count = mesh.shape["rows"], mesh.shape["cols"]
    small = row_count * col_count <= 64
    body = on_device_small if small else on_device
    return jax.shard_map(
        body,
        mesh=mesh,
        in_specs=(
            P(("rows", "cols"), None),
            P(None, ("rows", "cols")),
            P(),
            P(("rows", "cols"), None),
            P(None, ("rows", "cols"), None),
            P(("rows", "cols"), None),
            P(),
            P(),
            P(),
            P(),
            P(),
            P(),
            P(),
        ),
        out_specs=P(("rows", "cols"), None),
        check_vma=False,
    )
```

```python
import functools
import math

import jax
import jax.numpy as jnp
from jax import lax
from jax.experimental import pallas as pl
from jax.experimental.pallas import tpu as pltpu
from jax.sharding import PartitionSpec as P


rbf_step = 2.0
rbf_width = 2.0
two_pi = 2.0 * math.pi
highest = lax.Precision.HIGHEST


def with_halo(cells, sides, width):
    for axis, dim in sides:
        count = lax.axis_size(axis)
        head = lax.slice_in_dim(cells, 0, width, axis=dim)
        tail = lax.slice_in_dim(cells, cells.shape[dim] - width, cells.shape[dim], axis=dim)
        cells = jnp.concatenate(
            [
                lax.ppermute(tail, axis, [(i, (i + 1) % count) for i in range(count)]),
                cells,
                lax.ppermute(head, axis, [((i + 1) % count, i) for i in range(count)]),
            ],
            axis=dim,
        )
    return cells


def rms_rows(values, norm_gain):
    floats = values.astype(jnp.float32)
    spread = jnp.mean(floats * floats, axis=-1, keepdims=True)
    return (floats * lax.rsqrt(spread + 1e-06) * norm_gain).astype(jnp.bfloat16)


def near_attention(
    query_rows,
    own_pos,
    keys,
    key_pos,
    shifts,
    live,
    cell_lengths,
    rbf_weight,
    rbf_offset,
    pair_weight,
):
    entries, block_len = (keys.shape[0], keys.shape[1])
    model_dim = query_rows.shape[1]
    head_count = pair_weight.shape[1]
    head_dim = model_dim // head_count
    key_coords = key_pos.transpose(1, 0, 2) + shifts.astype(jnp.float32)[:, :, None]
    key_coords = key_coords.reshape(3, entries * block_len)
    displace = (key_coords[:, None, :] - own_pos[:, :, None]) * cell_lengths[:, None, None]
    distance = jnp.sqrt(jnp.sum(displace * displace, axis=0) + 0.25)
    centers = jnp.arange(rbf_weight.shape[0], dtype=jnp.float32) * rbf_step
    radial = jnp.exp(-((distance[None] - centers[:, None, None]) ** 2) * (0.5 / rbf_width**2))
    radial = radial.reshape(rbf_weight.shape[0], -1)
    hidden = jax.nn.silu(jnp.dot(rbf_weight.T, radial, precision=highest) + rbf_offset[:, None])
    pair_bias = jnp.dot(pair_weight.T, hidden, precision=highest).reshape(
        head_count, query_rows.shape[0], entries * block_len
    )
    query_heads = query_rows.reshape(-1, head_count, head_dim)
    key_heads = keys[:, :, :model_dim].reshape(entries * block_len, head_count, head_dim)
    value_heads = keys[:, :, model_dim:].reshape(entries * block_len, head_count, head_dim)
    scores = (
        jnp.einsum("ahd,khd->hak", query_heads, key_heads, preferred_element_type=jnp.float32)
        * head_dim ** (-0.5)
        + pair_bias
    )
    allowed = jnp.repeat(live > 0, block_len)
    scores = jnp.where(allowed[None, None, :], scores, -1e30)
    row_max = jnp.max(scores, axis=-1, keepdims=True)
    weights = jnp.exp(scores - row_max)
    row_sum = jnp.sum(weights, axis=-1, keepdims=True)
    prob_bf = weights.astype(jnp.bfloat16)
    attended = jnp.einsum(
        "hak,khd->ahd", prob_bf, value_heads, preferred_element_type=jnp.float32
    ) / row_sum.transpose(1, 0, 2)
    return attended.reshape(-1, model_dim).astype(jnp.bfloat16)


def on_device(
    features,
    positions,
    cell_lengths,
    block_lists,
    image_offsets,
    block_valid,
    norm_gain,
    w_qkv,
    w_out,
    rbf_weight,
    rbf_offset,
    pair_weight,
    cosine_scale,
):
    atom_count, model_dim = features.shape
    head_count = pair_weight.shape[1]
    head_dim = model_dim // head_count
    row_count = lax.axis_size("rows")
    col_count = lax.axis_size("cols")
    row_index = lax.axis_index("rows")
    col_index = lax.axis_index("cols")
    per_dev = head_count // row_count
    normed = rms_rows(features, norm_gain)
    packed = jnp.dot(normed, w_qkv, preferred_element_type=jnp.float32).astype(jnp.bfloat16)
    every_pos = lax.all_gather(positions, ("rows", "cols"), axis=1, tiled=True)
    near_rows = with_halo(normed[None, None], (("rows", 0), ("cols", 1)), 1)
    near_kv = jnp.dot(
        near_rows.reshape(9 * atom_count, model_dim),
        w_qkv[:, model_dim:],
        preferred_element_type=jnp.float32,
    )
    near_kv = near_kv.astype(jnp.bfloat16).reshape(9, atom_count, 2 * model_dim)
    listed = block_lists[0]
    list_row = listed // col_count
    list_col = listed % col_count
    slots = (list_row - row_index + 1) % row_count * 3 + (list_col - col_index + 1) % col_count
    keys = jnp.take(near_kv, slots, axis=0)
    block_pos = every_pos.reshape(3, row_count * col_count, atom_count)
    key_pos = jnp.take(block_pos, listed, axis=1).transpose(1, 0, 2)
    local_out = near_attention(
        packed[:, :model_dim],
        positions,
        keys,
        key_pos,
        image_offsets[:, 0, :],
        block_valid[0],
        cell_lengths,
        rbf_weight,
        rbf_offset,
        pair_weight,
    )
    grouped = (
        packed.reshape(atom_count, 3, head_count, head_dim)
        .transpose(1, 2, 0, 3)
        .reshape(3, head_count, atom_count * head_dim)
    )
    regrouped = lax.all_to_all(grouped, "rows", split_axis=1, concat_axis=2, tiled=True)
    query_count = row_count * atom_count
    queries = regrouped[0].reshape(per_dev, query_count, head_dim)
    key_vals = regrouped[1:]
    cycle_pos = (
        every_pos.reshape(3, row_count, col_count, atom_count).transpose(0, 2, 1, 3).reshape(3, -1)
    )
    query_pos = lax.dynamic_slice_in_dim(cycle_pos, col_index * query_count, query_count, 1)
    cycle_feats = jnp.concatenate(
        [jnp.cos(two_pi * cycle_pos), jnp.sin(two_pi * cycle_pos)], axis=0
    )
    query_feats = jnp.concatenate(
        [jnp.cos(two_pi * query_pos), jnp.sin(two_pi * query_pos)], axis=0
    )
    strengths = lax.dynamic_slice_in_dim(cosine_scale, row_index * per_dev, per_dev)
    scale = head_dim ** (-0.5)

    def update(state, kv_block, key_start, block_len):
        run_max, run_sum, accum = state
        scores = (
            jnp.einsum("hqd,hkd->hqk", queries, kv_block[0], preferred_element_type=jnp.float32)
            * scale
        )
        coords = lax.dynamic_slice_in_dim(cycle_feats, key_start, block_len, 1)
        cos_bias = jnp.dot(query_feats.T, coords, precision=highest)
        scores = scores + strengths[:, None, None] * cos_bias[None]
        new_max = jnp.maximum(run_max, jnp.max(scores, axis=-1))
        keep_part = jnp.exp(run_max - new_max)
        weights = jnp.exp(scores - new_max[:, :, None])
        run_sum = run_sum * keep_part + jnp.sum(weights, axis=-1)
        prob_bf = weights.astype(jnp.bfloat16)
        accum = accum * keep_part[:, None, :] + jnp.einsum(
            "hqk,hkd->hdq", prob_bf, kv_block[1], preferred_element_type=jnp.float32
        )
        return (new_max, run_sum, accum)

    initial = (
        jnp.full((per_dev, query_count), -1e30, jnp.float32),
        jnp.zeros((per_dev, query_count), jnp.float32),
        jnp.zeros((per_dev, head_dim, query_count), jnp.float32),
    )
    piece = lax.all_gather(key_vals, "cols", axis=2, tiled=True)
    key_total = piece.shape[2] // head_dim
    if key_total > 1024 and key_total % 1024 == 0:
        block_len = 1024
    else:
        block_len = key_total
    block_count = key_total // block_len
    kv_blocks = piece.reshape(2, per_dev, block_count, block_len, head_dim).transpose(2, 0, 1, 3, 4)
    block_starts = jnp.arange(block_count, dtype=jnp.int32) * block_len

    def one_block(state, block_in):
        kv_block, key_start = block_in
        return (update(state, kv_block, key_start, block_len), None)

    state, _ = lax.scan(one_block, initial, (kv_blocks, block_starts))
    _, run_sum, accum = state
    head_out = (
        (accum / run_sum[:, None, :])
        .transpose(0, 2, 1)
        .astype(jnp.bfloat16)
        .reshape(per_dev, query_count * head_dim)
    )
    returned = lax.all_to_all(head_out, "rows", split_axis=1, concat_axis=0, tiled=True)
    global_out = (
        returned.reshape(head_count, atom_count, head_dim)
        .transpose(1, 0, 2)
        .reshape(atom_count, model_dim)
    )
    combined = (local_out.astype(jnp.float32) + global_out.astype(jnp.float32)).astype(jnp.bfloat16)
    updated = features.astype(jnp.float32) + jnp.dot(
        combined, w_out, preferred_element_type=jnp.float32
    )
    return updated.astype(jnp.bfloat16)


def mm(a, b, dims):
    return lax.dot_general(a, b, (dims, ((), ())), preferred_element_type=jnp.float32)


def parts_of(value, count):
    out = []
    for _ in range(count):
        part = value.astype(jnp.bfloat16)
        out.append(part)
        value = value - part.astype(jnp.float32)
    return out


def unit(rows, cols, dtype):
    r = lax.broadcasted_iota(jnp.int32, (rows, cols), 0)
    c = lax.broadcasted_iota(jnp.int32, (rows, cols), 1)
    return (r == c).astype(dtype)


def to_column(row):
    count = row.shape[1]
    r = lax.broadcasted_iota(jnp.int32, (count, count), 0)
    c = lax.broadcasted_iota(jnp.int32, (count, count), 1)
    return jnp.sum(jnp.where(r == c, jnp.broadcast_to(row, (count, count)), 0.0), axis=1, keepdims=True)


def fetch(pairs, sems):
    copies = [pltpu.make_async_copy(src, dst, sems.at[k]) for k, (src, dst) in enumerate(pairs)]
    for copy in copies:
        copy.start()
    for copy in copies:
        copy.wait()


def pack_kernel(feat_hbm, gain_hbm, pos_hbm, out_ref, feat_ref, gain_ref, pos_ref, tmp_ref, sems):
    fetch(((feat_hbm, feat_ref), (gain_hbm, gain_ref), (pos_hbm, pos_ref)), sems)
    atoms, dim = feat_ref.shape
    floats = feat_ref[...].astype(jnp.float32)
    spread = jnp.mean(floats * floats, axis=-1, keepdims=True)
    normed = floats * lax.rsqrt(spread + 1e-06) * gain_ref[...]
    out_ref[:, :dim] = normed.astype(jnp.bfloat16)
    tmp_ref[...] = jnp.zeros(tmp_ref.shape, jnp.float32)
    for p, part in enumerate(parts_of(pos_ref[...], 3)):
        tmp_ref[8 * p : 8 * p + 3, :] = part.astype(jnp.float32)
    eye = unit(atoms, atoms, jnp.bfloat16)
    turned = mm(eye, tmp_ref[...].astype(jnp.bfloat16), ((1,), (1,)))
    out_ref[:, dim:] = turned.astype(jnp.bfloat16)


def query_kernel(
    head_dim,
    wqkv_hbm,
    rw_hbm,
    ro_hbm,
    pw_hbm,
    cs_hbm,
    pack_ref,
    qexp_ref,
    w1_ref,
    w2_ref,
    off_ref,
    str_ref,
    own_ref,
    wq_ref,
    rw_ref,
    ro_ref,
    pw_ref,
    cs_ref,
    sems,
):
    atoms = pack_ref.shape[0]
    dim = wq_ref.shape[0]
    fetch(
        (
            (wqkv_hbm.at[:, pl.ds(0, dim)], wq_ref),
            (rw_hbm, rw_ref),
            (ro_hbm, ro_ref),
            (pw_hbm, pw_ref),
            (cs_hbm, cs_ref),
        ),
        sems,
    )
    groups, rows, width = qexp_ref.shape
    per = rows // atoms
    q = mm(pack_ref[:, :dim], wq_ref[...], ((1,), (0,)))
    q = q.astype(jnp.bfloat16).astype(jnp.float32)
    lane = lax.broadcasted_iota(jnp.int32, (per, width), 1) // head_dim
    sub = lax.broadcasted_iota(jnp.int32, (per, width), 0)
    keep = (lane == sub)[None]
    for g in range(groups):
        part = q[:, g * width : (g + 1) * width]
        spread = jnp.broadcast_to(part[:, None, :], (atoms, per, width))
        spread = jnp.where(keep, spread, 0.0).reshape(rows, width)
        qexp_ref[g] = spread.astype(jnp.bfloat16)
    h, m, l = parts_of(rw_ref[...], 3)
    stack = jnp.concatenate([h, h, m, h, l, m], axis=0)
    hidden = rw_ref.shape[1]
    w1_ref[...] = mm(unit(hidden, hidden, jnp.bfloat16), stack, ((1,), (1,))).astype(jnp.bfloat16)
    h, l = parts_of(pw_ref[...], 2)
    w2_ref[...] = jnp.concatenate([h, h, l], axis=1)
    off_ref[...] = jnp.broadcast_to(to_column(ro_ref[...]), off_ref.shape)
    str_ref[...] = jnp.broadcast_to(to_column(cs_ref[...]), str_ref.shape)
    pos = pack_ref[:, dim:].astype(jnp.float32)
    pos = pos + pltpu.roll(pos, 120, 1) + pltpu.roll(pos, 112, 1)
    own_ref[0] = pos
    own_ref[1] = jnp.cos(two_pi * pos)
    own_ref[2] = jnp.sin(two_pi * pos)


def repack_kernel(*refs):
    blocks, out_ref = refs[:-1], refs[-1]
    atoms = blocks[0].shape[0]
    dim = out_ref.shape[1]
    count = atoms * len(blocks)
    for k, block in enumerate(blocks):
        out_ref[k * atoms : (k + 1) * atoms, :] = block[:, :dim]
    pos = jnp.concatenate([block[:, dim:] for block in blocks], axis=0)
    r = lax.broadcasted_iota(jnp.int32, (8, 128), 0)
    c = lax.broadcasted_iota(jnp.int32, (8, 128), 1)
    tail = []
    for p in range(3):
        pick = ((c == 8 * p + r) & (r < 3)).astype(jnp.bfloat16)
        tail.append(mm(pick, pos, ((1,), (1,))))
    tail.append(jnp.zeros((8, dim - 3 * count), jnp.float32))
    out_ref[count:, :] = jnp.concatenate(tail, axis=1).astype(jnp.bfloat16)


def piece_positions(piece_ref, count):
    tail = piece_ref[count:, :].astype(jnp.float32)
    return tail[:, :count] + tail[:, count : 2 * count] + tail[:, 2 * count : 3 * count]


def attend(qexp, keys, vals, scale, bias3):
    rows = qexp.shape[0]
    count = keys.shape[0]
    atoms, per, _ = bias3.shape
    s = mm(qexp, keys, ((1,), (1,))).reshape(atoms, per, count) * scale + bias3
    top = jnp.max(s, axis=-1, keepdims=True)
    p = jnp.exp(s - top)
    total = jnp.sum(p, axis=-1, keepdims=True)
    o = mm(p.astype(jnp.bfloat16).reshape(rows, count), vals, ((1,), (0,)))
    return top, total, o.reshape(atoms, per, vals.shape[1])


def absorb(head_dim, places, pieces, wqkv_ref, qexp_ref, str_ref, own_ref, kv_ref):
    dim = wqkv_ref.shape[0]
    atoms = own_ref.shape[1]
    groups, rows, width = qexp_ref.shape
    per = rows // atoms
    count = pieces[0].shape[0] - 8
    rows_in = jnp.concatenate([piece[:count, :] for piece in pieces], axis=0)
    kv = mm(rows_in, wqkv_ref[:, dim:], ((1,), (0,))).astype(jnp.bfloat16)
    for k, place in enumerate(places):
        kv_ref[place * count : (place + 1) * count, :] = kv[k * count : (k + 1) * count]
    pos8 = jnp.concatenate([piece_positions(piece, count) for piece in pieces], axis=1)
    cos_k, sin_k = jnp.cos(two_pi * pos8), jnp.sin(two_pi * pos8)
    waves = None
    for c in range(3):
        term = own_ref[1, :, c : c + 1] * cos_k[c : c + 1] + own_ref[2, :, c : c + 1] * sin_k[c : c + 1]
        waves = term if waves is None else waves + term
    out = []
    for g in range(groups):
        low, high = g * width, (g + 1) * width
        bias3 = str_ref[g * per : (g + 1) * per, :1][None] * waves[:, None, :]
        out.append(
            attend(
                qexp_ref[g],
                kv[:, low:high],
                kv[:, dim + low : dim + high],
                head_dim ** (-0.5),
                bias3,
            )
        )
    return out


def widen(column, lanes):
    return jnp.broadcast_to(column, column.shape[:-1] + (lanes,))


def repeat_lanes(array, lanes):
    return jnp.concatenate([array] * (lanes // array.shape[-1]), axis=-1)


def first_kernel(head_dim, places, *refs):
    pieces = refs[: len(places)]
    wqkv_ref, qexp_ref, str_ref, own_ref = refs[len(places) : -4]
    kv_ref, acc_ref, top_ref, sum_ref = refs[-4:]
    got = absorb(head_dim, places, pieces, wqkv_ref, qexp_ref, str_ref, own_ref, kv_ref)
    for g, (top, total, o) in enumerate(got):
        acc_ref[g] = o
        top_ref[g] = widen(top, 128)
        sum_ref[g] = widen(total, 128)


def merge(got, g, acc_ref, top_ref, sum_ref):
    top, total, o = got[g]
    width = o.shape[-1]
    best = jnp.maximum(widen(top, 128), top_ref[g])
    a, b = jnp.exp(top_ref[g] - best), jnp.exp(widen(top, 128) - best)
    summed = a * sum_ref[g] + b * widen(total, 128)
    acc = repeat_lanes(a, width) * acc_ref[g] + repeat_lanes(b, width) * o
    return best, summed, acc


def next_kernel(head_dim, places, *refs):
    pieces = refs[: len(places)]
    wqkv_ref, qexp_ref, str_ref, own_ref = refs[len(places) : len(places) + 4]
    _, acc_in, top_in, sum_in, kv_ref, acc_ref, top_ref, sum_ref = refs[len(places) + 4 :]
    got = absorb(head_dim, places, pieces, wqkv_ref, qexp_ref, str_ref, own_ref, kv_ref)
    for g in range(len(got)):
        best, summed, acc = merge(got, g, acc_in, top_in, sum_in)
        acc_ref[g] = acc
        top_ref[g] = best
        sum_ref[g] = summed


def chosen(scalars, lane):
    out = jnp.full(lane.shape, scalars[0])
    for e in range(1, len(scalars)):
        out = jnp.where(lane == e, scalars[e], out)
    return out


def last_kernel(head_dim, locate, col_count, list_ref, valid_ref, shift_ref, cell_ref, *refs):
    piece_refs = refs[:8]
    (
        wqkv_ref,
        qexp_ref,
        str_ref,
        own_ref,
        w1_ref,
        w2_ref,
        off_ref,
        wout_ref,
        in_ref,
        _,
        acc_in,
        top_in,
        sum_in,
        out_ref,
        kv_ref,
        near_ref,
        pos_ref,
        bias_ref,
    ) = refs[8:]
    dim = wqkv_ref.shape[0]
    atoms = own_ref.shape[1]
    groups, rows, width = qexp_ref.shape
    per = rows // atoms
    count = piece_refs[0].shape[0] - 8
    got = absorb(head_dim, (7,), piece_refs[7:], wqkv_ref, qexp_ref, str_ref, own_ref, kv_ref)
    for k in range(8):
        pos_ref[k] = piece_positions(piece_refs[k], count)
    me = lax.axis_index("rows") * col_count + lax.axis_index("cols")
    entries = list_ref.shape[1]
    listed = entries * atoms
    lane = lax.broadcasted_iota(jnp.int32, (1, listed), 1) // atoms
    in_tile = lax.broadcasted_iota(jnp.int32, (1, count), 1) // atoms
    a_tile = count // atoms
    tiles = []
    for e in range(entries):
        up, across, turn = locate(list_ref[0, e] ^ me)
        place = across + 4 * turn
        start = pl.multiple_of((place * a_tile + up) * atoms, atoms)
        near_ref[e * atoms : (e + 1) * atoms, :] = kv_ref[pl.ds(start, atoms), :]
        into = e % a_tile
        moved = pltpu.roll(pos_ref[place], (into - up + a_tile) % a_tile * atoms, 1)
        if into == 0:
            tiles.append(moved)
        else:
            tiles[-1] = jnp.where(in_tile == into, moved, tiles[-1])
    near = jnp.concatenate(tiles, axis=1)
    square = None
    for c in range(3):
        at = near[c : c + 1] + chosen([shift_ref[c, 0, e] for e in range(entries)], lane).astype(jnp.float32)
        gap = (at - own_ref[0, :, c : c + 1]) * cell_ref[c]
        square = gap * gap if square is None else square + gap * gap
    dist = jnp.sqrt(square + 0.25)
    nrbf = w1_ref.shape[1] // 6
    centers = lax.broadcasted_iota(jnp.int32, (nrbf, 1), 0).astype(jnp.float32) * rbf_step
    offset = off_ref[:, :1]
    step = 4
    for i in range(0, atoms, step):
        radial = jnp.concatenate(
            [
                jnp.exp(-((dist[j : j + 1] - centers) ** 2) * (0.5 / rbf_width**2))
                for j in range(i, i + step)
            ],
            axis=1,
        )
        h, m, l = parts_of(radial, 3)
        stack = jnp.concatenate([h, m, h, l, h, m], axis=0)
        u = mm(w1_ref[...], stack, ((1,), (0,))) + offset
        u = u / (1.0 + jnp.exp(-u))
        h, l = parts_of(u, 2)
        pair = mm(w2_ref[...], jnp.concatenate([h, l, h], axis=0), ((1,), (0,)))
        for j in range(step):
            for g in range(groups):
                bias_ref[g, i + j] = pair[g * per : (g + 1) * per, j * listed : (j + 1) * listed]
    lane3 = lax.broadcasted_iota(jnp.int32, (1, 1, listed), 2) // atoms
    live = chosen([valid_ref[0, e] for e in range(entries)], lane3) > 0
    block = lax.broadcasted_iota(jnp.int32, (1, per, width), 2) // head_dim
    keep = block == lax.broadcasted_iota(jnp.int32, (1, per, width), 1)
    pieces = []
    for g in range(groups):
        low, high = g * width, (g + 1) * width
        _, summed, far = merge(got, g, acc_in, top_in, sum_in)
        far = far / repeat_lanes(summed, width)
        far = jnp.sum(jnp.where(keep, far, 0.0), axis=1).astype(jnp.bfloat16)
        s = mm(qexp_ref[g], near_ref[:, low:high], ((1,), (1,)))
        s = s.reshape(atoms, per, listed) * head_dim ** (-0.5) + bias_ref[g]
        s = jnp.where(live, s, -1e30)
        p = jnp.exp(s - jnp.max(s, axis=-1, keepdims=True))
        summed = jnp.sum(p, axis=-1, keepdims=True)
        o = mm(
            p.astype(jnp.bfloat16).reshape(rows, listed),
            near_ref[:, dim + low : dim + high],
            ((1,), (0,)),
        )
        o = o.reshape(atoms, per, width) / summed
        close = jnp.sum(jnp.where(keep, o, 0.0), axis=1).astype(jnp.bfloat16)
        pieces.append((close.astype(jnp.float32) + far.astype(jnp.float32)).astype(jnp.bfloat16))
    combined = jnp.concatenate(pieces, axis=1)
    moved = mm(combined, wout_ref[...], ((1,), (0,)))
    out_ref[...] = (in_ref[...].astype(jnp.float32) + moved).astype(jnp.bfloat16)


def call(kernel, outs, scratch, smem, args, aliases=None, hbm=0):
    vmem = pl.BlockSpec(memory_space=pltpu.VMEM)
    first = smem + hbm
    specs = [pl.BlockSpec(memory_space=pltpu.SMEM)] * smem
    specs += [pl.BlockSpec(memory_space=pltpu.HBM)] * hbm + [vmem] * (len(args) - first)
    placed = [pltpu.with_memory_space_constraint(a, pltpu.HBM) for a in args[smem:first]]
    placed += [pltpu.with_memory_space_constraint(a, pltpu.VMEM) for a in args[first:]]
    many = isinstance(outs, list)
    return pl.pallas_call(
        kernel,
        out_shape=outs,
        in_specs=specs,
        out_specs=[vmem] * len(outs) if many else vmem,
        scratch_shapes=scratch,
        input_output_aliases=aliases or {},
        compiler_params=pltpu.CompilerParams(vmem_limit_bytes=24 << 20),
    )(*args[:smem], *placed)


def on_device_small(
    features,
    positions,
    cell_lengths,
    block_lists,
    image_offsets,
    block_valid,
    norm_gain,
    w_qkv,
    w_out,
    rbf_weight,
    rbf_offset,
    pair_weight,
    cosine_scale,
):
    atoms, dim = features.shape
    heads = pair_weight.shape[1]
    hidden = pair_weight.shape[0]
    nrbf = rbf_weight.shape[0]
    head_dim = dim // heads
    row_count = lax.axis_size("rows")
    col_count = lax.axis_size("cols")
    total = row_count * col_count
    axes = ("rows", "cols")
    col_bits = col_count.bit_length() - 1
    flip = 1 << col_bits
    across_bits = (0, col_bits + 1)
    entries = block_lists.shape[1]
    width = 256
    per = width // head_dim
    groups = heads // per
    rows = atoms * per
    f32, bf16 = jnp.float32, jnp.bfloat16
    vm = pltpu.VMEM

    def swap(array, mask):
        return lax.ppermute(array, axes, [(i, i ^ mask) for i in range(total)])

    def locate(rel):
        up = (rel >> 1) & 3
        across = (rel & 1) + 2 * ((rel >> across_bits[1]) & 1)
        turn = (rel >> col_bits) & 1
        turn = turn ^ jnp.minimum(up, 1) ^ jnp.minimum(across, 1)
        return up, across, turn

    tied = lax.optimization_barrier
    pack = call(
        pack_kernel,
        vm((atoms, dim + 128), bf16),
        [
            vm((atoms, dim), bf16),
            vm((1, dim), f32),
            vm(positions.shape, f32),
            vm((128, atoms), f32),
            pltpu.SemaphoreType.DMA((3,)),
        ],
        0,
        (features, norm_gain[None], positions),
        hbm=3,
    )
    ups = [swap(pack, (d << 1) | flip) for d in (1, 2, 3)]
    ready = call(
        functools.partial(query_kernel, head_dim),
        [
            vm((groups, rows, width), bf16),
            vm((hidden, 6 * nrbf), bf16),
            vm((heads, 3 * hidden), bf16),
            vm((hidden, 128), f32),
            vm((heads, 128), f32),
            vm((3, atoms, 128), f32),
        ],
        [
            vm((dim, dim), bf16),
            vm((nrbf, hidden), f32),
            vm((1, hidden), f32),
            vm((heads, hidden), f32),
            vm((1, heads), f32),
            pltpu.SemaphoreType.DMA((5,)),
        ],
        0,
        (w_qkv, rbf_weight, rbf_offset[None], pair_weight.T, cosine_scale[None], pack),
        hbm=5,
    )
    ups, ready = tied((ups, ready))
    qexp, w1, w2, off, strength, own = ready
    count = 4 * atoms
    base = call(repack_kernel, vm((count + 8, dim), bf16), [], 0, (pack, *ups))
    east = swap(base, 1 | flip)
    north = swap(base, (1 << across_bits[1]) | flip)
    diag = swap(base, 1 | (1 << across_bits[1]) | flip)
    state_shapes = [
        vm((8 * count, 2 * dim), bf16),
        vm((groups, atoms, per, width), f32),
        vm((groups, atoms, per, 128), f32),
        vm((groups, atoms, per, 128), f32),
    ]
    common = (w_qkv, qexp, strength, own)

    def step(places, pieces, state):
        if state is None:
            return call(
                functools.partial(first_kernel, head_dim, places),
                state_shapes,
                [],
                0,
                (*pieces, *common),
            )
        at = len(pieces) + len(common)
        return call(
            functools.partial(next_kernel, head_dim, places),
            state_shapes,
            [],
            0,
            (*pieces, *common, *state),
            {at + k: k for k in range(4)},
        )

    state = step((0,), (base,), None)
    base_late, state = tied((base, state))
    base2 = swap(base_late, flip)
    east, north, base2, state = tied((east, north, base2, state))
    east2, north2 = swap(east, flip), swap(north, flip)
    state = step((1, 2, 4), (east, north, base2), state)
    diag, east2, north2, state = tied((diag, east2, north2, state))
    diag2 = swap(diag, flip)
    state = step((3, 5, 6), (diag, east2, north2), state)
    diag2, state = tied((diag2, state))
    updated, _ = call(
        functools.partial(last_kernel, head_dim, locate, col_count),
        [jax.ShapeDtypeStruct((atoms, dim), bf16), state_shapes[0]],
        [
            vm((entries * atoms, 2 * dim), bf16),
            vm((8, 8, count), f32),
            vm((groups, atoms, per, entries * atoms), f32),
        ],
        4,
        (
            block_lists,
            block_valid,
            image_offsets,
            cell_lengths,
            base,
            east,
            north,
            diag,
            base2,
            east2,
            north2,
            diag2,
            *common,
            w1,
            w2,
            off,
            w_out,
            features,
            *state,
        ),
        {4 + 8 + len(common) + 5: 1},
    )
    return updated


def solution(mesh):
    row_count, col_count = mesh.shape["rows"], mesh.shape["cols"]
    small = (row_count, col_count) == (4, 8)
    body = on_device_small if small else on_device
    return jax.shard_map(
        body,
        mesh=mesh,
        in_specs=(
            P(("rows", "cols"), None),
            P(None, ("rows", "cols")),
            P(),
            P(("rows", "cols"), None),
            P(None, ("rows", "cols"), None),
            P(("rows", "cols"), None),
            P(),
            P(),
            P(),
            P(),
            P(),
            P(),
            P(),
        ),
        out_specs=P(("rows", "cols"), None),
        check_vma=False,
    )
```

```python
import functools
import math

import jax
import jax.numpy as jnp
from jax import lax
from jax.experimental import pallas as pl
from jax.experimental.pallas import tpu as pltpu
from jax.sharding import PartitionSpec as P


rbf_step = 2.0
rbf_width = 2.0
two_pi = 2.0 * math.pi
highest = lax.Precision.HIGHEST


def with_halo(cells, sides, width):
    for axis, dim in sides:
        count = lax.axis_size(axis)
        head = lax.slice_in_dim(cells, 0, width, axis=dim)
        tail = lax.slice_in_dim(cells, cells.shape[dim] - width, cells.shape[dim], axis=dim)
        cells = jnp.concatenate(
            [
                lax.ppermute(tail, axis, [(i, (i + 1) % count) for i in range(count)]),
                cells,
                lax.ppermute(head, axis, [((i + 1) % count, i) for i in range(count)]),
            ],
            axis=dim,
        )
    return cells


def rms_rows(values, norm_gain):
    floats = values.astype(jnp.float32)
    spread = jnp.mean(floats * floats, axis=-1, keepdims=True)
    return (floats * lax.rsqrt(spread + 1e-06) * norm_gain).astype(jnp.bfloat16)


def near_attention(
    query_rows,
    own_pos,
    keys,
    key_pos,
    shifts,
    live,
    cell_lengths,
    rbf_weight,
    rbf_offset,
    pair_weight,
):
    entries, block_len = (keys.shape[0], keys.shape[1])
    model_dim = query_rows.shape[1]
    head_count = pair_weight.shape[1]
    head_dim = model_dim // head_count
    key_coords = key_pos.transpose(1, 0, 2) + shifts.astype(jnp.float32)[:, :, None]
    key_coords = key_coords.reshape(3, entries * block_len)
    displace = (key_coords[:, None, :] - own_pos[:, :, None]) * cell_lengths[:, None, None]
    distance = jnp.sqrt(jnp.sum(displace * displace, axis=0) + 0.25)
    centers = jnp.arange(rbf_weight.shape[0], dtype=jnp.float32) * rbf_step
    radial = jnp.exp(-((distance[None] - centers[:, None, None]) ** 2) * (0.5 / rbf_width**2))
    radial = radial.reshape(rbf_weight.shape[0], -1)
    hidden = jax.nn.silu(jnp.dot(rbf_weight.T, radial, precision=highest) + rbf_offset[:, None])
    pair_bias = jnp.dot(pair_weight.T, hidden, precision=highest).reshape(
        head_count, query_rows.shape[0], entries * block_len
    )
    query_heads = query_rows.reshape(-1, head_count, head_dim)
    key_heads = keys[:, :, :model_dim].reshape(entries * block_len, head_count, head_dim)
    value_heads = keys[:, :, model_dim:].reshape(entries * block_len, head_count, head_dim)
    scores = (
        jnp.einsum("ahd,khd->hak", query_heads, key_heads, preferred_element_type=jnp.float32)
        * head_dim ** (-0.5)
        + pair_bias
    )
    allowed = jnp.repeat(live > 0, block_len)
    scores = jnp.where(allowed[None, None, :], scores, -1e30)
    row_max = jnp.max(scores, axis=-1, keepdims=True)
    weights = jnp.exp(scores - row_max)
    row_sum = jnp.sum(weights, axis=-1, keepdims=True)
    prob_bf = weights.astype(jnp.bfloat16)
    attended = jnp.einsum(
        "hak,khd->ahd", prob_bf, value_heads, preferred_element_type=jnp.float32
    ) / row_sum.transpose(1, 0, 2)
    return attended.reshape(-1, model_dim).astype(jnp.bfloat16)


def on_device(
    features,
    positions,
    cell_lengths,
    block_lists,
    image_offsets,
    block_valid,
    norm_gain,
    w_qkv,
    w_out,
    rbf_weight,
    rbf_offset,
    pair_weight,
    cosine_scale,
):
    atom_count, model_dim = features.shape
    head_count = pair_weight.shape[1]
    head_dim = model_dim // head_count
    row_count = lax.axis_size("rows")
    col_count = lax.axis_size("cols")
    row_index = lax.axis_index("rows")
    col_index = lax.axis_index("cols")
    per_dev = head_count // row_count
    normed = rms_rows(features, norm_gain)
    packed = jnp.dot(normed, w_qkv, preferred_element_type=jnp.float32).astype(jnp.bfloat16)
    every_pos = lax.all_gather(positions, ("rows", "cols"), axis=1, tiled=True)
    near_rows = with_halo(normed[None, None], (("rows", 0), ("cols", 1)), 1)
    near_kv = jnp.dot(
        near_rows.reshape(9 * atom_count, model_dim),
        w_qkv[:, model_dim:],
        preferred_element_type=jnp.float32,
    )
    near_kv = near_kv.astype(jnp.bfloat16).reshape(9, atom_count, 2 * model_dim)
    listed = block_lists[0]
    list_row = listed // col_count
    list_col = listed % col_count
    slots = (list_row - row_index + 1) % row_count * 3 + (list_col - col_index + 1) % col_count
    keys = jnp.take(near_kv, slots, axis=0)
    block_pos = every_pos.reshape(3, row_count * col_count, atom_count)
    key_pos = jnp.take(block_pos, listed, axis=1).transpose(1, 0, 2)
    local_out = near_attention(
        packed[:, :model_dim],
        positions,
        keys,
        key_pos,
        image_offsets[:, 0, :],
        block_valid[0],
        cell_lengths,
        rbf_weight,
        rbf_offset,
        pair_weight,
    )
    grouped = (
        packed.reshape(atom_count, 3, head_count, head_dim)
        .transpose(1, 2, 0, 3)
        .reshape(3, head_count, atom_count * head_dim)
    )
    regrouped = lax.all_to_all(grouped, "rows", split_axis=1, concat_axis=2, tiled=True)
    query_count = row_count * atom_count
    queries = regrouped[0].reshape(per_dev, query_count, head_dim)
    key_vals = regrouped[1:]
    cycle_pos = (
        every_pos.reshape(3, row_count, col_count, atom_count).transpose(0, 2, 1, 3).reshape(3, -1)
    )
    query_pos = lax.dynamic_slice_in_dim(cycle_pos, col_index * query_count, query_count, 1)
    cycle_feats = jnp.concatenate(
        [jnp.cos(two_pi * cycle_pos), jnp.sin(two_pi * cycle_pos)], axis=0
    )
    query_feats = jnp.concatenate(
        [jnp.cos(two_pi * query_pos), jnp.sin(two_pi * query_pos)], axis=0
    )
    strengths = lax.dynamic_slice_in_dim(cosine_scale, row_index * per_dev, per_dev)
    scale = head_dim ** (-0.5)

    def update(state, kv_block, key_start, block_len):
        run_max, run_sum, accum = state
        scores = (
            jnp.einsum("hqd,hkd->hqk", queries, kv_block[0], preferred_element_type=jnp.float32)
            * scale
        )
        coords = lax.dynamic_slice_in_dim(cycle_feats, key_start, block_len, 1)
        cos_bias = jnp.dot(query_feats.T, coords, precision=highest)
        scores = scores + strengths[:, None, None] * cos_bias[None]
        new_max = jnp.maximum(run_max, jnp.max(scores, axis=-1))
        keep_part = jnp.exp(run_max - new_max)
        weights = jnp.exp(scores - new_max[:, :, None])
        run_sum = run_sum * keep_part + jnp.sum(weights, axis=-1)
        prob_bf = weights.astype(jnp.bfloat16)
        accum = accum * keep_part[:, None, :] + jnp.einsum(
            "hqk,hkd->hdq", prob_bf, kv_block[1], preferred_element_type=jnp.float32
        )
        return (new_max, run_sum, accum)

    initial = (
        jnp.full((per_dev, query_count), -1e30, jnp.float32),
        jnp.zeros((per_dev, query_count), jnp.float32),
        jnp.zeros((per_dev, head_dim, query_count), jnp.float32),
    )
    piece = lax.all_gather(key_vals, "cols", axis=2, tiled=True)
    key_total = piece.shape[2] // head_dim
    if key_total > 1024 and key_total % 1024 == 0:
        block_len = 1024
    else:
        block_len = key_total
    block_count = key_total // block_len
    kv_blocks = piece.reshape(2, per_dev, block_count, block_len, head_dim).transpose(2, 0, 1, 3, 4)
    block_starts = jnp.arange(block_count, dtype=jnp.int32) * block_len

    def one_block(state, block_in):
        kv_block, key_start = block_in
        return (update(state, kv_block, key_start, block_len), None)

    state, _ = lax.scan(one_block, initial, (kv_blocks, block_starts))
    _, run_sum, accum = state
    head_out = (
        (accum / run_sum[:, None, :])
        .transpose(0, 2, 1)
        .astype(jnp.bfloat16)
        .reshape(per_dev, query_count * head_dim)
    )
    returned = lax.all_to_all(head_out, "rows", split_axis=1, concat_axis=0, tiled=True)
    global_out = (
        returned.reshape(head_count, atom_count, head_dim)
        .transpose(1, 0, 2)
        .reshape(atom_count, model_dim)
    )
    combined = (local_out.astype(jnp.float32) + global_out.astype(jnp.float32)).astype(jnp.bfloat16)
    updated = features.astype(jnp.float32) + jnp.dot(
        combined, w_out, preferred_element_type=jnp.float32
    )
    return updated.astype(jnp.bfloat16)


def mm(a, b, dims):
    return lax.dot_general(a, b, (dims, ((), ())), preferred_element_type=jnp.float32)


def parts_of(value, count):
    out = []
    for _ in range(count):
        part = value.astype(jnp.bfloat16)
        out.append(part)
        value = value - part.astype(jnp.float32)
    return out


def unit(rows, cols, dtype):
    r = lax.broadcasted_iota(jnp.int32, (rows, cols), 0)
    c = lax.broadcasted_iota(jnp.int32, (rows, cols), 1)
    return (r == c).astype(dtype)


def to_column(row):
    count = row.shape[1]
    r = lax.broadcasted_iota(jnp.int32, (count, count), 0)
    c = lax.broadcasted_iota(jnp.int32, (count, count), 1)
    return jnp.sum(jnp.where(r == c, jnp.broadcast_to(row, (count, count)), 0.0), axis=1, keepdims=True)


def fetch(pairs, sems):
    copies = [pltpu.make_async_copy(src, dst, sems.at[k]) for k, (src, dst) in enumerate(pairs)]
    for copy in copies:
        copy.start()
    for copy in copies:
        copy.wait()


def pack_kernel(feat_hbm, gain_hbm, pos_hbm, out_ref, feat_ref, gain_ref, pos_ref, tmp_ref, sems):
    fetch(((feat_hbm, feat_ref), (gain_hbm, gain_ref), (pos_hbm, pos_ref)), sems)
    atoms, dim = feat_ref.shape
    floats = feat_ref[...].astype(jnp.float32)
    spread = jnp.mean(floats * floats, axis=-1, keepdims=True)
    normed = floats * lax.rsqrt(spread + 1e-06) * gain_ref[...]
    out_ref[:, :dim] = normed.astype(jnp.bfloat16)
    tmp_ref[...] = jnp.zeros(tmp_ref.shape, jnp.float32)
    for p, part in enumerate(parts_of(pos_ref[...], 3)):
        tmp_ref[8 * p : 8 * p + 3, :] = part.astype(jnp.float32)
    eye = unit(atoms, atoms, jnp.bfloat16)
    turned = mm(eye, tmp_ref[...].astype(jnp.bfloat16), ((1,), (1,)))
    out_ref[:, dim:] = turned.astype(jnp.bfloat16)


def query_kernel(
    head_dim,
    wqkv_hbm,
    rw_hbm,
    ro_hbm,
    pw_hbm,
    cs_hbm,
    pack_ref,
    qexp_ref,
    w1_ref,
    w2_ref,
    str_ref,
    own_ref,
    wq_ref,
    rw_ref,
    ro_ref,
    pw_ref,
    cs_ref,
    sems,
):
    atoms = pack_ref.shape[0]
    dim = wq_ref.shape[0]
    fetch(
        (
            (wqkv_hbm.at[:, pl.ds(0, dim)], wq_ref),
            (rw_hbm, rw_ref),
            (ro_hbm, ro_ref),
            (pw_hbm, pw_ref),
            (cs_hbm, cs_ref),
        ),
        sems,
    )
    groups, rows, width = qexp_ref.shape
    per = rows // atoms
    q = mm(pack_ref[:, :dim], wq_ref[...], ((1,), (0,)))
    q = q.astype(jnp.bfloat16).astype(jnp.float32)
    lane = lax.broadcasted_iota(jnp.int32, (per, width), 1) // head_dim
    sub = lax.broadcasted_iota(jnp.int32, (per, width), 0)
    keep = (lane == sub)[None]
    for g in range(groups):
        part = q[:, g * width : (g + 1) * width]
        spread = jnp.broadcast_to(part[:, None, :], (atoms, per, width))
        spread = jnp.where(keep, spread, 0.0).reshape(rows, width)
        qexp_ref[g] = spread.astype(jnp.bfloat16)
    h, m, l = parts_of(0.5 * rw_ref[...], 3)
    hidden = rw_ref.shape[1]
    row = lax.broadcasted_iota(jnp.int32, (16, hidden), 0)
    tail = jnp.zeros((16, hidden), jnp.float32)
    for k, part in enumerate(parts_of(0.5 * ro_ref[...], 3)):
        tail = jnp.where(row == k, part.astype(jnp.float32), tail)
    stack = jnp.concatenate([h, h, m, h, l, m, tail.astype(jnp.bfloat16)], axis=0)
    w1_ref[...] = mm(unit(hidden, hidden, jnp.bfloat16), stack, ((1,), (1,))).astype(jnp.bfloat16)
    h, l = parts_of(pw_ref[...], 2)
    w2_ref[...] = jnp.concatenate([h, h, l], axis=1)
    str_ref[...] = jnp.broadcast_to(to_column(cs_ref[...]), str_ref.shape)
    pos = pack_ref[:, dim:].astype(jnp.float32)
    pos = pos + pltpu.roll(pos, 120, 1) + pltpu.roll(pos, 112, 1)
    own_ref[0] = pos
    own_ref[1] = jnp.cos(two_pi * pos)
    own_ref[2] = jnp.sin(two_pi * pos)


def repack_kernel(*refs):
    blocks, out_ref = refs[:-1], refs[-1]
    atoms = blocks[0].shape[0]
    dim = out_ref.shape[1]
    count = atoms * len(blocks)
    for k, block in enumerate(blocks):
        out_ref[k * atoms : (k + 1) * atoms, :] = block[:, :dim]
    pos = jnp.concatenate([block[:, dim:] for block in blocks], axis=0)
    r = lax.broadcasted_iota(jnp.int32, (8, 128), 0)
    c = lax.broadcasted_iota(jnp.int32, (8, 128), 1)
    tail = []
    for p in range(3):
        pick = ((c == 8 * p + r) & (r < 3)).astype(jnp.bfloat16)
        tail.append(mm(pick, pos, ((1,), (1,))))
    tail.append(jnp.zeros((8, dim - 3 * count), jnp.float32))
    out_ref[count:, :] = jnp.concatenate(tail, axis=1).astype(jnp.bfloat16)


def piece_positions(piece_ref, count):
    tail = piece_ref[count:, :].astype(jnp.float32)
    return tail[:, :count] + tail[:, count : 2 * count] + tail[:, 2 * count : 3 * count]


def attend(qexp, keys, vals, scale, bias3):
    rows = qexp.shape[0]
    count = keys.shape[0]
    atoms, per, _ = bias3.shape
    s = mm(qexp, keys, ((1,), (1,))).reshape(atoms, per, count) * scale + bias3
    top = jnp.max(s, axis=-1, keepdims=True)
    p = jnp.exp(s - top)
    total = jnp.sum(p, axis=-1, keepdims=True)
    o = mm(p.astype(jnp.bfloat16).reshape(rows, count), vals, ((1,), (0,)))
    return top, total, o.reshape(atoms, per, vals.shape[1])


def absorb(head_dim, places, pieces, wqkv_ref, qexp_ref, str_ref, own_ref, kv_ref):
    dim = wqkv_ref.shape[0]
    atoms = own_ref.shape[1]
    groups, rows, width = qexp_ref.shape
    per = rows // atoms
    count = pieces[0].shape[0] - 8
    rows_in = jnp.concatenate([piece[:count, :] for piece in pieces], axis=0)
    kv = mm(rows_in, wqkv_ref[:, dim:], ((1,), (0,))).astype(jnp.bfloat16)
    for k, place in enumerate(places):
        kv_ref[place * count : (place + 1) * count, :] = kv[k * count : (k + 1) * count]
    pos8 = jnp.concatenate([piece_positions(piece, count) for piece in pieces], axis=1)
    cos_k, sin_k = jnp.cos(two_pi * pos8), jnp.sin(two_pi * pos8)
    waves = None
    for c in range(3):
        term = own_ref[1, :, c : c + 1] * cos_k[c : c + 1] + own_ref[2, :, c : c + 1] * sin_k[c : c + 1]
        waves = term if waves is None else waves + term
    out = []
    for g in range(groups):
        low, high = g * width, (g + 1) * width
        bias3 = str_ref[g * per : (g + 1) * per, :1][None] * waves[:, None, :]
        out.append(
            attend(
                qexp_ref[g],
                kv[:, low:high],
                kv[:, dim + low : dim + high],
                head_dim ** (-0.5),
                bias3,
            )
        )
    return out


def widen(column, lanes):
    return jnp.broadcast_to(column, column.shape[:-1] + (lanes,))


def repeat_lanes(array, lanes):
    return jnp.concatenate([array] * (lanes // array.shape[-1]), axis=-1)


def first_kernel(head_dim, places, *refs):
    pieces = refs[: len(places)]
    wqkv_ref, qexp_ref, str_ref, own_ref = refs[len(places) : -4]
    kv_ref, acc_ref, top_ref, sum_ref = refs[-4:]
    got = absorb(head_dim, places, pieces, wqkv_ref, qexp_ref, str_ref, own_ref, kv_ref)
    for g, (top, total, o) in enumerate(got):
        acc_ref[g] = o
        top_ref[g] = widen(top, 128)
        sum_ref[g] = widen(total, 128)


def merge(got, g, acc_ref, top_ref, sum_ref):
    top, total, o = got[g]
    width = o.shape[-1]
    best = jnp.maximum(widen(top, 128), top_ref[g])
    a, b = jnp.exp(top_ref[g] - best), jnp.exp(widen(top, 128) - best)
    summed = a * sum_ref[g] + b * widen(total, 128)
    acc = repeat_lanes(a, width) * acc_ref[g] + repeat_lanes(b, width) * o
    return best, summed, acc


def next_kernel(head_dim, places, *refs):
    pieces = refs[: len(places)]
    wqkv_ref, qexp_ref, str_ref, own_ref = refs[len(places) : len(places) + 4]
    _, acc_in, top_in, sum_in, kv_ref, acc_ref, top_ref, sum_ref = refs[len(places) + 4 :]
    got = absorb(head_dim, places, pieces, wqkv_ref, qexp_ref, str_ref, own_ref, kv_ref)
    for g in range(len(got)):
        best, summed, acc = merge(got, g, acc_in, top_in, sum_in)
        acc_ref[g] = acc
        top_ref[g] = best
        sum_ref[g] = summed


def chosen(scalars, lane):
    out = jnp.full(lane.shape, scalars[0])
    for e in range(1, len(scalars)):
        out = jnp.where(lane == e, scalars[e], out)
    return out


def last_kernel(head_dim, locate, col_count, list_ref, valid_ref, shift_ref, cell_ref, *refs):
    piece_refs = refs[:8]
    (
        wqkv_ref,
        qexp_ref,
        str_ref,
        own_ref,
        w1_ref,
        w2_ref,
        wout_ref,
        in_ref,
        _,
        acc_in,
        top_in,
        sum_in,
        out_ref,
        kv_ref,
        near_ref,
        pos_ref,
        bias_ref,
    ) = refs[8:]
    dim = wqkv_ref.shape[0]
    atoms = own_ref.shape[1]
    groups, rows, width = qexp_ref.shape
    per = rows // atoms
    count = piece_refs[0].shape[0] - 8
    got = absorb(head_dim, (7,), piece_refs[7:], wqkv_ref, qexp_ref, str_ref, own_ref, kv_ref)
    for k in range(8):
        pos_ref[k] = piece_positions(piece_refs[k], count)
    me = lax.axis_index("rows") * col_count + lax.axis_index("cols")
    entries = list_ref.shape[1]
    listed = entries * atoms
    lane = lax.broadcasted_iota(jnp.int32, (1, listed), 1) // atoms
    in_tile = lax.broadcasted_iota(jnp.int32, (1, count), 1) // atoms
    a_tile = count // atoms
    tiles = []
    for e in range(entries):
        up, across, turn = locate(list_ref[0, e] ^ me)
        place = across + 4 * turn
        start = pl.multiple_of((place * a_tile + up) * atoms, atoms)
        near_ref[e * atoms : (e + 1) * atoms, :] = kv_ref[pl.ds(start, atoms), :]
        into = e % a_tile
        moved = pltpu.roll(pos_ref[place], (into - up + a_tile) % a_tile * atoms, 1)
        if into == 0:
            tiles.append(moved)
        else:
            tiles[-1] = jnp.where(in_tile == into, moved, tiles[-1])
    near = jnp.concatenate(tiles, axis=1)
    square = None
    for c in range(3):
        at = near[c : c + 1] + chosen([shift_ref[c, 0, e] for e in range(entries)], lane).astype(jnp.float32)
        gap = (at - own_ref[0, :, c : c + 1]) * cell_ref[c]
        square = gap * gap if square is None else square + gap * gap
    dist = jnp.sqrt(square + 0.25)
    nrbf = (w1_ref.shape[1] - 16) // 6
    centers = lax.broadcasted_iota(jnp.int32, (nrbf, 1), 0).astype(jnp.float32) * rbf_step
    step = 16
    ones = jnp.ones((16, step * listed), jnp.bfloat16)
    for i in range(0, atoms, step):
        gap = jnp.concatenate([dist[j : j + 1] - centers for j in range(i, i + step)], axis=1)
        radial = jnp.exp(gap * gap * (-0.5 / rbf_width**2))
        h, m, l = parts_of(radial, 3)
        stack = jnp.concatenate([h, m, h, l, h, m, ones], axis=0)
        u = mm(w1_ref[...], stack, ((1,), (0,)))
        u = u + u * jnp.tanh(u)
        h, l = parts_of(u, 2)
        pair = mm(w2_ref[...], jnp.concatenate([h, l, h], axis=0), ((1,), (0,)))
        for j in range(step):
            for g in range(groups):
                bias_ref[g, i + j] = pair[g * per : (g + 1) * per, j * listed : (j + 1) * listed]
    lane3 = lax.broadcasted_iota(jnp.int32, (1, 1, listed), 2) // atoms
    live = chosen([valid_ref[0, e] for e in range(entries)], lane3) > 0
    block = lax.broadcasted_iota(jnp.int32, (1, per, width), 2) // head_dim
    keep = block == lax.broadcasted_iota(jnp.int32, (1, per, width), 1)
    pieces = []
    for g in range(groups):
        low, high = g * width, (g + 1) * width
        _, summed, far = merge(got, g, acc_in, top_in, sum_in)
        far = far / repeat_lanes(summed, width)
        far = jnp.sum(jnp.where(keep, far, 0.0), axis=1).astype(jnp.bfloat16)
        s = mm(qexp_ref[g], near_ref[:, low:high], ((1,), (1,)))
        s = s.reshape(atoms, per, listed) * head_dim ** (-0.5) + bias_ref[g]
        s = jnp.where(live, s, -1e30)
        p = jnp.exp(s - jnp.max(s, axis=-1, keepdims=True))
        summed = jnp.sum(p, axis=-1, keepdims=True)
        o = mm(
            p.astype(jnp.bfloat16).reshape(rows, listed),
            near_ref[:, dim + low : dim + high],
            ((1,), (0,)),
        )
        o = o.reshape(atoms, per, width) / summed
        close = jnp.sum(jnp.where(keep, o, 0.0), axis=1).astype(jnp.bfloat16)
        pieces.append((close.astype(jnp.float32) + far.astype(jnp.float32)).astype(jnp.bfloat16))
    combined = jnp.concatenate(pieces, axis=1)
    moved = mm(combined, wout_ref[...], ((1,), (0,)))
    out_ref[...] = (in_ref[...].astype(jnp.float32) + moved).astype(jnp.bfloat16)


def call(kernel, outs, scratch, smem, args, aliases=None, hbm=0):
    vmem = pl.BlockSpec(memory_space=pltpu.VMEM)
    first = smem + hbm
    specs = [pl.BlockSpec(memory_space=pltpu.SMEM)] * smem
    specs += [pl.BlockSpec(memory_space=pltpu.HBM)] * hbm + [vmem] * (len(args) - first)
    placed = [pltpu.with_memory_space_constraint(a, pltpu.HBM) for a in args[smem:first]]
    placed += [pltpu.with_memory_space_constraint(a, pltpu.VMEM) for a in args[first:]]
    many = isinstance(outs, list)
    return pl.pallas_call(
        kernel,
        out_shape=outs,
        in_specs=specs,
        out_specs=[vmem] * len(outs) if many else vmem,
        scratch_shapes=scratch,
        input_output_aliases=aliases or {},
        compiler_params=pltpu.CompilerParams(vmem_limit_bytes=24 << 20),
    )(*args[:smem], *placed)


def on_device_small(
    features,
    positions,
    cell_lengths,
    block_lists,
    image_offsets,
    block_valid,
    norm_gain,
    w_qkv,
    w_out,
    rbf_weight,
    rbf_offset,
    pair_weight,
    cosine_scale,
):
    atoms, dim = features.shape
    heads = pair_weight.shape[1]
    hidden = pair_weight.shape[0]
    nrbf = rbf_weight.shape[0]
    head_dim = dim // heads
    row_count = lax.axis_size("rows")
    col_count = lax.axis_size("cols")
    total = row_count * col_count
    axes = ("rows", "cols")
    col_bits = col_count.bit_length() - 1
    flip = 1 << col_bits
    across_bits = (0, col_bits + 1)
    entries = block_lists.shape[1]
    width = 256
    per = width // head_dim
    groups = heads // per
    rows = atoms * per
    f32, bf16 = jnp.float32, jnp.bfloat16
    vm = pltpu.VMEM

    def swap(array, mask):
        return lax.ppermute(array, axes, [(i, i ^ mask) for i in range(total)])

    def locate(rel):
        up = (rel >> 1) & 3
        across = (rel & 1) + 2 * ((rel >> across_bits[1]) & 1)
        turn = (rel >> col_bits) & 1
        turn = turn ^ jnp.minimum(up, 1) ^ jnp.minimum(across, 1)
        return up, across, turn

    tied = lax.optimization_barrier
    pack = call(
        pack_kernel,
        vm((atoms, dim + 128), bf16),
        [
            vm((atoms, dim), bf16),
            vm((1, dim), f32),
            vm(positions.shape, f32),
            vm((128, atoms), f32),
            pltpu.SemaphoreType.DMA((3,)),
        ],
        0,
        (features, norm_gain[None], positions),
        hbm=3,
    )
    ups = [swap(pack, (d << 1) | flip) for d in (1, 2, 3)]
    ready = call(
        functools.partial(query_kernel, head_dim),
        [
            vm((groups, rows, width), bf16),
            vm((hidden, 6 * nrbf + 16), bf16),
            vm((heads, 3 * hidden), bf16),
            vm((heads, 128), f32),
            vm((3, atoms, 128), f32),
        ],
        [
            vm((dim, dim), bf16),
            vm((nrbf, hidden), f32),
            vm((1, hidden), f32),
            vm((heads, hidden), f32),
            vm((1, heads), f32),
            pltpu.SemaphoreType.DMA((5,)),
        ],
        0,
        (w_qkv, rbf_weight, rbf_offset[None], pair_weight.T, cosine_scale[None], pack),
        hbm=5,
    )
    ups, ready = tied((ups, ready))
    qexp, w1, w2, strength, own = ready
    count = 4 * atoms
    base = call(repack_kernel, vm((count + 8, dim), bf16), [], 0, (pack, *ups))
    east = swap(base, 1 | flip)
    north = swap(base, (1 << across_bits[1]) | flip)
    diag = swap(base, 1 | (1 << across_bits[1]) | flip)
    state_shapes = [
        vm((8 * count, 2 * dim), bf16),
        vm((groups, atoms, per, width), f32),
        vm((groups, atoms, per, 128), f32),
        vm((groups, atoms, per, 128), f32),
    ]
    common = (w_qkv, qexp, strength, own)

    def step(places, pieces, state):
        if state is None:
            return call(
                functools.partial(first_kernel, head_dim, places),
                state_shapes,
                [],
                0,
                (*pieces, *common),
            )
        at = len(pieces) + len(common)
        return call(
            functools.partial(next_kernel, head_dim, places),
            state_shapes,
            [],
            0,
            (*pieces, *common, *state),
            {at + k: k for k in range(4)},
        )

    state = step((0,), (base,), None)
    base_late, state = tied((base, state))
    base2 = swap(base_late, flip)
    base2, state = tied((base2, state))
    state = step((4,), (base2,), state)
    east, north, state = tied((east, north, state))
    east2, north2 = swap(east, flip), swap(north, flip)
    state = step((1, 2), (east, north), state)
    diag, state = tied((diag, state))
    diag2 = swap(diag, flip)
    state = step((3, 5, 6), (diag, east2, north2), state)
    diag2, state = tied((diag2, state))
    updated, _ = call(
        functools.partial(last_kernel, head_dim, locate, col_count),
        [jax.ShapeDtypeStruct((atoms, dim), bf16), state_shapes[0]],
        [
            vm((entries * atoms, 2 * dim), bf16),
            vm((8, 8, count), f32),
            vm((groups, atoms, per, entries * atoms), f32),
        ],
        4,
        (
            block_lists,
            block_valid,
            image_offsets,
            cell_lengths,
            base,
            east,
            north,
            diag,
            base2,
            east2,
            north2,
            diag2,
            *common,
            w1,
            w2,
            w_out,
            features,
            *state,
        ),
        {4 + 8 + len(common) + 4: 1},
    )
    return updated


def solution(mesh):
    row_count, col_count = mesh.shape["rows"], mesh.shape["cols"]
    small = (row_count, col_count) == (4, 8)
    body = on_device_small if small else on_device
    return jax.shard_map(
        body,
        mesh=mesh,
        in_specs=(
            P(("rows", "cols"), None),
            P(None, ("rows", "cols")),
            P(),
            P(("rows", "cols"), None),
            P(None, ("rows", "cols"), None),
            P(("rows", "cols"), None),
            P(),
            P(),
            P(),
            P(),
            P(),
            P(),
            P(),
        ),
        out_specs=P(("rows", "cols"), None),
        check_vma=False,
    )
```

```python
import functools
import math

import jax
import jax.numpy as jnp
from jax import lax
from jax.experimental import pallas as pl
from jax.experimental.pallas import tpu as pltpu
from jax.sharding import PartitionSpec as P


rbf_step = 2.0
rbf_width = 2.0
two_pi = 2.0 * math.pi
highest = lax.Precision.HIGHEST


def with_halo(cells, sides, width):
    for axis, dim in sides:
        count = lax.axis_size(axis)
        head = lax.slice_in_dim(cells, 0, width, axis=dim)
        tail = lax.slice_in_dim(cells, cells.shape[dim] - width, cells.shape[dim], axis=dim)
        cells = jnp.concatenate(
            [
                lax.ppermute(tail, axis, [(i, (i + 1) % count) for i in range(count)]),
                cells,
                lax.ppermute(head, axis, [((i + 1) % count, i) for i in range(count)]),
            ],
            axis=dim,
        )
    return cells


def rms_rows(values, norm_gain):
    floats = values.astype(jnp.float32)
    spread = jnp.mean(floats * floats, axis=-1, keepdims=True)
    return (floats * lax.rsqrt(spread + 1e-06) * norm_gain).astype(jnp.bfloat16)


def near_attention(
    query_rows,
    own_pos,
    keys,
    key_pos,
    shifts,
    live,
    cell_lengths,
    rbf_weight,
    rbf_offset,
    pair_weight,
):
    entries, block_len = (keys.shape[0], keys.shape[1])
    model_dim = query_rows.shape[1]
    head_count = pair_weight.shape[1]
    head_dim = model_dim // head_count
    key_coords = key_pos.transpose(1, 0, 2) + shifts.astype(jnp.float32)[:, :, None]
    key_coords = key_coords.reshape(3, entries * block_len)
    displace = (key_coords[:, None, :] - own_pos[:, :, None]) * cell_lengths[:, None, None]
    distance = jnp.sqrt(jnp.sum(displace * displace, axis=0) + 0.25)
    centers = jnp.arange(rbf_weight.shape[0], dtype=jnp.float32) * rbf_step
    radial = jnp.exp(-((distance[None] - centers[:, None, None]) ** 2) * (0.5 / rbf_width**2))
    radial = radial.reshape(rbf_weight.shape[0], -1)
    hidden = jax.nn.silu(jnp.dot(rbf_weight.T, radial, precision=highest) + rbf_offset[:, None])
    pair_bias = jnp.dot(pair_weight.T, hidden, precision=highest).reshape(
        head_count, query_rows.shape[0], entries * block_len
    )
    query_heads = query_rows.reshape(-1, head_count, head_dim)
    key_heads = keys[:, :, :model_dim].reshape(entries * block_len, head_count, head_dim)
    value_heads = keys[:, :, model_dim:].reshape(entries * block_len, head_count, head_dim)
    scores = (
        jnp.einsum("ahd,khd->hak", query_heads, key_heads, preferred_element_type=jnp.float32)
        * head_dim ** (-0.5)
        + pair_bias
    )
    allowed = jnp.repeat(live > 0, block_len)
    scores = jnp.where(allowed[None, None, :], scores, -1e30)
    row_max = jnp.max(scores, axis=-1, keepdims=True)
    weights = jnp.exp(scores - row_max)
    row_sum = jnp.sum(weights, axis=-1, keepdims=True)
    prob_bf = weights.astype(jnp.bfloat16)
    attended = jnp.einsum(
        "hak,khd->ahd", prob_bf, value_heads, preferred_element_type=jnp.float32
    ) / row_sum.transpose(1, 0, 2)
    return attended.reshape(-1, model_dim).astype(jnp.bfloat16)


def on_device(
    features,
    positions,
    cell_lengths,
    block_lists,
    image_offsets,
    block_valid,
    norm_gain,
    w_qkv,
    w_out,
    rbf_weight,
    rbf_offset,
    pair_weight,
    cosine_scale,
):
    atom_count, model_dim = features.shape
    head_count = pair_weight.shape[1]
    head_dim = model_dim // head_count
    row_count = lax.axis_size("rows")
    col_count = lax.axis_size("cols")
    row_index = lax.axis_index("rows")
    col_index = lax.axis_index("cols")
    per_dev = head_count // row_count
    normed = rms_rows(features, norm_gain)
    packed = jnp.dot(normed, w_qkv, preferred_element_type=jnp.float32).astype(jnp.bfloat16)
    every_pos = lax.all_gather(positions, ("rows", "cols"), axis=1, tiled=True)
    near_rows = with_halo(normed[None, None], (("rows", 0), ("cols", 1)), 1)
    near_kv = jnp.dot(
        near_rows.reshape(9 * atom_count, model_dim),
        w_qkv[:, model_dim:],
        preferred_element_type=jnp.float32,
    )
    near_kv = near_kv.astype(jnp.bfloat16).reshape(9, atom_count, 2 * model_dim)
    listed = block_lists[0]
    list_row = listed // col_count
    list_col = listed % col_count
    slots = (list_row - row_index + 1) % row_count * 3 + (list_col - col_index + 1) % col_count
    keys = jnp.take(near_kv, slots, axis=0)
    block_pos = every_pos.reshape(3, row_count * col_count, atom_count)
    key_pos = jnp.take(block_pos, listed, axis=1).transpose(1, 0, 2)
    local_out = near_attention(
        packed[:, :model_dim],
        positions,
        keys,
        key_pos,
        image_offsets[:, 0, :],
        block_valid[0],
        cell_lengths,
        rbf_weight,
        rbf_offset,
        pair_weight,
    )
    grouped = (
        packed.reshape(atom_count, 3, head_count, head_dim)
        .transpose(1, 2, 0, 3)
        .reshape(3, head_count, atom_count * head_dim)
    )
    regrouped = lax.all_to_all(grouped, "rows", split_axis=1, concat_axis=2, tiled=True)
    query_count = row_count * atom_count
    queries = regrouped[0].reshape(per_dev, query_count, head_dim)
    key_vals = regrouped[1:]
    cycle_pos = (
        every_pos.reshape(3, row_count, col_count, atom_count).transpose(0, 2, 1, 3).reshape(3, -1)
    )
    query_pos = lax.dynamic_slice_in_dim(cycle_pos, col_index * query_count, query_count, 1)
    cycle_feats = jnp.concatenate(
        [jnp.cos(two_pi * cycle_pos), jnp.sin(two_pi * cycle_pos)], axis=0
    )
    query_feats = jnp.concatenate(
        [jnp.cos(two_pi * query_pos), jnp.sin(two_pi * query_pos)], axis=0
    )
    strengths = lax.dynamic_slice_in_dim(cosine_scale, row_index * per_dev, per_dev)
    scale = head_dim ** (-0.5)

    def update(state, kv_block, key_start, block_len):
        run_max, run_sum, accum = state
        scores = (
            jnp.einsum("hqd,hkd->hqk", queries, kv_block[0], preferred_element_type=jnp.float32)
            * scale
        )
        coords = lax.dynamic_slice_in_dim(cycle_feats, key_start, block_len, 1)
        cos_bias = jnp.dot(query_feats.T, coords, precision=highest)
        scores = scores + strengths[:, None, None] * cos_bias[None]
        new_max = jnp.maximum(run_max, jnp.max(scores, axis=-1))
        keep_part = jnp.exp(run_max - new_max)
        weights = jnp.exp(scores - new_max[:, :, None])
        run_sum = run_sum * keep_part + jnp.sum(weights, axis=-1)
        prob_bf = weights.astype(jnp.bfloat16)
        accum = accum * keep_part[:, None, :] + jnp.einsum(
            "hqk,hkd->hdq", prob_bf, kv_block[1], preferred_element_type=jnp.float32
        )
        return (new_max, run_sum, accum)

    initial = (
        jnp.full((per_dev, query_count), -1e30, jnp.float32),
        jnp.zeros((per_dev, query_count), jnp.float32),
        jnp.zeros((per_dev, head_dim, query_count), jnp.float32),
    )
    piece = lax.all_gather(key_vals, "cols", axis=2, tiled=True)
    key_total = piece.shape[2] // head_dim
    if key_total > 1024 and key_total % 1024 == 0:
        block_len = 1024
    else:
        block_len = key_total
    block_count = key_total // block_len
    kv_blocks = piece.reshape(2, per_dev, block_count, block_len, head_dim).transpose(2, 0, 1, 3, 4)
    block_starts = jnp.arange(block_count, dtype=jnp.int32) * block_len

    def one_block(state, block_in):
        kv_block, key_start = block_in
        return (update(state, kv_block, key_start, block_len), None)

    state, _ = lax.scan(one_block, initial, (kv_blocks, block_starts))
    _, run_sum, accum = state
    head_out = (
        (accum / run_sum[:, None, :])
        .transpose(0, 2, 1)
        .astype(jnp.bfloat16)
        .reshape(per_dev, query_count * head_dim)
    )
    returned = lax.all_to_all(head_out, "rows", split_axis=1, concat_axis=0, tiled=True)
    global_out = (
        returned.reshape(head_count, atom_count, head_dim)
        .transpose(1, 0, 2)
        .reshape(atom_count, model_dim)
    )
    combined = (local_out.astype(jnp.float32) + global_out.astype(jnp.float32)).astype(jnp.bfloat16)
    updated = features.astype(jnp.float32) + jnp.dot(
        combined, w_out, preferred_element_type=jnp.float32
    )
    return updated.astype(jnp.bfloat16)


def mm(a, b, dims):
    return lax.dot_general(a, b, (dims, ((), ())), preferred_element_type=jnp.float32)


def parts_of(value, count):
    out = []
    for _ in range(count):
        part = value.astype(jnp.bfloat16)
        out.append(part)
        value = value - part.astype(jnp.float32)
    return out


def unit(rows, cols, dtype):
    r = lax.broadcasted_iota(jnp.int32, (rows, cols), 0)
    c = lax.broadcasted_iota(jnp.int32, (rows, cols), 1)
    return (r == c).astype(dtype)


def to_column(row):
    count = row.shape[1]
    r = lax.broadcasted_iota(jnp.int32, (count, count), 0)
    c = lax.broadcasted_iota(jnp.int32, (count, count), 1)
    return jnp.sum(jnp.where(r == c, jnp.broadcast_to(row, (count, count)), 0.0), axis=1, keepdims=True)


def fetch(pairs, sems):
    copies = [pltpu.make_async_copy(src, dst, sems.at[k]) for k, (src, dst) in enumerate(pairs)]
    for copy in copies:
        copy.start()
    return copies


def settle(copies):
    for copy in copies:
        copy.wait()


def pack_kernel(feat_hbm, gain_hbm, pos_hbm, out_ref, feat_ref, gain_ref, pos_ref, tmp_ref, sems):
    settle(fetch(((feat_hbm, feat_ref), (gain_hbm, gain_ref), (pos_hbm, pos_ref)), sems))
    atoms, dim = feat_ref.shape
    floats = feat_ref[...].astype(jnp.float32)
    spread = jnp.mean(floats * floats, axis=-1, keepdims=True)
    normed = floats * lax.rsqrt(spread + 1e-06) * gain_ref[...]
    out_ref[:, :dim] = normed.astype(jnp.bfloat16)
    tmp_ref[...] = jnp.zeros(tmp_ref.shape, jnp.float32)
    for p, part in enumerate(parts_of(pos_ref[...], 3)):
        tmp_ref[8 * p : 8 * p + 3, :] = part.astype(jnp.float32)
    eye = unit(atoms, atoms, jnp.bfloat16)
    turned = mm(eye, tmp_ref[...].astype(jnp.bfloat16), ((1,), (1,)))
    out_ref[:, dim:] = turned.astype(jnp.bfloat16)


def query_kernel(
    head_dim,
    wqkv_hbm,
    rw_hbm,
    ro_hbm,
    pw_hbm,
    cs_hbm,
    pack_ref,
    qexp_ref,
    w1_ref,
    w2_ref,
    str_ref,
    own_ref,
    wq_ref,
    rw_ref,
    ro_ref,
    pw_ref,
    cs_ref,
    sems,
):
    atoms = pack_ref.shape[0]
    dim = wq_ref.shape[0]
    copies = fetch(
        (
            (wqkv_hbm.at[:, pl.ds(0, dim)], wq_ref),
            (rw_hbm, rw_ref),
            (ro_hbm, ro_ref),
            (pw_hbm, pw_ref),
            (cs_hbm, cs_ref),
        ),
        sems,
    )
    groups, rows, width = qexp_ref.shape
    per = rows // atoms
    pos = pack_ref[:, dim:].astype(jnp.float32)
    pos = pos + pltpu.roll(pos, 120, 1) + pltpu.roll(pos, 112, 1)
    own_ref[0] = pos
    own_ref[1] = jnp.cos(two_pi * pos)
    own_ref[2] = jnp.sin(two_pi * pos)
    settle(copies[1:])
    h, m, l = parts_of(0.5 * rw_ref[...], 3)
    hidden = rw_ref.shape[1]
    row = lax.broadcasted_iota(jnp.int32, (16, hidden), 0)
    tail = jnp.zeros((16, hidden), jnp.float32)
    for k, part in enumerate(parts_of(0.5 * ro_ref[...], 3)):
        tail = jnp.where(row == k, part.astype(jnp.float32), tail)
    stack = jnp.concatenate([h, h, m, h, l, m, tail.astype(jnp.bfloat16)], axis=0)
    w1_ref[...] = mm(unit(hidden, hidden, jnp.bfloat16), stack, ((1,), (1,))).astype(jnp.bfloat16)
    h, l = parts_of(pw_ref[...], 2)
    w2_ref[...] = jnp.concatenate([h, h, l], axis=1)
    str_ref[...] = jnp.broadcast_to(to_column(cs_ref[...]), str_ref.shape)
    settle(copies[:1])
    q = mm(pack_ref[:, :dim], wq_ref[...], ((1,), (0,)))
    q = q.astype(jnp.bfloat16).astype(jnp.float32)
    lane = lax.broadcasted_iota(jnp.int32, (per, width), 1) // head_dim
    sub = lax.broadcasted_iota(jnp.int32, (per, width), 0)
    keep = (lane == sub)[None]
    for g in range(groups):
        part = q[:, g * width : (g + 1) * width]
        spread = jnp.broadcast_to(part[:, None, :], (atoms, per, width))
        spread = jnp.where(keep, spread, 0.0).reshape(rows, width)
        qexp_ref[g] = spread.astype(jnp.bfloat16)


def repack_kernel(*refs):
    blocks, out_ref = refs[:-1], refs[-1]
    atoms = blocks[0].shape[0]
    dim = out_ref.shape[1]
    count = atoms * len(blocks)
    for k, block in enumerate(blocks):
        out_ref[k * atoms : (k + 1) * atoms, :] = block[:, :dim]
    pos = jnp.concatenate([block[:, dim:] for block in blocks], axis=0)
    r = lax.broadcasted_iota(jnp.int32, (8, 128), 0)
    c = lax.broadcasted_iota(jnp.int32, (8, 128), 1)
    tail = []
    for p in range(3):
        pick = ((c == 8 * p + r) & (r < 3)).astype(jnp.bfloat16)
        tail.append(mm(pick, pos, ((1,), (1,))))
    tail.append(jnp.zeros((8, dim - 3 * count), jnp.float32))
    out_ref[count:, :] = jnp.concatenate(tail, axis=1).astype(jnp.bfloat16)


def piece_positions(piece_ref, count):
    tail = piece_ref[count:, :].astype(jnp.float32)
    return tail[:, :count] + tail[:, count : 2 * count] + tail[:, 2 * count : 3 * count]


def attend(qexp, keys, vals, scale, bias3):
    rows = qexp.shape[0]
    count = keys.shape[0]
    atoms, per, _ = bias3.shape
    s = mm(qexp, keys, ((1,), (1,))).reshape(atoms, per, count) * scale + bias3
    top = jnp.max(s, axis=-1, keepdims=True)
    p = jnp.exp(s - top)
    total = jnp.sum(p, axis=-1, keepdims=True)
    o = mm(p.astype(jnp.bfloat16).reshape(rows, count), vals, ((1,), (0,)))
    return top, total, o.reshape(atoms, per, vals.shape[1])


def absorb(head_dim, places, pieces, wqkv_ref, qexp_ref, str_ref, own_ref, kv_ref):
    dim = wqkv_ref.shape[0]
    atoms = own_ref.shape[1]
    groups, rows, width = qexp_ref.shape
    per = rows // atoms
    count = pieces[0].shape[0] - 8
    rows_in = jnp.concatenate([piece[:count, :] for piece in pieces], axis=0)
    kv = mm(rows_in, wqkv_ref[:, dim:], ((1,), (0,))).astype(jnp.bfloat16)
    for k, place in enumerate(places):
        kv_ref[place * count : (place + 1) * count, :] = kv[k * count : (k + 1) * count]
    pos8 = jnp.concatenate([piece_positions(piece, count) for piece in pieces], axis=1)
    cos_k, sin_k = jnp.cos(two_pi * pos8), jnp.sin(two_pi * pos8)
    waves = None
    for c in range(3):
        term = own_ref[1, :, c : c + 1] * cos_k[c : c + 1] + own_ref[2, :, c : c + 1] * sin_k[c : c + 1]
        waves = term if waves is None else waves + term
    out = []
    for g in range(groups):
        low, high = g * width, (g + 1) * width
        bias3 = str_ref[g * per : (g + 1) * per, :1][None] * waves[:, None, :]
        out.append(
            attend(
                qexp_ref[g],
                kv[:, low:high],
                kv[:, dim + low : dim + high],
                head_dim ** (-0.5),
                bias3,
            )
        )
    return out


def widen(column, lanes):
    return jnp.broadcast_to(column, column.shape[:-1] + (lanes,))


def repeat_lanes(array, lanes):
    return jnp.concatenate([array] * (lanes // array.shape[-1]), axis=-1)


def first_kernel(head_dim, places, *refs):
    pieces = refs[: len(places)]
    wqkv_ref, qexp_ref, str_ref, own_ref = refs[len(places) : -4]
    kv_ref, acc_ref, top_ref, sum_ref = refs[-4:]
    got = absorb(head_dim, places, pieces, wqkv_ref, qexp_ref, str_ref, own_ref, kv_ref)
    for g, (top, total, o) in enumerate(got):
        acc_ref[g] = o
        top_ref[g] = widen(top, 128)
        sum_ref[g] = widen(total, 128)


def merge(got, g, acc_ref, top_ref, sum_ref):
    top, total, o = got[g]
    width = o.shape[-1]
    best = jnp.maximum(widen(top, 128), top_ref[g])
    a, b = jnp.exp(top_ref[g] - best), jnp.exp(widen(top, 128) - best)
    summed = a * sum_ref[g] + b * widen(total, 128)
    acc = repeat_lanes(a, width) * acc_ref[g] + repeat_lanes(b, width) * o
    return best, summed, acc


def next_kernel(head_dim, places, *refs):
    pieces = refs[: len(places)]
    wqkv_ref, qexp_ref, str_ref, own_ref = refs[len(places) : len(places) + 4]
    _, acc_in, top_in, sum_in, kv_ref, acc_ref, top_ref, sum_ref = refs[len(places) + 4 :]
    got = absorb(head_dim, places, pieces, wqkv_ref, qexp_ref, str_ref, own_ref, kv_ref)
    for g in range(len(got)):
        best, summed, acc = merge(got, g, acc_in, top_in, sum_in)
        acc_ref[g] = acc
        top_ref[g] = best
        sum_ref[g] = summed


def chosen(scalars, lane):
    out = jnp.full(lane.shape, scalars[0])
    for e in range(1, len(scalars)):
        out = jnp.where(lane == e, scalars[e], out)
    return out


def last_kernel(head_dim, locate, col_count, list_ref, valid_ref, shift_ref, cell_ref, *refs):
    piece_refs = refs[:8]
    (
        wqkv_ref,
        qexp_ref,
        str_ref,
        own_ref,
        w1_ref,
        w2_ref,
        wout_ref,
        in_ref,
        _,
        acc_in,
        top_in,
        sum_in,
        out_ref,
        kv_ref,
        near_ref,
        pos_ref,
        bias_ref,
    ) = refs[8:]
    dim = wqkv_ref.shape[0]
    atoms = own_ref.shape[1]
    groups, rows, width = qexp_ref.shape
    per = rows // atoms
    count = piece_refs[0].shape[0] - 8
    got = absorb(head_dim, (7,), piece_refs[7:], wqkv_ref, qexp_ref, str_ref, own_ref, kv_ref)
    for k in range(8):
        pos_ref[k] = piece_positions(piece_refs[k], count)
    me = lax.axis_index("rows") * col_count + lax.axis_index("cols")
    entries = list_ref.shape[1]
    listed = entries * atoms
    lane = lax.broadcasted_iota(jnp.int32, (1, listed), 1) // atoms
    in_tile = lax.broadcasted_iota(jnp.int32, (1, count), 1) // atoms
    a_tile = count // atoms
    tiles = []
    for e in range(entries):
        up, across, turn = locate(list_ref[0, e] ^ me)
        place = across + 4 * turn
        start = pl.multiple_of((place * a_tile + up) * atoms, atoms)
        near_ref[e * atoms : (e + 1) * atoms, :] = kv_ref[pl.ds(start, atoms), :]
        into = e % a_tile
        moved = pltpu.roll(pos_ref[place], (into - up + a_tile) % a_tile * atoms, 1)
        if into == 0:
            tiles.append(moved)
        else:
            tiles[-1] = jnp.where(in_tile == into, moved, tiles[-1])
    near = jnp.concatenate(tiles, axis=1)
    square = None
    for c in range(3):
        at = near[c : c + 1] + chosen([shift_ref[c, 0, e] for e in range(entries)], lane).astype(jnp.float32)
        gap = (at - own_ref[0, :, c : c + 1]) * cell_ref[c]
        square = gap * gap if square is None else square + gap * gap
    dist = jnp.sqrt(square + 0.25)
    nrbf = (w1_ref.shape[1] - 16) // 6
    centers = lax.broadcasted_iota(jnp.int32, (nrbf, 1), 0).astype(jnp.float32) * rbf_step
    step = 16
    ones = jnp.ones((16, step * listed), jnp.bfloat16)
    for i in range(0, atoms, step):
        gap = jnp.concatenate([dist[j : j + 1] - centers for j in range(i, i + step)], axis=1)
        radial = jnp.exp(gap * gap * (-0.5 / rbf_width**2))
        h, m, l = parts_of(radial, 3)
        stack = jnp.concatenate([h, m, h, l, h, m, ones], axis=0)
        u = mm(w1_ref[...], stack, ((1,), (0,)))
        u = u + u * jnp.tanh(u)
        h, l = parts_of(u, 2)
        pair = mm(w2_ref[...], jnp.concatenate([h, l, h], axis=0), ((1,), (0,)))
        for j in range(step):
            for g in range(groups):
                bias_ref[g, i + j] = pair[g * per : (g + 1) * per, j * listed : (j + 1) * listed]
    lane3 = lax.broadcasted_iota(jnp.int32, (1, 1, listed), 2) // atoms
    live = chosen([valid_ref[0, e] for e in range(entries)], lane3) > 0
    block = lax.broadcasted_iota(jnp.int32, (1, per, width), 2) // head_dim
    keep = block == lax.broadcasted_iota(jnp.int32, (1, per, width), 1)
    pieces = []
    for g in range(groups):
        low, high = g * width, (g + 1) * width
        _, summed, far = merge(got, g, acc_in, top_in, sum_in)
        far = far / repeat_lanes(summed, width)
        far = jnp.sum(jnp.where(keep, far, 0.0), axis=1).astype(jnp.bfloat16)
        s = mm(qexp_ref[g], near_ref[:, low:high], ((1,), (1,)))
        s = s.reshape(atoms, per, listed) * head_dim ** (-0.5) + bias_ref[g]
        s = jnp.where(live, s, -1e30)
        p = jnp.exp(s - jnp.max(s, axis=-1, keepdims=True))
        summed = jnp.sum(p, axis=-1, keepdims=True)
        o = mm(
            p.astype(jnp.bfloat16).reshape(rows, listed),
            near_ref[:, dim + low : dim + high],
            ((1,), (0,)),
        )
        o = o.reshape(atoms, per, width) / summed
        close = jnp.sum(jnp.where(keep, o, 0.0), axis=1).astype(jnp.bfloat16)
        pieces.append((close.astype(jnp.float32) + far.astype(jnp.float32)).astype(jnp.bfloat16))
    combined = jnp.concatenate(pieces, axis=1)
    moved = mm(combined, wout_ref[...], ((1,), (0,)))
    out_ref[...] = (in_ref[...].astype(jnp.float32) + moved).astype(jnp.bfloat16)


def call(kernel, outs, scratch, smem, args, aliases=None, hbm=0):
    vmem = pl.BlockSpec(memory_space=pltpu.VMEM)
    first = smem + hbm
    specs = [pl.BlockSpec(memory_space=pltpu.SMEM)] * smem
    specs += [pl.BlockSpec(memory_space=pltpu.HBM)] * hbm + [vmem] * (len(args) - first)
    placed = [pltpu.with_memory_space_constraint(a, pltpu.HBM) for a in args[smem:first]]
    placed += [pltpu.with_memory_space_constraint(a, pltpu.VMEM) for a in args[first:]]
    many = isinstance(outs, list)
    return pl.pallas_call(
        kernel,
        out_shape=outs,
        in_specs=specs,
        out_specs=[vmem] * len(outs) if many else vmem,
        scratch_shapes=scratch,
        input_output_aliases=aliases or {},
        compiler_params=pltpu.CompilerParams(vmem_limit_bytes=24 << 20),
    )(*args[:smem], *placed)


def on_device_small(
    features,
    positions,
    cell_lengths,
    block_lists,
    image_offsets,
    block_valid,
    norm_gain,
    w_qkv,
    w_out,
    rbf_weight,
    rbf_offset,
    pair_weight,
    cosine_scale,
):
    atoms, dim = features.shape
    heads = pair_weight.shape[1]
    hidden = pair_weight.shape[0]
    nrbf = rbf_weight.shape[0]
    head_dim = dim // heads
    row_count = lax.axis_size("rows")
    col_count = lax.axis_size("cols")
    total = row_count * col_count
    axes = ("rows", "cols")
    col_bits = col_count.bit_length() - 1
    flip = 1 << col_bits
    across_bits = (0, col_bits + 1)
    entries = block_lists.shape[1]
    width = 256
    per = width // head_dim
    groups = heads // per
    rows = atoms * per
    f32, bf16 = jnp.float32, jnp.bfloat16
    vm = pltpu.VMEM

    def swap(array, mask):
        return lax.ppermute(array, axes, [(i, i ^ mask) for i in range(total)])

    def locate(rel):
        up = (rel >> 1) & 3
        across = (rel & 1) + 2 * ((rel >> across_bits[1]) & 1)
        turn = (rel >> col_bits) & 1
        turn = turn ^ jnp.minimum(up, 1) ^ jnp.minimum(across, 1)
        return up, across, turn

    tied = lax.optimization_barrier
    pack = call(
        pack_kernel,
        vm((atoms, dim + 128), bf16),
        [
            vm((atoms, dim), bf16),
            vm((1, dim), f32),
            vm(positions.shape, f32),
            vm((128, atoms), f32),
            pltpu.SemaphoreType.DMA((3,)),
        ],
        0,
        (features, norm_gain[None], positions),
        hbm=3,
    )
    ups = [swap(pack, (d << 1) | flip) for d in (1, 2, 3)]
    ready = call(
        functools.partial(query_kernel, head_dim),
        [
            vm((groups, rows, width), bf16),
            vm((hidden, 6 * nrbf + 16), bf16),
            vm((heads, 3 * hidden), bf16),
            vm((heads, 128), f32),
            vm((3, atoms, 128), f32),
        ],
        [
            vm((dim, dim), bf16),
            vm((nrbf, hidden), f32),
            vm((1, hidden), f32),
            vm((heads, hidden), f32),
            vm((1, heads), f32),
            pltpu.SemaphoreType.DMA((5,)),
        ],
        0,
        (w_qkv, rbf_weight, rbf_offset[None], pair_weight.T, cosine_scale[None], pack),
        hbm=5,
    )
    ups, ready = tied((ups, ready))
    qexp, w1, w2, strength, own = ready
    count = 4 * atoms
    base = call(repack_kernel, vm((count + 8, dim), bf16), [], 0, (pack, *ups))
    east = swap(base, 1 | flip)
    north = swap(base, (1 << across_bits[1]) | flip)
    diag = swap(base, 1 | (1 << across_bits[1]) | flip)
    state_shapes = [
        vm((8 * count, 2 * dim), bf16),
        vm((groups, atoms, per, width), f32),
        vm((groups, atoms, per, 128), f32),
        vm((groups, atoms, per, 128), f32),
    ]
    common = (w_qkv, qexp, strength, own)

    def step(places, pieces, state):
        if state is None:
            return call(
                functools.partial(first_kernel, head_dim, places),
                state_shapes,
                [],
                0,
                (*pieces, *common),
            )
        at = len(pieces) + len(common)
        return call(
            functools.partial(next_kernel, head_dim, places),
            state_shapes,
            [],
            0,
            (*pieces, *common, *state),
            {at + k: k for k in range(4)},
        )

    state = step((0,), (base,), None)
    base_late, state = tied((base, state))
    base2 = swap(base_late, flip)
    base2, state = tied((base2, state))
    state = step((4,), (base2,), state)
    east, north, state = tied((east, north, state))
    east2, north2 = swap(east, flip), swap(north, flip)
    state = step((1, 2), (east, north), state)
    diag, state = tied((diag, state))
    diag2 = swap(diag, flip)
    state = step((3, 5, 6), (diag, east2, north2), state)
    diag2, state = tied((diag2, state))
    updated, _ = call(
        functools.partial(last_kernel, head_dim, locate, col_count),
        [jax.ShapeDtypeStruct((atoms, dim), bf16), state_shapes[0]],
        [
            vm((entries * atoms, 2 * dim), bf16),
            vm((8, 8, count), f32),
            vm((groups, atoms, per, entries * atoms), f32),
        ],
        4,
        (
            block_lists,
            block_valid,
            image_offsets,
            cell_lengths,
            base,
            east,
            north,
            diag,
            base2,
            east2,
            north2,
            diag2,
            *common,
            w1,
            w2,
            w_out,
            features,
            *state,
        ),
        {4 + 8 + len(common) + 4: 1},
    )
    return updated


def solution(mesh):
    row_count, col_count = mesh.shape["rows"], mesh.shape["cols"]
    small = (row_count, col_count) == (4, 8)
    body = on_device_small if small else on_device
    return jax.shard_map(
        body,
        mesh=mesh,
        in_specs=(
            P(("rows", "cols"), None),
            P(None, ("rows", "cols")),
            P(),
            P(("rows", "cols"), None),
            P(None, ("rows", "cols"), None),
            P(("rows", "cols"), None),
            P(),
            P(),
            P(),
            P(),
            P(),
            P(),
            P(),
        ),
        out_specs=P(("rows", "cols"), None),
        check_vma=False,
    )
```

```python
import functools
import math

import jax
import jax.numpy as jnp
from jax import lax
from jax.experimental import pallas as pl
from jax.experimental.pallas import tpu as pltpu
from jax.sharding import PartitionSpec as P


rbf_step = 2.0
rbf_width = 2.0
two_pi = 2.0 * math.pi
highest = lax.Precision.HIGHEST


def with_halo(cells, sides, width):
    for axis, dim in sides:
        count = lax.axis_size(axis)
        head = lax.slice_in_dim(cells, 0, width, axis=dim)
        tail = lax.slice_in_dim(cells, cells.shape[dim] - width, cells.shape[dim], axis=dim)
        cells = jnp.concatenate(
            [
                lax.ppermute(tail, axis, [(i, (i + 1) % count) for i in range(count)]),
                cells,
                lax.ppermute(head, axis, [((i + 1) % count, i) for i in range(count)]),
            ],
            axis=dim,
        )
    return cells


def rms_rows(values, norm_gain):
    floats = values.astype(jnp.float32)
    spread = jnp.mean(floats * floats, axis=-1, keepdims=True)
    return (floats * lax.rsqrt(spread + 1e-06) * norm_gain).astype(jnp.bfloat16)


def near_attention(
    query_rows,
    own_pos,
    keys,
    key_pos,
    shifts,
    live,
    cell_lengths,
    rbf_weight,
    rbf_offset,
    pair_weight,
):
    entries, block_len = (keys.shape[0], keys.shape[1])
    model_dim = query_rows.shape[1]
    head_count = pair_weight.shape[1]
    head_dim = model_dim // head_count
    key_coords = key_pos.transpose(1, 0, 2) + shifts.astype(jnp.float32)[:, :, None]
    key_coords = key_coords.reshape(3, entries * block_len)
    displace = (key_coords[:, None, :] - own_pos[:, :, None]) * cell_lengths[:, None, None]
    distance = jnp.sqrt(jnp.sum(displace * displace, axis=0) + 0.25)
    centers = jnp.arange(rbf_weight.shape[0], dtype=jnp.float32) * rbf_step
    radial = jnp.exp(-((distance[None] - centers[:, None, None]) ** 2) * (0.5 / rbf_width**2))
    radial = radial.reshape(rbf_weight.shape[0], -1)
    hidden = jax.nn.silu(jnp.dot(rbf_weight.T, radial, precision=highest) + rbf_offset[:, None])
    pair_bias = jnp.dot(pair_weight.T, hidden, precision=highest).reshape(
        head_count, query_rows.shape[0], entries * block_len
    )
    query_heads = query_rows.reshape(-1, head_count, head_dim)
    key_heads = keys[:, :, :model_dim].reshape(entries * block_len, head_count, head_dim)
    value_heads = keys[:, :, model_dim:].reshape(entries * block_len, head_count, head_dim)
    scores = (
        jnp.einsum("ahd,khd->hak", query_heads, key_heads, preferred_element_type=jnp.float32)
        * head_dim ** (-0.5)
        + pair_bias
    )
    allowed = jnp.repeat(live > 0, block_len)
    scores = jnp.where(allowed[None, None, :], scores, -1e30)
    row_max = jnp.max(scores, axis=-1, keepdims=True)
    weights = jnp.exp(scores - row_max)
    row_sum = jnp.sum(weights, axis=-1, keepdims=True)
    prob_bf = weights.astype(jnp.bfloat16)
    attended = jnp.einsum(
        "hak,khd->ahd", prob_bf, value_heads, preferred_element_type=jnp.float32
    ) / row_sum.transpose(1, 0, 2)
    return attended.reshape(-1, model_dim).astype(jnp.bfloat16)


def on_device(
    features,
    positions,
    cell_lengths,
    block_lists,
    image_offsets,
    block_valid,
    norm_gain,
    w_qkv,
    w_out,
    rbf_weight,
    rbf_offset,
    pair_weight,
    cosine_scale,
):
    atom_count, model_dim = features.shape
    head_count = pair_weight.shape[1]
    head_dim = model_dim // head_count
    row_count = lax.axis_size("rows")
    col_count = lax.axis_size("cols")
    row_index = lax.axis_index("rows")
    col_index = lax.axis_index("cols")
    per_dev = head_count // row_count
    normed = rms_rows(features, norm_gain)
    packed = jnp.dot(normed, w_qkv, preferred_element_type=jnp.float32).astype(jnp.bfloat16)
    every_pos = lax.all_gather(positions, ("rows", "cols"), axis=1, tiled=True)
    near_rows = with_halo(normed[None, None], (("rows", 0), ("cols", 1)), 1)
    near_kv = jnp.dot(
        near_rows.reshape(9 * atom_count, model_dim),
        w_qkv[:, model_dim:],
        preferred_element_type=jnp.float32,
    )
    near_kv = near_kv.astype(jnp.bfloat16).reshape(9, atom_count, 2 * model_dim)
    listed = block_lists[0]
    list_row = listed // col_count
    list_col = listed % col_count
    slots = (list_row - row_index + 1) % row_count * 3 + (list_col - col_index + 1) % col_count
    keys = jnp.take(near_kv, slots, axis=0)
    block_pos = every_pos.reshape(3, row_count * col_count, atom_count)
    key_pos = jnp.take(block_pos, listed, axis=1).transpose(1, 0, 2)
    local_out = near_attention(
        packed[:, :model_dim],
        positions,
        keys,
        key_pos,
        image_offsets[:, 0, :],
        block_valid[0],
        cell_lengths,
        rbf_weight,
        rbf_offset,
        pair_weight,
    )
    grouped = (
        packed.reshape(atom_count, 3, head_count, head_dim)
        .transpose(1, 2, 0, 3)
        .reshape(3, head_count, atom_count * head_dim)
    )
    regrouped = lax.all_to_all(grouped, "rows", split_axis=1, concat_axis=2, tiled=True)
    query_count = row_count * atom_count
    queries = regrouped[0].reshape(per_dev, query_count, head_dim)
    key_vals = regrouped[1:]
    cycle_pos = (
        every_pos.reshape(3, row_count, col_count, atom_count).transpose(0, 2, 1, 3).reshape(3, -1)
    )
    query_pos = lax.dynamic_slice_in_dim(cycle_pos, col_index * query_count, query_count, 1)
    cycle_feats = jnp.concatenate(
        [jnp.cos(two_pi * cycle_pos), jnp.sin(two_pi * cycle_pos)], axis=0
    )
    query_feats = jnp.concatenate(
        [jnp.cos(two_pi * query_pos), jnp.sin(two_pi * query_pos)], axis=0
    )
    strengths = lax.dynamic_slice_in_dim(cosine_scale, row_index * per_dev, per_dev)
    scale = head_dim ** (-0.5)

    def update(state, kv_block, key_start, block_len):
        run_max, run_sum, accum = state
        scores = (
            jnp.einsum("hqd,hkd->hqk", queries, kv_block[0], preferred_element_type=jnp.float32)
            * scale
        )
        coords = lax.dynamic_slice_in_dim(cycle_feats, key_start, block_len, 1)
        cos_bias = jnp.dot(query_feats.T, coords, precision=highest)
        scores = scores + strengths[:, None, None] * cos_bias[None]
        new_max = jnp.maximum(run_max, jnp.max(scores, axis=-1))
        keep_part = jnp.exp(run_max - new_max)
        weights = jnp.exp(scores - new_max[:, :, None])
        run_sum = run_sum * keep_part + jnp.sum(weights, axis=-1)
        prob_bf = weights.astype(jnp.bfloat16)
        accum = accum * keep_part[:, None, :] + jnp.einsum(
            "hqk,hkd->hdq", prob_bf, kv_block[1], preferred_element_type=jnp.float32
        )
        return (new_max, run_sum, accum)

    initial = (
        jnp.full((per_dev, query_count), -1e30, jnp.float32),
        jnp.zeros((per_dev, query_count), jnp.float32),
        jnp.zeros((per_dev, head_dim, query_count), jnp.float32),
    )
    piece = lax.all_gather(key_vals, "cols", axis=2, tiled=True)
    key_total = piece.shape[2] // head_dim
    if key_total > 1024 and key_total % 1024 == 0:
        block_len = 1024
    else:
        block_len = key_total
    block_count = key_total // block_len
    kv_blocks = piece.reshape(2, per_dev, block_count, block_len, head_dim).transpose(2, 0, 1, 3, 4)
    block_starts = jnp.arange(block_count, dtype=jnp.int32) * block_len

    def one_block(state, block_in):
        kv_block, key_start = block_in
        return (update(state, kv_block, key_start, block_len), None)

    state, _ = lax.scan(one_block, initial, (kv_blocks, block_starts))
    _, run_sum, accum = state
    head_out = (
        (accum / run_sum[:, None, :])
        .transpose(0, 2, 1)
        .astype(jnp.bfloat16)
        .reshape(per_dev, query_count * head_dim)
    )
    returned = lax.all_to_all(head_out, "rows", split_axis=1, concat_axis=0, tiled=True)
    global_out = (
        returned.reshape(head_count, atom_count, head_dim)
        .transpose(1, 0, 2)
        .reshape(atom_count, model_dim)
    )
    combined = (local_out.astype(jnp.float32) + global_out.astype(jnp.float32)).astype(jnp.bfloat16)
    updated = features.astype(jnp.float32) + jnp.dot(
        combined, w_out, preferred_element_type=jnp.float32
    )
    return updated.astype(jnp.bfloat16)


def mm(a, b, dims):
    return lax.dot_general(a, b, (dims, ((), ())), preferred_element_type=jnp.float32)


def parts_of(value, count):
    out = []
    for _ in range(count):
        part = value.astype(jnp.bfloat16)
        out.append(part)
        value = value - part.astype(jnp.float32)
    return out


def unit(rows, cols, dtype):
    r = lax.broadcasted_iota(jnp.int32, (rows, cols), 0)
    c = lax.broadcasted_iota(jnp.int32, (rows, cols), 1)
    return (r == c).astype(dtype)


def to_column(row):
    count = row.shape[1]
    r = lax.broadcasted_iota(jnp.int32, (count, count), 0)
    c = lax.broadcasted_iota(jnp.int32, (count, count), 1)
    return jnp.sum(jnp.where(r == c, jnp.broadcast_to(row, (count, count)), 0.0), axis=1, keepdims=True)


def fetch(pairs, sems):
    copies = [pltpu.make_async_copy(src, dst, sems.at[k]) for k, (src, dst) in enumerate(pairs)]
    for copy in copies:
        copy.start()
    return copies


def settle(copies):
    for copy in copies:
        copy.wait()


def pack_kernel(feat_hbm, gain_hbm, pos_hbm, out_ref, feat_ref, gain_ref, pos_ref, tmp_ref, sems):
    settle(fetch(((feat_hbm, feat_ref), (gain_hbm, gain_ref), (pos_hbm, pos_ref)), sems))
    atoms, dim = feat_ref.shape
    floats = feat_ref[...].astype(jnp.float32)
    spread = jnp.mean(floats * floats, axis=-1, keepdims=True)
    normed = floats * lax.rsqrt(spread + 1e-06) * gain_ref[...]
    out_ref[:, :dim] = normed.astype(jnp.bfloat16)
    tmp_ref[...] = jnp.zeros(tmp_ref.shape, jnp.float32)
    for p, part in enumerate(parts_of(pos_ref[...], 3)):
        tmp_ref[8 * p : 8 * p + 3, :] = part.astype(jnp.float32)
    eye = unit(atoms, atoms, jnp.bfloat16)
    turned = mm(eye, tmp_ref[...].astype(jnp.bfloat16), ((1,), (1,)))
    out_ref[:, dim:] = turned.astype(jnp.bfloat16)


def query_kernel(
    head_dim,
    wqkv_hbm,
    rw_hbm,
    ro_hbm,
    pw_hbm,
    cs_hbm,
    pack_ref,
    qexp_ref,
    w1_ref,
    w2_ref,
    str_ref,
    own_ref,
    wq_ref,
    rw_ref,
    ro_ref,
    pw_ref,
    cs_ref,
    sems,
):
    atoms = pack_ref.shape[0]
    dim = wq_ref.shape[0]
    copies = fetch(
        (
            (wqkv_hbm.at[:, pl.ds(0, dim)], wq_ref),
            (rw_hbm, rw_ref),
            (ro_hbm, ro_ref),
            (pw_hbm, pw_ref),
            (cs_hbm, cs_ref),
        ),
        sems,
    )
    groups, rows, width = qexp_ref.shape
    per = rows // atoms
    pos = pack_ref[:, dim:].astype(jnp.float32)
    pos = pos + pltpu.roll(pos, 120, 1) + pltpu.roll(pos, 112, 1)
    own_ref[0] = pos
    own_ref[1] = jnp.cos(two_pi * pos)
    own_ref[2] = jnp.sin(two_pi * pos)
    settle(copies[1:])
    h, m, l = parts_of(0.5 * rw_ref[...], 3)
    hidden = rw_ref.shape[1]
    row = lax.broadcasted_iota(jnp.int32, (16, hidden), 0)
    tail = jnp.zeros((16, hidden), jnp.float32)
    for k, part in enumerate(parts_of(0.5 * ro_ref[...], 3)):
        tail = jnp.where(row == k, part.astype(jnp.float32), tail)
    stack = jnp.concatenate([h, h, m, h, l, m, tail.astype(jnp.bfloat16)], axis=0)
    w1_ref[...] = mm(unit(hidden, hidden, jnp.bfloat16), stack, ((1,), (1,))).astype(jnp.bfloat16)
    h, l = parts_of(pw_ref[...], 2)
    w2_ref[...] = jnp.concatenate([h, h, l], axis=1)
    str_ref[...] = jnp.broadcast_to(to_column(cs_ref[...]), str_ref.shape)
    settle(copies[:1])
    q = mm(pack_ref[:, :dim], wq_ref[...], ((1,), (0,)))
    q = q.astype(jnp.bfloat16).astype(jnp.float32)
    lane = lax.broadcasted_iota(jnp.int32, (per, width), 1) // head_dim
    sub = lax.broadcasted_iota(jnp.int32, (per, width), 0)
    keep = (lane == sub)[None]
    for g in range(groups):
        part = q[:, g * width : (g + 1) * width]
        spread = jnp.broadcast_to(part[:, None, :], (atoms, per, width))
        spread = jnp.where(keep, spread, 0.0).reshape(rows, width)
        qexp_ref[g] = spread.astype(jnp.bfloat16)


def position_tile(blocks, dim):
    pos = jnp.concatenate([block[:, dim:] for block in blocks], axis=0)
    r = lax.broadcasted_iota(jnp.int32, (8, 128), 0)
    c = lax.broadcasted_iota(jnp.int32, (8, 128), 1)
    out = []
    for p in range(3):
        pick = ((c == 8 * p + r) & (r < 3)).astype(jnp.bfloat16)
        part = mm(pick, pos, ((1,), (1,)))
        if part.shape[1] < 128:
            part = jnp.concatenate([part, jnp.zeros((8, 128 - part.shape[1]), jnp.float32)], axis=1)
        out.append(part)
    out.append(jnp.zeros((8, dim - 3 * 128), jnp.float32))
    return jnp.concatenate(out, axis=1).astype(jnp.bfloat16)


def repack_kernel(*refs):
    blocks, out_ref = refs[:-1], refs[-1]
    atoms = blocks[0].shape[0]
    dim = out_ref.shape[1]
    for k, block in enumerate(blocks):
        out_ref[k * atoms : (k + 1) * atoms, :] = block[:, :dim]
    out_ref[len(blocks) * atoms :, :] = position_tile(blocks, dim)


def piece_tiles(piece, counts):
    total = sum(counts)
    out = []
    for k in range(len(counts)):
        tail = piece[total + 8 * k : total + 8 * (k + 1), :].astype(jnp.float32)
        out.append(tail[:, :128] + tail[:, 128:256] + tail[:, 256:384])
    return out


def attend(qexp, keys, vals, scale, bias3):
    rows = qexp.shape[0]
    count = keys.shape[0]
    atoms, per, _ = bias3.shape
    s = mm(qexp, keys, ((1,), (1,))).reshape(atoms, per, count) * scale + bias3
    top = jnp.max(s, axis=-1, keepdims=True)
    p = jnp.exp(s - top)
    total = jnp.sum(p, axis=-1, keepdims=True)
    o = mm(p.astype(jnp.bfloat16).reshape(rows, count), vals, ((1,), (0,)))
    return top, total, o.reshape(atoms, per, vals.shape[1])


def absorb(head_dim, plan, pieces, wqkv_ref, qexp_ref, str_ref, own_ref, kv_ref):
    dim = wqkv_ref.shape[0]
    atoms = own_ref.shape[1]
    groups, rows, width = qexp_ref.shape
    per = rows // atoms
    rows_in = jnp.concatenate(
        [piece[: sum(counts), :] for piece, (_, counts) in zip(pieces, plan)], axis=0
    )
    kv = mm(rows_in, wqkv_ref[:, dim:], ((1,), (0,))).astype(jnp.bfloat16)
    at = 0
    tiles = []
    for piece, (start, counts) in zip(pieces, plan):
        kv_ref[start : start + sum(counts), :] = kv[at : at + sum(counts)]
        at += sum(counts)
        tiles += [t[:, :n] for t, n in zip(piece_tiles(piece, counts), counts)]
    pos8 = jnp.concatenate(tiles, axis=1)
    cos_k, sin_k = jnp.cos(two_pi * pos8), jnp.sin(two_pi * pos8)
    waves = None
    for c in range(3):
        term = own_ref[1, :, c : c + 1] * cos_k[c : c + 1] + own_ref[2, :, c : c + 1] * sin_k[c : c + 1]
        waves = term if waves is None else waves + term
    out = []
    for g in range(groups):
        low, high = g * width, (g + 1) * width
        bias3 = str_ref[g * per : (g + 1) * per, :1][None] * waves[:, None, :]
        out.append(
            attend(
                qexp_ref[g],
                kv[:, low:high],
                kv[:, dim + low : dim + high],
                head_dim ** (-0.5),
                bias3,
            )
        )
    return out


def widen(column, lanes):
    return jnp.broadcast_to(column, column.shape[:-1] + (lanes,))


def repeat_lanes(array, lanes):
    return jnp.concatenate([array] * (lanes // array.shape[-1]), axis=-1)


def first_kernel(head_dim, plan, own_ref0, *refs):
    blocks = (own_ref0,) + refs[:3]
    ring_ref, wqkv_ref, qexp_ref, str_ref, own_ref = refs[3:8]
    core_ref, kv_ref, acc_ref, top_ref, sum_ref = refs[8:]
    atoms = own_ref.shape[1]
    dim = wqkv_ref.shape[0]
    four, three = plan[0][1]
    for k, block in enumerate(blocks):
        core_ref[k * atoms : (k + 1) * atoms, :] = block[:, :dim]
    core_ref[four : four + three, :] = ring_ref[:three, :]
    core_ref[four + three : four + three + 8, :] = position_tile(blocks, dim)
    core_ref[four + three + 8 :, :] = ring_ref[three:, :]
    got = absorb(head_dim, plan, (core_ref,), wqkv_ref, qexp_ref, str_ref, own_ref, kv_ref)
    for g, (top, total, o) in enumerate(got):
        acc_ref[g] = o
        top_ref[g] = widen(top, 128)
        sum_ref[g] = widen(total, 128)


def merge(got, g, acc_ref, top_ref, sum_ref):
    top, total, o = got[g]
    width = o.shape[-1]
    best = jnp.maximum(widen(top, 128), top_ref[g])
    a, b = jnp.exp(top_ref[g] - best), jnp.exp(widen(top, 128) - best)
    summed = a * sum_ref[g] + b * widen(total, 128)
    acc = repeat_lanes(a, width) * acc_ref[g] + repeat_lanes(b, width) * o
    return best, summed, acc


def next_kernel(head_dim, plan, *refs):
    pieces = refs[: len(plan)]
    wqkv_ref, qexp_ref, str_ref, own_ref = refs[len(plan) : len(plan) + 4]
    _, acc_in, top_in, sum_in, kv_ref, acc_ref, top_ref, sum_ref = refs[len(plan) + 4 :]
    got = absorb(head_dim, plan, pieces, wqkv_ref, qexp_ref, str_ref, own_ref, kv_ref)
    for g in range(len(got)):
        best, summed, acc = merge(got, g, acc_in, top_in, sum_in)
        acc_ref[g] = acc
        top_ref[g] = best
        sum_ref[g] = summed


def chosen(scalars, lane):
    out = jnp.full(lane.shape, scalars[0])
    for e in range(1, len(scalars)):
        out = jnp.where(lane == e, scalars[e], out)
    return out


def last_kernel(head_dim, locate, plan, col_count, list_ref, valid_ref, shift_ref, cell_ref, *refs):
    piece_refs = refs[:8]
    (
        wqkv_ref,
        qexp_ref,
        str_ref,
        own_ref,
        w1_ref,
        w2_ref,
        wout_ref,
        in_ref,
        _,
        acc_in,
        top_in,
        sum_in,
        out_ref,
        kv_ref,
        near_ref,
        pos_ref,
        bias_ref,
    ) = refs[8:]
    dim = wqkv_ref.shape[0]
    atoms = own_ref.shape[1]
    groups, rows, width = qexp_ref.shape
    per = rows // atoms
    got = absorb(head_dim, plan[7:], piece_refs[7:], wqkv_ref, qexp_ref, str_ref, own_ref, kv_ref)
    at = 0
    for piece, (_, counts) in zip(piece_refs, plan):
        for tile in piece_tiles(piece, counts):
            pos_ref[at] = tile
            at += 1
    me = lax.axis_index("rows") * col_count + lax.axis_index("cols")
    entries = list_ref.shape[1]
    listed = entries * atoms
    lane = lax.broadcasted_iota(jnp.int32, (1, listed), 1) // atoms
    a_tile = 128 // atoms
    in_tile = lax.broadcasted_iota(jnp.int32, (1, 128), 1) // atoms
    tiles = []
    for e in range(entries):
        slot, tile, spot = locate(list_ref[0, e] ^ me)
        start = pl.multiple_of(slot * atoms, atoms)
        near_ref[e * atoms : (e + 1) * atoms, :] = kv_ref[pl.ds(start, atoms), :]
        into = e % a_tile
        moved = pltpu.roll(pos_ref[tile], (into - spot + a_tile) % a_tile * atoms, 1)
        if into == 0:
            tiles.append(moved)
        else:
            tiles[-1] = jnp.where(in_tile == into, moved, tiles[-1])
    near = jnp.concatenate(tiles, axis=1)
    square = None
    for c in range(3):
        at = near[c : c + 1] + chosen([shift_ref[c, 0, e] for e in range(entries)], lane).astype(jnp.float32)
        gap = (at - own_ref[0, :, c : c + 1]) * cell_ref[c]
        square = gap * gap if square is None else square + gap * gap
    dist = jnp.sqrt(square + 0.25)
    nrbf = (w1_ref.shape[1] - 16) // 6
    centers = lax.broadcasted_iota(jnp.int32, (nrbf, 1), 0).astype(jnp.float32) * rbf_step
    step = 16
    ones = jnp.ones((16, step * listed), jnp.bfloat16)
    for i in range(0, atoms, step):
        gap = jnp.concatenate([dist[j : j + 1] - centers for j in range(i, i + step)], axis=1)
        radial = jnp.exp(gap * gap * (-0.5 / rbf_width**2))
        h, m, l = parts_of(radial, 3)
        stack = jnp.concatenate([h, m, h, l, h, m, ones], axis=0)
        u = mm(w1_ref[...], stack, ((1,), (0,)))
        u = u + u * jnp.tanh(u)
        h, l = parts_of(u, 2)
        pair = mm(w2_ref[...], jnp.concatenate([h, l, h], axis=0), ((1,), (0,)))
        for j in range(step):
            for g in range(groups):
                bias_ref[g, i + j] = pair[g * per : (g + 1) * per, j * listed : (j + 1) * listed]
    lane3 = lax.broadcasted_iota(jnp.int32, (1, 1, listed), 2) // atoms
    live = chosen([valid_ref[0, e] for e in range(entries)], lane3) > 0
    block = lax.broadcasted_iota(jnp.int32, (1, per, width), 2) // head_dim
    keep = block == lax.broadcasted_iota(jnp.int32, (1, per, width), 1)
    pieces = []
    for g in range(groups):
        low, high = g * width, (g + 1) * width
        _, summed, far = merge(got, g, acc_in, top_in, sum_in)
        far = far / repeat_lanes(summed, width)
        far = jnp.sum(jnp.where(keep, far, 0.0), axis=1).astype(jnp.bfloat16)
        s = mm(qexp_ref[g], near_ref[:, low:high], ((1,), (1,)))
        s = s.reshape(atoms, per, listed) * head_dim ** (-0.5) + bias_ref[g]
        s = jnp.where(live, s, -1e30)
        p = jnp.exp(s - jnp.max(s, axis=-1, keepdims=True))
        summed = jnp.sum(p, axis=-1, keepdims=True)
        o = mm(
            p.astype(jnp.bfloat16).reshape(rows, listed),
            near_ref[:, dim + low : dim + high],
            ((1,), (0,)),
        )
        o = o.reshape(atoms, per, width) / summed
        close = jnp.sum(jnp.where(keep, o, 0.0), axis=1).astype(jnp.bfloat16)
        pieces.append((close.astype(jnp.float32) + far.astype(jnp.float32)).astype(jnp.bfloat16))
    combined = jnp.concatenate(pieces, axis=1)
    moved = mm(combined, wout_ref[...], ((1,), (0,)))
    out_ref[...] = (in_ref[...].astype(jnp.float32) + moved).astype(jnp.bfloat16)


def call(kernel, outs, scratch, smem, args, aliases=None, hbm=0):
    vmem = pl.BlockSpec(memory_space=pltpu.VMEM)
    first = smem + hbm
    specs = [pl.BlockSpec(memory_space=pltpu.SMEM)] * smem
    specs += [pl.BlockSpec(memory_space=pltpu.HBM)] * hbm + [vmem] * (len(args) - first)
    placed = [pltpu.with_memory_space_constraint(a, pltpu.HBM) for a in args[smem:first]]
    placed += [pltpu.with_memory_space_constraint(a, pltpu.VMEM) for a in args[first:]]
    many = isinstance(outs, list)
    return pl.pallas_call(
        kernel,
        out_shape=outs,
        in_specs=specs,
        out_specs=[vmem] * len(outs) if many else vmem,
        scratch_shapes=scratch,
        input_output_aliases=aliases or {},
        compiler_params=pltpu.CompilerParams(vmem_limit_bytes=24 << 20),
    )(*args[:smem], *placed)


def on_device_small(
    features,
    positions,
    cell_lengths,
    block_lists,
    image_offsets,
    block_valid,
    norm_gain,
    w_qkv,
    w_out,
    rbf_weight,
    rbf_offset,
    pair_weight,
    cosine_scale,
):
    atoms, dim = features.shape
    heads = pair_weight.shape[1]
    hidden = pair_weight.shape[0]
    nrbf = rbf_weight.shape[0]
    head_dim = dim // heads
    row_count = lax.axis_size("rows")
    col_count = lax.axis_size("cols")
    total = row_count * col_count
    axes = ("rows", "cols")
    col_bits = col_count.bit_length() - 1
    flip = 1 << col_bits
    across_bits = (0, col_bits + 1)
    entries = block_lists.shape[1]
    width = 256
    per = width // head_dim
    groups = heads // per
    rows = atoms * per
    f32, bf16 = jnp.float32, jnp.bfloat16
    vm = pltpu.VMEM

    def swap(array, mask):
        return lax.ppermute(array, axes, [(i, i ^ mask) for i in range(total)])

    def locate(rel):
        up = (rel >> 1) & 3
        across = (rel & 1) + 2 * ((rel >> across_bits[1]) & 1)
        turn = (rel >> col_bits) & 1
        turn = turn ^ jnp.minimum(up, 1) ^ jnp.minimum(across, 1)
        far = jnp.minimum(up, 1)
        slot = turn * 16 + across + far * (3 + 2 * across + up)
        tile = turn * 5 + far * (1 + across)
        spot = across + far * (up - 1 - across)
        return slot, tile, spot

    tied = lax.optimization_barrier
    pack = call(
        pack_kernel,
        vm((atoms, dim + 128), bf16),
        [
            vm((atoms, dim), bf16),
            vm((1, dim), f32),
            vm(positions.shape, f32),
            vm((128, atoms), f32),
            pltpu.SemaphoreType.DMA((3,)),
        ],
        0,
        (features, norm_gain[None], positions),
        hbm=3,
    )
    across_masks = {"e": 1 | flip, "n": (1 << across_bits[1]) | flip}
    across_masks["d"] = 1 | across_masks["n"]
    ups = [swap(pack, (d << 1) | flip) for d in (1, 2, 3)]
    owns = [swap(pack, mask) for mask in across_masks.values()]
    ready = call(
        functools.partial(query_kernel, head_dim),
        [
            vm((groups, rows, width), bf16),
            vm((hidden, 6 * nrbf + 16), bf16),
            vm((heads, 3 * hidden), bf16),
            vm((heads, 128), f32),
            vm((3, atoms, 128), f32),
        ],
        [
            vm((dim, dim), bf16),
            vm((nrbf, hidden), f32),
            vm((1, hidden), f32),
            vm((heads, hidden), f32),
            vm((1, heads), f32),
            pltpu.SemaphoreType.DMA((5,)),
        ],
        0,
        (w_qkv, rbf_weight, rbf_offset[None], pair_weight.T, cosine_scale[None], pack),
        hbm=5,
    )
    qexp, w1, w2, strength, own = ready
    four, three = 4 * atoms, 3 * atoms
    ring = call(repack_kernel, vm((three + 8, dim), bf16), [], 0, tuple(ups))
    east, north, diag = [swap(ring, mask) for mask in across_masks.values()]
    state_shapes = [
        vm((total * atoms, 2 * dim), bf16),
        vm((groups, atoms, per, width), f32),
        vm((groups, atoms, per, 128), f32),
        vm((groups, atoms, per, 128), f32),
    ]
    common = (w_qkv, qexp, strength, own)
    half = total // 2 * atoms
    plan = [(0, (four, three))] + [(four + k * three, (three,)) for k in (1, 2, 3)]
    plan += [(half + start, counts) for start, counts in plan]

    core, *state = call(
        functools.partial(first_kernel, head_dim, plan[:1]),
        [vm((four + three + 16, dim), bf16)] + state_shapes,
        [],
        0,
        (pack, *owns, ring, *common),
    )

    def step(places, pieces, state):
        at = len(pieces) + len(common)
        return call(
            functools.partial(next_kernel, head_dim, [plan[k] for k in places]),
            state_shapes,
            [],
            0,
            (*pieces, *common, *state),
            {at + k: k for k in range(4)},
        )

    core2 = swap(core, flip)
    east, north, state = tied((east, north, state))
    east2, north2 = swap(east, flip), swap(north, flip)
    state = step((1, 2, 4), (east, north, core2), state)
    diag, state = tied((diag, state))
    diag2 = swap(diag, flip)
    state = step((3, 5, 6), (diag, east2, north2), state)
    diag2, state = tied((diag2, state))
    updated, _ = call(
        functools.partial(last_kernel, head_dim, locate, plan, col_count),
        [jax.ShapeDtypeStruct((atoms, dim), bf16), state_shapes[0]],
        [
            vm((entries * atoms, 2 * dim), bf16),
            vm((10, 8, 128), f32),
            vm((groups, atoms, per, entries * atoms), f32),
        ],
        4,
        (
            block_lists,
            block_valid,
            image_offsets,
            cell_lengths,
            core,
            east,
            north,
            diag,
            core2,
            east2,
            north2,
            diag2,
            *common,
            w1,
            w2,
            w_out,
            features,
            *state,
        ),
        {4 + 8 + len(common) + 4: 1},
    )
    return updated


def solution(mesh):
    row_count, col_count = mesh.shape["rows"], mesh.shape["cols"]
    small = (row_count, col_count) == (4, 8)
    body = on_device_small if small else on_device
    return jax.shard_map(
        body,
        mesh=mesh,
        in_specs=(
            P(("rows", "cols"), None),
            P(None, ("rows", "cols")),
            P(),
            P(("rows", "cols"), None),
            P(None, ("rows", "cols"), None),
            P(("rows", "cols"), None),
            P(),
            P(),
            P(),
            P(),
            P(),
            P(),
            P(),
        ),
        out_specs=P(("rows", "cols"), None),
        check_vma=False,
    )
```

```python
import functools
import math

import jax
import jax.numpy as jnp
from jax import lax
from jax.experimental import pallas as pl
from jax.experimental.pallas import tpu as pltpu
from jax.sharding import PartitionSpec as P


rbf_step = 2.0
rbf_width = 2.0
two_pi = 2.0 * math.pi
highest = lax.Precision.HIGHEST


def with_halo(cells, sides, width):
    for axis, dim in sides:
        count = lax.axis_size(axis)
        head = lax.slice_in_dim(cells, 0, width, axis=dim)
        tail = lax.slice_in_dim(cells, cells.shape[dim] - width, cells.shape[dim], axis=dim)
        cells = jnp.concatenate(
            [
                lax.ppermute(tail, axis, [(i, (i + 1) % count) for i in range(count)]),
                cells,
                lax.ppermute(head, axis, [((i + 1) % count, i) for i in range(count)]),
            ],
            axis=dim,
        )
    return cells


def rms_rows(values, norm_gain):
    floats = values.astype(jnp.float32)
    spread = jnp.mean(floats * floats, axis=-1, keepdims=True)
    return (floats * lax.rsqrt(spread + 1e-06) * norm_gain).astype(jnp.bfloat16)


def near_attention(
    query_rows,
    own_pos,
    keys,
    key_pos,
    shifts,
    live,
    cell_lengths,
    rbf_weight,
    rbf_offset,
    pair_weight,
):
    entries, block_len = (keys.shape[0], keys.shape[1])
    model_dim = query_rows.shape[1]
    head_count = pair_weight.shape[1]
    head_dim = model_dim // head_count
    key_coords = key_pos.transpose(1, 0, 2) + shifts.astype(jnp.float32)[:, :, None]
    key_coords = key_coords.reshape(3, entries * block_len)
    displace = (key_coords[:, None, :] - own_pos[:, :, None]) * cell_lengths[:, None, None]
    distance = jnp.sqrt(jnp.sum(displace * displace, axis=0) + 0.25)
    centers = jnp.arange(rbf_weight.shape[0], dtype=jnp.float32) * rbf_step
    radial = jnp.exp(-((distance[None] - centers[:, None, None]) ** 2) * (0.5 / rbf_width**2))
    radial = radial.reshape(rbf_weight.shape[0], -1)
    hidden = jax.nn.silu(jnp.dot(rbf_weight.T, radial, precision=highest) + rbf_offset[:, None])
    pair_bias = jnp.dot(pair_weight.T, hidden, precision=highest).reshape(
        head_count, query_rows.shape[0], entries * block_len
    )
    query_heads = query_rows.reshape(-1, head_count, head_dim)
    key_heads = keys[:, :, :model_dim].reshape(entries * block_len, head_count, head_dim)
    value_heads = keys[:, :, model_dim:].reshape(entries * block_len, head_count, head_dim)
    scores = (
        jnp.einsum("ahd,khd->hak", query_heads, key_heads, preferred_element_type=jnp.float32)
        * head_dim ** (-0.5)
        + pair_bias
    )
    allowed = jnp.repeat(live > 0, block_len)
    scores = jnp.where(allowed[None, None, :], scores, -1e30)
    row_max = jnp.max(scores, axis=-1, keepdims=True)
    weights = jnp.exp(scores - row_max)
    row_sum = jnp.sum(weights, axis=-1, keepdims=True)
    prob_bf = weights.astype(jnp.bfloat16)
    attended = jnp.einsum(
        "hak,khd->ahd", prob_bf, value_heads, preferred_element_type=jnp.float32
    ) / row_sum.transpose(1, 0, 2)
    return attended.reshape(-1, model_dim).astype(jnp.bfloat16)


def on_device(
    features,
    positions,
    cell_lengths,
    block_lists,
    image_offsets,
    block_valid,
    norm_gain,
    w_qkv,
    w_out,
    rbf_weight,
    rbf_offset,
    pair_weight,
    cosine_scale,
):
    atom_count, model_dim = features.shape
    head_count = pair_weight.shape[1]
    head_dim = model_dim // head_count
    row_count = lax.axis_size("rows")
    col_count = lax.axis_size("cols")
    row_index = lax.axis_index("rows")
    col_index = lax.axis_index("cols")
    per_dev = head_count // row_count
    normed = rms_rows(features, norm_gain)
    packed = jnp.dot(normed, w_qkv, preferred_element_type=jnp.float32).astype(jnp.bfloat16)
    every_pos = lax.all_gather(positions, ("rows", "cols"), axis=1, tiled=True)
    near_rows = with_halo(normed[None, None], (("rows", 0), ("cols", 1)), 1)
    near_kv = jnp.dot(
        near_rows.reshape(9 * atom_count, model_dim),
        w_qkv[:, model_dim:],
        preferred_element_type=jnp.float32,
    )
    near_kv = near_kv.astype(jnp.bfloat16).reshape(9, atom_count, 2 * model_dim)
    listed = block_lists[0]
    list_row = listed // col_count
    list_col = listed % col_count
    slots = (list_row - row_index + 1) % row_count * 3 + (list_col - col_index + 1) % col_count
    keys = jnp.take(near_kv, slots, axis=0)
    block_pos = every_pos.reshape(3, row_count * col_count, atom_count)
    key_pos = jnp.take(block_pos, listed, axis=1).transpose(1, 0, 2)
    local_out = near_attention(
        packed[:, :model_dim],
        positions,
        keys,
        key_pos,
        image_offsets[:, 0, :],
        block_valid[0],
        cell_lengths,
        rbf_weight,
        rbf_offset,
        pair_weight,
    )
    grouped = (
        packed.reshape(atom_count, 3, head_count, head_dim)
        .transpose(1, 2, 0, 3)
        .reshape(3, head_count, atom_count * head_dim)
    )
    regrouped = lax.all_to_all(grouped, "rows", split_axis=1, concat_axis=2, tiled=True)
    query_count = row_count * atom_count
    queries = regrouped[0].reshape(per_dev, query_count, head_dim)
    key_vals = regrouped[1:]
    cycle_pos = (
        every_pos.reshape(3, row_count, col_count, atom_count).transpose(0, 2, 1, 3).reshape(3, -1)
    )
    query_pos = lax.dynamic_slice_in_dim(cycle_pos, col_index * query_count, query_count, 1)
    cycle_feats = jnp.concatenate(
        [jnp.cos(two_pi * cycle_pos), jnp.sin(two_pi * cycle_pos)], axis=0
    )
    query_feats = jnp.concatenate(
        [jnp.cos(two_pi * query_pos), jnp.sin(two_pi * query_pos)], axis=0
    )
    strengths = lax.dynamic_slice_in_dim(cosine_scale, row_index * per_dev, per_dev)
    scale = head_dim ** (-0.5)

    def update(state, kv_block, key_start, block_len):
        run_max, run_sum, accum = state
        scores = (
            jnp.einsum("hqd,hkd->hqk", queries, kv_block[0], preferred_element_type=jnp.float32)
            * scale
        )
        coords = lax.dynamic_slice_in_dim(cycle_feats, key_start, block_len, 1)
        cos_bias = jnp.dot(query_feats.T, coords, precision=highest)
        scores = scores + strengths[:, None, None] * cos_bias[None]
        new_max = jnp.maximum(run_max, jnp.max(scores, axis=-1))
        keep_part = jnp.exp(run_max - new_max)
        weights = jnp.exp(scores - new_max[:, :, None])
        run_sum = run_sum * keep_part + jnp.sum(weights, axis=-1)
        prob_bf = weights.astype(jnp.bfloat16)
        accum = accum * keep_part[:, None, :] + jnp.einsum(
            "hqk,hkd->hdq", prob_bf, kv_block[1], preferred_element_type=jnp.float32
        )
        return (new_max, run_sum, accum)

    initial = (
        jnp.full((per_dev, query_count), -1e30, jnp.float32),
        jnp.zeros((per_dev, query_count), jnp.float32),
        jnp.zeros((per_dev, head_dim, query_count), jnp.float32),
    )
    piece = lax.all_gather(key_vals, "cols", axis=2, tiled=True)
    key_total = piece.shape[2] // head_dim
    if key_total > 1024 and key_total % 1024 == 0:
        block_len = 1024
    else:
        block_len = key_total
    block_count = key_total // block_len
    kv_blocks = piece.reshape(2, per_dev, block_count, block_len, head_dim).transpose(2, 0, 1, 3, 4)
    block_starts = jnp.arange(block_count, dtype=jnp.int32) * block_len

    def one_block(state, block_in):
        kv_block, key_start = block_in
        return (update(state, kv_block, key_start, block_len), None)

    state, _ = lax.scan(one_block, initial, (kv_blocks, block_starts))
    _, run_sum, accum = state
    head_out = (
        (accum / run_sum[:, None, :])
        .transpose(0, 2, 1)
        .astype(jnp.bfloat16)
        .reshape(per_dev, query_count * head_dim)
    )
    returned = lax.all_to_all(head_out, "rows", split_axis=1, concat_axis=0, tiled=True)
    global_out = (
        returned.reshape(head_count, atom_count, head_dim)
        .transpose(1, 0, 2)
        .reshape(atom_count, model_dim)
    )
    combined = (local_out.astype(jnp.float32) + global_out.astype(jnp.float32)).astype(jnp.bfloat16)
    updated = features.astype(jnp.float32) + jnp.dot(
        combined, w_out, preferred_element_type=jnp.float32
    )
    return updated.astype(jnp.bfloat16)


def mm(a, b, dims):
    return lax.dot_general(a, b, (dims, ((), ())), preferred_element_type=jnp.float32)


def parts_of(value, count):
    out = []
    for _ in range(count):
        part = value.astype(jnp.bfloat16)
        out.append(part)
        value = value - part.astype(jnp.float32)
    return out


def unit(rows, cols, dtype):
    r = lax.broadcasted_iota(jnp.int32, (rows, cols), 0)
    c = lax.broadcasted_iota(jnp.int32, (rows, cols), 1)
    return (r == c).astype(dtype)


def to_column(row):
    count = row.shape[1]
    r = lax.broadcasted_iota(jnp.int32, (count, count), 0)
    c = lax.broadcasted_iota(jnp.int32, (count, count), 1)
    return jnp.sum(jnp.where(r == c, jnp.broadcast_to(row, (count, count)), 0.0), axis=1, keepdims=True)


def fetch(pairs, sems):
    copies = [pltpu.make_async_copy(src, dst, sems.at[k]) for k, (src, dst) in enumerate(pairs)]
    for copy in copies:
        copy.start()
    return copies


def settle(copies):
    for copy in copies:
        copy.wait()


def pack_kernel(*refs):
    sources, out_ref, tables = refs[:7], refs[7], refs[8:12]
    feat_ref, gain_ref, pos_ref, tmp_ref, sems = refs[12:]
    copies = fetch(list(zip(sources, (feat_ref, gain_ref, pos_ref, *tables))), sems)
    settle(copies[:3])
    atoms, dim = feat_ref.shape
    floats = feat_ref[...].astype(jnp.float32)
    spread = jnp.mean(floats * floats, axis=-1, keepdims=True)
    normed = floats * lax.rsqrt(spread + 1e-06) * gain_ref[...]
    out_ref[:, :dim] = normed.astype(jnp.bfloat16)
    tmp_ref[...] = jnp.zeros(tmp_ref.shape, jnp.float32)
    for p, part in enumerate(parts_of(pos_ref[...], 3)):
        tmp_ref[8 * p : 8 * p + 3, :] = part.astype(jnp.float32)
    eye = unit(atoms, atoms, jnp.bfloat16)
    turned = mm(eye, tmp_ref[...].astype(jnp.bfloat16), ((1,), (1,)))
    out_ref[:, dim:] = turned.astype(jnp.bfloat16)
    settle(copies[3:])


def prepare(
    head_dim,
    wqkv_ref,
    rw_ref,
    ro_ref,
    pw_ref,
    cs_ref,
    pack_ref,
    qexp_ref,
    w1_ref,
    w2_ref,
    str_ref,
    own_ref,
):
    atoms = pack_ref.shape[0]
    dim = wqkv_ref.shape[0]
    groups, rows, width = qexp_ref.shape
    per = rows // atoms
    pos = pack_ref[:, dim:].astype(jnp.float32)
    pos = pos + pltpu.roll(pos, 120, 1) + pltpu.roll(pos, 112, 1)
    own_ref[0] = pos
    own_ref[1] = jnp.cos(two_pi * pos)
    own_ref[2] = jnp.sin(two_pi * pos)
    h, m, l = parts_of(0.5 * rw_ref[...], 3)
    hidden = rw_ref.shape[1]
    row = lax.broadcasted_iota(jnp.int32, (16, hidden), 0)
    tail = jnp.zeros((16, hidden), jnp.float32)
    for k, part in enumerate(parts_of(0.5 * ro_ref[...], 3)):
        tail = jnp.where(row == k, part.astype(jnp.float32), tail)
    stack = jnp.concatenate([h, h, m, h, l, m, tail.astype(jnp.bfloat16)], axis=0)
    w1_ref[...] = mm(unit(hidden, hidden, jnp.bfloat16), stack, ((1,), (1,))).astype(jnp.bfloat16)
    h, l = parts_of(pw_ref[...], 2)
    w2_ref[...] = jnp.concatenate([h, h, l], axis=1)
    str_ref[...] = jnp.broadcast_to(to_column(cs_ref[...]), str_ref.shape)
    q = mm(pack_ref[:, :dim], wqkv_ref[:, :dim], ((1,), (0,)))
    q = q.astype(jnp.bfloat16).astype(jnp.float32)
    lane = lax.broadcasted_iota(jnp.int32, (per, width), 1) // head_dim
    sub = lax.broadcasted_iota(jnp.int32, (per, width), 0)
    keep = (lane == sub)[None]
    for g in range(groups):
        part = q[:, g * width : (g + 1) * width]
        spread = jnp.broadcast_to(part[:, None, :], (atoms, per, width))
        spread = jnp.where(keep, spread, 0.0).reshape(rows, width)
        qexp_ref[g] = spread.astype(jnp.bfloat16)


def position_tile(blocks, dim):
    pos = jnp.concatenate([block[:, dim:] for block in blocks], axis=0)
    r = lax.broadcasted_iota(jnp.int32, (8, 128), 0)
    c = lax.broadcasted_iota(jnp.int32, (8, 128), 1)
    out = []
    for p in range(3):
        pick = ((c == 8 * p + r) & (r < 3)).astype(jnp.bfloat16)
        part = mm(pick, pos, ((1,), (1,)))
        if part.shape[1] < 128:
            part = jnp.concatenate([part, jnp.zeros((8, 128 - part.shape[1]), jnp.float32)], axis=1)
        out.append(part)
    out.append(jnp.zeros((8, dim - 3 * 128), jnp.float32))
    return jnp.concatenate(out, axis=1).astype(jnp.bfloat16)


def repack_kernel(_, *refs):
    blocks, out_ref = refs[:-1], refs[-1]
    atoms = blocks[0].shape[0]
    dim = out_ref.shape[1]
    for k, block in enumerate(blocks):
        out_ref[k * atoms : (k + 1) * atoms, :] = block[:, :dim]
    out_ref[len(blocks) * atoms :, :] = position_tile(blocks, dim)


def piece_tiles(piece, counts):
    total = sum(counts)
    out = []
    for k in range(len(counts)):
        tail = piece[total + 8 * k : total + 8 * (k + 1), :].astype(jnp.float32)
        out.append(tail[:, :128] + tail[:, 128:256] + tail[:, 256:384])
    return out


def attend(qexp, keys, vals, scale, bias3):
    rows = qexp.shape[0]
    count = keys.shape[0]
    atoms, per, _ = bias3.shape
    s = mm(qexp, keys, ((1,), (1,))).reshape(atoms, per, count) * scale + bias3
    top = jnp.max(s, axis=-1, keepdims=True)
    p = jnp.exp(s - top)
    total = jnp.sum(p, axis=-1, keepdims=True)
    o = mm(p.astype(jnp.bfloat16).reshape(rows, count), vals, ((1,), (0,)))
    return top, total, o.reshape(atoms, per, vals.shape[1])


def absorb(head_dim, plan, pieces, wqkv_ref, qexp_ref, str_ref, own_ref, kv_ref):
    dim = wqkv_ref.shape[0]
    atoms = own_ref.shape[1]
    groups, rows, width = qexp_ref.shape
    per = rows // atoms
    rows_in = jnp.concatenate(
        [piece[: sum(counts), :] for piece, (_, counts) in zip(pieces, plan)], axis=0
    )
    kv = mm(rows_in, wqkv_ref[:, dim:], ((1,), (0,))).astype(jnp.bfloat16)
    at = 0
    tiles = []
    for piece, (start, counts) in zip(pieces, plan):
        kv_ref[start : start + sum(counts), :] = kv[at : at + sum(counts)]
        at += sum(counts)
        tiles += [t[:, :n] for t, n in zip(piece_tiles(piece, counts), counts)]
    pos8 = jnp.concatenate(tiles, axis=1)
    cos_k, sin_k = jnp.cos(two_pi * pos8), jnp.sin(two_pi * pos8)
    waves = None
    for c in range(3):
        term = own_ref[1, :, c : c + 1] * cos_k[c : c + 1] + own_ref[2, :, c : c + 1] * sin_k[c : c + 1]
        waves = term if waves is None else waves + term
    out = []
    for g in range(groups):
        low, high = g * width, (g + 1) * width
        bias3 = str_ref[g * per : (g + 1) * per, :1][None] * waves[:, None, :]
        out.append(
            attend(
                qexp_ref[g],
                kv[:, low:high],
                kv[:, dim + low : dim + high],
                head_dim ** (-0.5),
                bias3,
            )
        )
    return out


def widen(column, lanes):
    return jnp.broadcast_to(column, column.shape[:-1] + (lanes,))


def repeat_lanes(array, lanes):
    return jnp.concatenate([array] * (lanes // array.shape[-1]), axis=-1)


def first_kernel(head_dim, plan, *refs):
    blocks, ring_ref, wqkv_ref, tables = refs[:4], refs[4], refs[5], refs[6:10]
    core_ref, kv_ref, acc_ref, top_ref, sum_ref, qexp_ref, w1_ref, w2_ref, str_ref, own_ref = refs[10:]
    prepare(
        head_dim, wqkv_ref, *tables, blocks[0], qexp_ref, w1_ref, w2_ref, str_ref, own_ref
    )
    atoms = own_ref.shape[1]
    dim = wqkv_ref.shape[0]
    four, three = plan[0][1]
    for k, block in enumerate(blocks):
        core_ref[k * atoms : (k + 1) * atoms, :] = block[:, :dim]
    core_ref[four : four + three, :] = ring_ref[:three, :]
    core_ref[four + three : four + three + 8, :] = position_tile(blocks, dim)
    core_ref[four + three + 8 :, :] = ring_ref[three:, :]
    got = absorb(head_dim, plan, (core_ref,), wqkv_ref, qexp_ref, str_ref, own_ref, kv_ref)
    for g, (top, total, o) in enumerate(got):
        acc_ref[g] = o
        top_ref[g] = widen(top, 128)
        sum_ref[g] = widen(total, 128)


def merge(got, g, acc_ref, top_ref, sum_ref):
    top, total, o = got[g]
    width = o.shape[-1]
    best = jnp.maximum(widen(top, 128), top_ref[g])
    a, b = jnp.exp(top_ref[g] - best), jnp.exp(widen(top, 128) - best)
    summed = a * sum_ref[g] + b * widen(total, 128)
    acc = repeat_lanes(a, width) * acc_ref[g] + repeat_lanes(b, width) * o
    return best, summed, acc


def next_kernel(head_dim, plan, *refs):
    pieces = refs[: len(plan)]
    wqkv_ref, qexp_ref, str_ref, own_ref = refs[len(plan) : len(plan) + 4]
    _, acc_in, top_in, sum_in, kv_ref, acc_ref, top_ref, sum_ref = refs[len(plan) + 4 :]
    got = absorb(head_dim, plan, pieces, wqkv_ref, qexp_ref, str_ref, own_ref, kv_ref)
    for g in range(len(got)):
        best, summed, acc = merge(got, g, acc_in, top_in, sum_in)
        acc_ref[g] = acc
        top_ref[g] = best
        sum_ref[g] = summed


def chosen(row, lane):
    out = jnp.broadcast_to(row[:, :1], lane.shape)
    for e in range(1, row.shape[1]):
        out = jnp.where(lane == e, row[:, e : e + 1], out)
    return out


def last_kernel(head_dim, locate, plan, col_count, list_ref, valid_ref, shift_ref, cell_ref, *refs):
    piece_refs = refs[:8]
    (
        wqkv_ref,
        qexp_ref,
        str_ref,
        own_ref,
        w1_ref,
        w2_ref,
        wout_ref,
        in_ref,
        _,
        acc_in,
        top_in,
        sum_in,
        out_ref,
        kv_ref,
        near_ref,
        pos_ref,
        bias_ref,
    ) = refs[8:]
    dim = wqkv_ref.shape[0]
    atoms = own_ref.shape[1]
    groups, rows, width = qexp_ref.shape
    per = rows // atoms
    got = absorb(head_dim, plan[7:], piece_refs[7:], wqkv_ref, qexp_ref, str_ref, own_ref, kv_ref)
    at = 0
    for piece, (_, counts) in zip(piece_refs, plan):
        for tile in piece_tiles(piece, counts):
            pos_ref[at] = tile
            at += 1
    me = lax.axis_index("rows") * col_count + lax.axis_index("cols")
    entries = list_ref.shape[1]
    listed = entries * atoms
    lane = lax.broadcasted_iota(jnp.int32, (1, listed), 1) // atoms
    a_tile = 128 // atoms
    in_tile = lax.broadcasted_iota(jnp.int32, (1, 128), 1) // atoms
    tiles = []
    for e in range(entries):
        slot, tile, spot = locate(jnp.sum(list_ref[:, e : e + 1]) ^ me)
        start = pl.multiple_of(slot * atoms, atoms)
        near_ref[e * atoms : (e + 1) * atoms, :] = kv_ref[pl.ds(start, atoms), :]
        into = e % a_tile
        moved = pltpu.roll(pos_ref[tile], (into - spot + a_tile) % a_tile * atoms, 1)
        if into == 0:
            tiles.append(moved)
        else:
            tiles[-1] = jnp.where(in_tile == into, moved, tiles[-1])
    near = jnp.concatenate(tiles, axis=1)
    square = None
    for c in range(3):
        at = near[c : c + 1] + chosen(shift_ref[c].astype(jnp.float32), lane)
        gap = (at - own_ref[0, :, c : c + 1]) * cell_ref[:, c : c + 1]
        square = gap * gap if square is None else square + gap * gap
    dist = jnp.sqrt(square + 0.25)
    nrbf = (w1_ref.shape[1] - 16) // 6
    centers = lax.broadcasted_iota(jnp.int32, (nrbf, 1), 0).astype(jnp.float32) * rbf_step
    step = 16
    ones = jnp.ones((16, step * listed), jnp.bfloat16)
    for i in range(0, atoms, step):
        gap = jnp.concatenate([dist[j : j + 1] - centers for j in range(i, i + step)], axis=1)
        radial = jnp.exp(gap * gap * (-0.5 / rbf_width**2))
        h, m, l = parts_of(radial, 3)
        stack = jnp.concatenate([h, m, h, l, h, m, ones], axis=0)
        u = mm(w1_ref[...], stack, ((1,), (0,)))
        u = u + u * jnp.tanh(u)
        h, l = parts_of(u, 2)
        pair = mm(w2_ref[...], jnp.concatenate([h, l, h], axis=0), ((1,), (0,)))
        for j in range(step):
            for g in range(groups):
                bias_ref[g, i + j] = pair[g * per : (g + 1) * per, j * listed : (j + 1) * listed]
    live = (chosen(valid_ref[...], lane) > 0)[None]
    block = lax.broadcasted_iota(jnp.int32, (1, per, width), 2) // head_dim
    keep = block == lax.broadcasted_iota(jnp.int32, (1, per, width), 1)
    pieces = []
    for g in range(groups):
        low, high = g * width, (g + 1) * width
        _, summed, far = merge(got, g, acc_in, top_in, sum_in)
        far = far / repeat_lanes(summed, width)
        far = jnp.sum(jnp.where(keep, far, 0.0), axis=1).astype(jnp.bfloat16)
        s = mm(qexp_ref[g], near_ref[:, low:high], ((1,), (1,)))
        s = s.reshape(atoms, per, listed) * head_dim ** (-0.5) + bias_ref[g]
        s = jnp.where(live, s, -1e30)
        p = jnp.exp(s - jnp.max(s, axis=-1, keepdims=True))
        summed = jnp.sum(p, axis=-1, keepdims=True)
        o = mm(
            p.astype(jnp.bfloat16).reshape(rows, listed),
            near_ref[:, dim + low : dim + high],
            ((1,), (0,)),
        )
        o = o.reshape(atoms, per, width) / summed
        close = jnp.sum(jnp.where(keep, o, 0.0), axis=1).astype(jnp.bfloat16)
        pieces.append((close.astype(jnp.float32) + far.astype(jnp.float32)).astype(jnp.bfloat16))
    combined = jnp.concatenate(pieces, axis=1)
    moved = mm(combined, wout_ref[...], ((1,), (0,)))
    out_ref[...] = (in_ref[...].astype(jnp.float32) + moved).astype(jnp.bfloat16)


def call(kernel, outs, scratch, smem, args, aliases=None, hbm=0):
    vmem = pl.BlockSpec(memory_space=pltpu.VMEM)
    first = smem + hbm
    specs = [pl.BlockSpec(memory_space=pltpu.SMEM)] * smem
    specs += [pl.BlockSpec(memory_space=pltpu.HBM)] * hbm + [vmem] * (len(args) - first)
    placed = [pltpu.with_memory_space_constraint(a, pltpu.HBM) for a in args[smem:first]]
    placed += [pltpu.with_memory_space_constraint(a, pltpu.VMEM) for a in args[first:]]
    many = isinstance(outs, list)
    return pl.pallas_call(
        kernel,
        out_shape=outs,
        in_specs=specs,
        out_specs=[vmem] * len(outs) if many else vmem,
        scratch_shapes=scratch,
        input_output_aliases=aliases or {},
        compiler_params=pltpu.CompilerParams(vmem_limit_bytes=24 << 20),
    )(*args[:smem], *placed)


def on_device_small(
    features,
    positions,
    cell_lengths,
    block_lists,
    image_offsets,
    block_valid,
    norm_gain,
    w_qkv,
    w_out,
    rbf_weight,
    rbf_offset,
    pair_weight,
    cosine_scale,
):
    atoms, dim = features.shape
    heads = pair_weight.shape[1]
    hidden = pair_weight.shape[0]
    nrbf = rbf_weight.shape[0]
    head_dim = dim // heads
    row_count = lax.axis_size("rows")
    col_count = lax.axis_size("cols")
    total = row_count * col_count
    axes = ("rows", "cols")
    col_bits = col_count.bit_length() - 1
    flip = 1 << col_bits
    across_bits = (0, col_bits + 1)
    entries = block_lists.shape[1]
    width = 256
    per = width // head_dim
    groups = heads // per
    rows = atoms * per
    f32, bf16 = jnp.float32, jnp.bfloat16
    vm = pltpu.VMEM

    def swap(array, mask):
        return lax.ppermute(array, axes, [(i, i ^ mask) for i in range(total)])

    def locate(rel):
        up = (rel >> 1) & 3
        across = (rel & 1) + 2 * ((rel >> across_bits[1]) & 1)
        turn = (rel >> col_bits) & 1
        turn = turn ^ jnp.minimum(up, 1) ^ jnp.minimum(across, 1)
        far = jnp.minimum(up, 1)
        slot = turn * 16 + across + far * (3 + 2 * across + up)
        tile = turn * 5 + far * (1 + across)
        spot = across + far * (up - 1 - across)
        return slot, tile, spot

    tied = lax.optimization_barrier
    tables = (rbf_weight, rbf_offset[None], pair_weight.T, cosine_scale[None])
    pack, *tables = call(
        pack_kernel,
        [vm((atoms, dim + 128), bf16)] + [vm(table.shape, f32) for table in tables],
        [
            vm((atoms, dim), bf16),
            vm((1, dim), f32),
            vm(positions.shape, f32),
            vm((128, atoms), f32),
            pltpu.SemaphoreType.DMA((7,)),
        ],
        0,
        (features, norm_gain[None], positions, *tables),
        hbm=7,
    )
    across_masks = {"e": 1 | flip, "n": (1 << across_bits[1]) | flip}
    across_masks["d"] = 1 | across_masks["n"]
    ups = [swap(pack, (d << 1) | flip) for d in (1, 2, 3)]
    owns = [swap(pack, mask) for mask in across_masks.values()]
    four, three = 4 * atoms, 3 * atoms
    ring = call(repack_kernel, vm((three + 8, dim), bf16), [], 0, (w_qkv, *ups), hbm=1)
    east, north, diag = [swap(ring, mask) for mask in across_masks.values()]
    state_shapes = [
        vm((total * atoms, 2 * dim), bf16),
        vm((groups, atoms, per, width), f32),
        vm((groups, atoms, per, 128), f32),
        vm((groups, atoms, per, 128), f32),
    ]
    half = total // 2 * atoms
    plan = [(0, (four, three))] + [(four + k * three, (three,)) for k in (1, 2, 3)]
    plan += [(half + start, counts) for start, counts in plan]

    core, kv, acc, top, summed, qexp, w1, w2, strength, own = call(
        functools.partial(first_kernel, head_dim, plan[:1]),
        [vm((four + three + 16, dim), bf16)]
        + state_shapes
        + [
            vm((groups, rows, width), bf16),
            vm((hidden, 6 * nrbf + 16), bf16),
            vm((heads, 3 * hidden), bf16),
            vm((heads, 128), f32),
            vm((3, atoms, 128), f32),
        ],
        [],
        0,
        (pack, *owns, ring, w_qkv, *tables),
    )
    state = (kv, acc, top, summed)
    common = (w_qkv, qexp, strength, own)

    def step(places, pieces, state):
        at = len(pieces) + len(common)
        return call(
            functools.partial(next_kernel, head_dim, [plan[k] for k in places]),
            state_shapes,
            [],
            0,
            (*pieces, *common, *state),
            {at + k: k for k in range(4)},
        )

    core2 = swap(core, flip)
    east, north, state = tied((east, north, state))
    east2, north2 = swap(east, flip), swap(north, flip)
    state = step((1, 2, 4), (east, north, core2), state)
    diag, state = tied((diag, state))
    diag2 = swap(diag, flip)
    state = step((3, 5, 6), (diag, east2, north2), state)
    diag2, state = tied((diag2, state))
    updated, _ = call(
        functools.partial(last_kernel, head_dim, locate, plan, col_count),
        [jax.ShapeDtypeStruct((atoms, dim), bf16), state_shapes[0]],
        [
            vm((entries * atoms, 2 * dim), bf16),
            vm((10, 8, 128), f32),
            vm((groups, atoms, per, entries * atoms), f32),
        ],
        0,
        (
            block_lists,
            block_valid,
            image_offsets,
            cell_lengths[None],
            core,
            east,
            north,
            diag,
            core2,
            east2,
            north2,
            diag2,
            *common,
            w1,
            w2,
            w_out,
            features,
            *state,
        ),
        {4 + 8 + len(common) + 4: 1},
    )
    return updated


def solution(mesh):
    row_count, col_count = mesh.shape["rows"], mesh.shape["cols"]
    small = (row_count, col_count) == (4, 8)
    body = on_device_small if small else on_device
    return jax.shard_map(
        body,
        mesh=mesh,
        in_specs=(
            P(("rows", "cols"), None),
            P(None, ("rows", "cols")),
            P(),
            P(("rows", "cols"), None),
            P(None, ("rows", "cols"), None),
            P(("rows", "cols"), None),
            P(),
            P(),
            P(),
            P(),
            P(),
            P(),
            P(),
        ),
        out_specs=P(("rows", "cols"), None),
        check_vma=False,
    )
```

```python
import functools
import math

import jax
import jax.numpy as jnp
from jax import lax
from jax.experimental import pallas as pl
from jax.experimental.pallas import tpu as pltpu
from jax.sharding import PartitionSpec as P


rbf_step = 2.0
rbf_width = 2.0
two_pi = 2.0 * math.pi
highest = lax.Precision.HIGHEST


def with_halo(cells, sides, width):
    for axis, dim in sides:
        count = lax.axis_size(axis)
        head = lax.slice_in_dim(cells, 0, width, axis=dim)
        tail = lax.slice_in_dim(cells, cells.shape[dim] - width, cells.shape[dim], axis=dim)
        cells = jnp.concatenate(
            [
                lax.ppermute(tail, axis, [(i, (i + 1) % count) for i in range(count)]),
                cells,
                lax.ppermute(head, axis, [((i + 1) % count, i) for i in range(count)]),
            ],
            axis=dim,
        )
    return cells


def rms_rows(values, norm_gain):
    floats = values.astype(jnp.float32)
    spread = jnp.mean(floats * floats, axis=-1, keepdims=True)
    return (floats * lax.rsqrt(spread + 1e-06) * norm_gain).astype(jnp.bfloat16)


def near_attention(
    query_rows,
    own_pos,
    keys,
    key_pos,
    shifts,
    live,
    cell_lengths,
    rbf_weight,
    rbf_offset,
    pair_weight,
):
    entries, block_len = (keys.shape[0], keys.shape[1])
    model_dim = query_rows.shape[1]
    head_count = pair_weight.shape[1]
    head_dim = model_dim // head_count
    key_coords = key_pos.transpose(1, 0, 2) + shifts.astype(jnp.float32)[:, :, None]
    key_coords = key_coords.reshape(3, entries * block_len)
    displace = (key_coords[:, None, :] - own_pos[:, :, None]) * cell_lengths[:, None, None]
    distance = jnp.sqrt(jnp.sum(displace * displace, axis=0) + 0.25)
    centers = jnp.arange(rbf_weight.shape[0], dtype=jnp.float32) * rbf_step
    radial = jnp.exp(-((distance[None] - centers[:, None, None]) ** 2) * (0.5 / rbf_width**2))
    radial = radial.reshape(rbf_weight.shape[0], -1)
    hidden = jax.nn.silu(jnp.dot(rbf_weight.T, radial, precision=highest) + rbf_offset[:, None])
    pair_bias = jnp.dot(pair_weight.T, hidden, precision=highest).reshape(
        head_count, query_rows.shape[0], entries * block_len
    )
    query_heads = query_rows.reshape(-1, head_count, head_dim)
    key_heads = keys[:, :, :model_dim].reshape(entries * block_len, head_count, head_dim)
    value_heads = keys[:, :, model_dim:].reshape(entries * block_len, head_count, head_dim)
    scores = (
        jnp.einsum("ahd,khd->hak", query_heads, key_heads, preferred_element_type=jnp.float32)
        * head_dim ** (-0.5)
        + pair_bias
    )
    allowed = jnp.repeat(live > 0, block_len)
    scores = jnp.where(allowed[None, None, :], scores, -1e30)
    row_max = jnp.max(scores, axis=-1, keepdims=True)
    weights = jnp.exp(scores - row_max)
    row_sum = jnp.sum(weights, axis=-1, keepdims=True)
    prob_bf = weights.astype(jnp.bfloat16)
    attended = jnp.einsum(
        "hak,khd->ahd", prob_bf, value_heads, preferred_element_type=jnp.float32
    ) / row_sum.transpose(1, 0, 2)
    return attended.reshape(-1, model_dim).astype(jnp.bfloat16)


def on_device(
    features,
    positions,
    cell_lengths,
    block_lists,
    image_offsets,
    block_valid,
    norm_gain,
    w_qkv,
    w_out,
    rbf_weight,
    rbf_offset,
    pair_weight,
    cosine_scale,
):
    atom_count, model_dim = features.shape
    head_count = pair_weight.shape[1]
    head_dim = model_dim // head_count
    row_count = lax.axis_size("rows")
    col_count = lax.axis_size("cols")
    row_index = lax.axis_index("rows")
    col_index = lax.axis_index("cols")
    per_dev = head_count // row_count
    normed = rms_rows(features, norm_gain)
    packed = jnp.dot(normed, w_qkv, preferred_element_type=jnp.float32).astype(jnp.bfloat16)
    every_pos = lax.all_gather(positions, ("rows", "cols"), axis=1, tiled=True)
    near_rows = with_halo(normed[None, None], (("rows", 0), ("cols", 1)), 1)
    near_kv = jnp.dot(
        near_rows.reshape(9 * atom_count, model_dim),
        w_qkv[:, model_dim:],
        preferred_element_type=jnp.float32,
    )
    near_kv = near_kv.astype(jnp.bfloat16).reshape(9, atom_count, 2 * model_dim)
    listed = block_lists[0]
    list_row = listed // col_count
    list_col = listed % col_count
    slots = (list_row - row_index + 1) % row_count * 3 + (list_col - col_index + 1) % col_count
    keys = jnp.take(near_kv, slots, axis=0)
    block_pos = every_pos.reshape(3, row_count * col_count, atom_count)
    key_pos = jnp.take(block_pos, listed, axis=1).transpose(1, 0, 2)
    local_out = near_attention(
        packed[:, :model_dim],
        positions,
        keys,
        key_pos,
        image_offsets[:, 0, :],
        block_valid[0],
        cell_lengths,
        rbf_weight,
        rbf_offset,
        pair_weight,
    )
    grouped = (
        packed.reshape(atom_count, 3, head_count, head_dim)
        .transpose(1, 2, 0, 3)
        .reshape(3, head_count, atom_count * head_dim)
    )
    regrouped = lax.all_to_all(grouped, "rows", split_axis=1, concat_axis=2, tiled=True)
    query_count = row_count * atom_count
    queries = regrouped[0].reshape(per_dev, query_count, head_dim)
    key_vals = regrouped[1:]
    cycle_pos = (
        every_pos.reshape(3, row_count, col_count, atom_count).transpose(0, 2, 1, 3).reshape(3, -1)
    )
    query_pos = lax.dynamic_slice_in_dim(cycle_pos, col_index * query_count, query_count, 1)
    cycle_feats = jnp.concatenate(
        [jnp.cos(two_pi * cycle_pos), jnp.sin(two_pi * cycle_pos)], axis=0
    )
    query_feats = jnp.concatenate(
        [jnp.cos(two_pi * query_pos), jnp.sin(two_pi * query_pos)], axis=0
    )
    strengths = lax.dynamic_slice_in_dim(cosine_scale, row_index * per_dev, per_dev)
    scale = head_dim ** (-0.5)

    def update(state, kv_block, key_start, block_len):
        run_max, run_sum, accum = state
        scores = (
            jnp.einsum("hqd,hkd->hqk", queries, kv_block[0], preferred_element_type=jnp.float32)
            * scale
        )
        coords = lax.dynamic_slice_in_dim(cycle_feats, key_start, block_len, 1)
        cos_bias = jnp.dot(query_feats.T, coords, precision=highest)
        scores = scores + strengths[:, None, None] * cos_bias[None]
        new_max = jnp.maximum(run_max, jnp.max(scores, axis=-1))
        keep_part = jnp.exp(run_max - new_max)
        weights = jnp.exp(scores - new_max[:, :, None])
        run_sum = run_sum * keep_part + jnp.sum(weights, axis=-1)
        prob_bf = weights.astype(jnp.bfloat16)
        accum = accum * keep_part[:, None, :] + jnp.einsum(
            "hqk,hkd->hdq", prob_bf, kv_block[1], preferred_element_type=jnp.float32
        )
        return (new_max, run_sum, accum)

    initial = (
        jnp.full((per_dev, query_count), -1e30, jnp.float32),
        jnp.zeros((per_dev, query_count), jnp.float32),
        jnp.zeros((per_dev, head_dim, query_count), jnp.float32),
    )
    piece = lax.all_gather(key_vals, "cols", axis=2, tiled=True)
    key_total = piece.shape[2] // head_dim
    if key_total > 1024 and key_total % 1024 == 0:
        block_len = 1024
    else:
        block_len = key_total
    block_count = key_total // block_len
    kv_blocks = piece.reshape(2, per_dev, block_count, block_len, head_dim).transpose(2, 0, 1, 3, 4)
    block_starts = jnp.arange(block_count, dtype=jnp.int32) * block_len

    def one_block(state, block_in):
        kv_block, key_start = block_in
        return (update(state, kv_block, key_start, block_len), None)

    state, _ = lax.scan(one_block, initial, (kv_blocks, block_starts))
    _, run_sum, accum = state
    head_out = (
        (accum / run_sum[:, None, :])
        .transpose(0, 2, 1)
        .astype(jnp.bfloat16)
        .reshape(per_dev, query_count * head_dim)
    )
    returned = lax.all_to_all(head_out, "rows", split_axis=1, concat_axis=0, tiled=True)
    global_out = (
        returned.reshape(head_count, atom_count, head_dim)
        .transpose(1, 0, 2)
        .reshape(atom_count, model_dim)
    )
    combined = (local_out.astype(jnp.float32) + global_out.astype(jnp.float32)).astype(jnp.bfloat16)
    updated = features.astype(jnp.float32) + jnp.dot(
        combined, w_out, preferred_element_type=jnp.float32
    )
    return updated.astype(jnp.bfloat16)


def mm(a, b, dims):
    return lax.dot_general(a, b, (dims, ((), ())), preferred_element_type=jnp.float32)


def parts_of(value, count):
    out = []
    for _ in range(count):
        part = value.astype(jnp.bfloat16)
        out.append(part)
        value = value - part.astype(jnp.float32)
    return out


def unit(rows, cols, dtype):
    r = lax.broadcasted_iota(jnp.int32, (rows, cols), 0)
    c = lax.broadcasted_iota(jnp.int32, (rows, cols), 1)
    return (r == c).astype(dtype)


def to_column(row):
    count = row.shape[1]
    r = lax.broadcasted_iota(jnp.int32, (count, count), 0)
    c = lax.broadcasted_iota(jnp.int32, (count, count), 1)
    return jnp.sum(jnp.where(r == c, jnp.broadcast_to(row, (count, count)), 0.0), axis=1, keepdims=True)


def fetch(pairs, sems):
    copies = [pltpu.make_async_copy(src, dst, sems.at[k]) for k, (src, dst) in enumerate(pairs)]
    for copy in copies:
        copy.start()
    return copies


def settle(copies):
    for copy in copies:
        copy.wait()


def pack_kernel(*refs):
    sources, out_ref, tables = refs[:7], refs[7], refs[8:12]
    feat_ref, gain_ref, pos_ref, tmp_ref, sems = refs[12:]
    copies = fetch(list(zip(sources, (feat_ref, gain_ref, pos_ref, *tables))), sems)
    settle(copies[:3])
    atoms, dim = feat_ref.shape
    floats = feat_ref[...].astype(jnp.float32)
    spread = jnp.mean(floats * floats, axis=-1, keepdims=True)
    normed = floats * lax.rsqrt(spread + 1e-06) * gain_ref[...]
    out_ref[:, :dim] = normed.astype(jnp.bfloat16)
    tmp_ref[...] = jnp.zeros(tmp_ref.shape, jnp.float32)
    for p, part in enumerate(parts_of(pos_ref[...], 3)):
        tmp_ref[8 * p : 8 * p + 3, :] = part.astype(jnp.float32)
    eye = unit(atoms, atoms, jnp.bfloat16)
    turned = mm(eye, tmp_ref[...].astype(jnp.bfloat16), ((1,), (1,)))
    out_ref[:, dim:] = turned.astype(jnp.bfloat16)
    settle(copies[3:])


def prepare(
    head_dim,
    wqkv_ref,
    rw_ref,
    ro_ref,
    pw_ref,
    cs_ref,
    pack_ref,
    qexp_ref,
    w1_ref,
    w2_ref,
    str_ref,
    own_ref,
):
    atoms = pack_ref.shape[0]
    dim = wqkv_ref.shape[0]
    groups, rows, width = qexp_ref.shape
    per = rows // atoms
    pos = pack_ref[:, dim:].astype(jnp.float32)
    pos = pos + pltpu.roll(pos, 120, 1) + pltpu.roll(pos, 112, 1)
    own_ref[0] = pos
    own_ref[1] = jnp.cos(two_pi * pos)
    own_ref[2] = jnp.sin(two_pi * pos)
    h, m, l = parts_of(0.5 * rw_ref[...], 3)
    hidden = rw_ref.shape[1]
    row = lax.broadcasted_iota(jnp.int32, (16, hidden), 0)
    tail = jnp.zeros((16, hidden), jnp.float32)
    for k, part in enumerate(parts_of(0.5 * ro_ref[...], 3)):
        tail = jnp.where(row == k, part.astype(jnp.float32), tail)
    stack = jnp.concatenate([h, h, m, h, l, m, tail.astype(jnp.bfloat16)], axis=0)
    w1_ref[...] = mm(unit(hidden, hidden, jnp.bfloat16), stack, ((1,), (1,))).astype(jnp.bfloat16)
    h, l = parts_of(pw_ref[...], 2)
    w2_ref[...] = jnp.concatenate([h, h, l], axis=1)
    str_ref[...] = jnp.broadcast_to(to_column(cs_ref[...]), str_ref.shape)
    q = mm(pack_ref[:, :dim], wqkv_ref[:, :dim], ((1,), (0,)))
    q = q.astype(jnp.bfloat16).astype(jnp.float32)
    lane = lax.broadcasted_iota(jnp.int32, (per, width), 1) // head_dim
    sub = lax.broadcasted_iota(jnp.int32, (per, width), 0)
    keep = (lane == sub)[None]
    for g in range(groups):
        part = q[:, g * width : (g + 1) * width]
        spread = jnp.broadcast_to(part[:, None, :], (atoms, per, width))
        spread = jnp.where(keep, spread, 0.0).reshape(rows, width)
        qexp_ref[g] = spread.astype(jnp.bfloat16)


def position_tile(blocks, dim):
    pos = jnp.concatenate([block[:, dim:] for block in blocks], axis=0)
    r = lax.broadcasted_iota(jnp.int32, (8, 128), 0)
    c = lax.broadcasted_iota(jnp.int32, (8, 128), 1)
    out = []
    for p in range(3):
        pick = ((c == 8 * p + r) & (r < 3)).astype(jnp.bfloat16)
        part = mm(pick, pos, ((1,), (1,)))
        if part.shape[1] < 128:
            part = jnp.concatenate([part, jnp.zeros((8, 128 - part.shape[1]), jnp.float32)], axis=1)
        out.append(part)
    out.append(jnp.zeros((8, dim - 3 * 128), jnp.float32))
    return jnp.concatenate(out, axis=1).astype(jnp.bfloat16)


def repack_kernel(_, *refs):
    blocks, out_ref = refs[:-1], refs[-1]
    atoms = blocks[0].shape[0]
    dim = out_ref.shape[1]
    for k, block in enumerate(blocks):
        out_ref[k * atoms : (k + 1) * atoms, :] = block[:, :dim]
    out_ref[len(blocks) * atoms :, :] = position_tile(blocks, dim)


def piece_tiles(piece, counts):
    total = sum(counts)
    out = []
    for k in range(len(counts)):
        tail = piece[total + 8 * k : total + 8 * (k + 1), :].astype(jnp.float32)
        out.append(tail[:, :128] + tail[:, 128:256] + tail[:, 256:384])
    return out


def attend(qexp, keys, vals, scale, bias3):
    rows = qexp.shape[0]
    count = keys.shape[0]
    atoms, per, _ = bias3.shape
    s = mm(qexp, keys, ((1,), (1,))).reshape(atoms, per, count) * scale + bias3
    top = jnp.max(s, axis=-1, keepdims=True)
    p = jnp.exp(s - top)
    total = jnp.sum(p, axis=-1, keepdims=True)
    o = mm(p.astype(jnp.bfloat16).reshape(rows, count), vals, ((1,), (0,)))
    return top, total, o.reshape(atoms, per, vals.shape[1])


def absorb(head_dim, plan, pieces, wqkv_ref, qexp_ref, str_ref, own_ref, kv_ref):
    dim = wqkv_ref.shape[0]
    atoms = own_ref.shape[1]
    groups, rows, width = qexp_ref.shape
    per = rows // atoms
    rows_in = jnp.concatenate(
        [piece[: sum(counts), :] for piece, (_, counts) in zip(pieces, plan)], axis=0
    )
    kv = mm(rows_in, wqkv_ref[:, dim:], ((1,), (0,))).astype(jnp.bfloat16)
    at = 0
    tiles = []
    for piece, (start, counts) in zip(pieces, plan):
        kv_ref[start : start + sum(counts), :] = kv[at : at + sum(counts)]
        at += sum(counts)
        tiles += [t[:, :n] for t, n in zip(piece_tiles(piece, counts), counts)]
    pos8 = jnp.concatenate(tiles, axis=1)
    cos_k, sin_k = jnp.cos(two_pi * pos8), jnp.sin(two_pi * pos8)
    waves = None
    for c in range(3):
        term = own_ref[1, :, c : c + 1] * cos_k[c : c + 1] + own_ref[2, :, c : c + 1] * sin_k[c : c + 1]
        waves = term if waves is None else waves + term
    out = []
    for g in range(groups):
        low, high = g * width, (g + 1) * width
        bias3 = str_ref[g * per : (g + 1) * per, :1][None] * waves[:, None, :]
        out.append(
            attend(
                qexp_ref[g],
                kv[:, low:high],
                kv[:, dim + low : dim + high],
                head_dim ** (-0.5),
                bias3,
            )
        )
    return out


def widen(column, lanes):
    return jnp.broadcast_to(column, column.shape[:-1] + (lanes,))


def repeat_lanes(array, lanes):
    return jnp.concatenate([array] * (lanes // array.shape[-1]), axis=-1)


def core_kernel(*refs):
    blocks, ring_ref, core_ref = refs[:4], refs[4], refs[5]
    atoms = blocks[0].shape[0]
    dim = core_ref.shape[1]
    four, three = 4 * atoms, 3 * atoms
    for k, block in enumerate(blocks):
        core_ref[k * atoms : (k + 1) * atoms, :] = block[:, :dim]
    core_ref[four : four + three, :] = ring_ref[:three, :]
    core_ref[four + three : four + three + 8, :] = position_tile(blocks, dim)
    core_ref[four + three + 8 :, :] = ring_ref[three:, :]


def first_kernel(head_dim, plan, *refs):
    pack_ref, core_ref, wqkv_ref, tables = refs[0], refs[1], refs[2], refs[3:7]
    kv_ref, acc_ref, top_ref, sum_ref, qexp_ref, w1_ref, w2_ref, str_ref, own_ref = refs[7:]
    prepare(head_dim, wqkv_ref, *tables, pack_ref, qexp_ref, w1_ref, w2_ref, str_ref, own_ref)
    got = absorb(head_dim, plan, (core_ref,), wqkv_ref, qexp_ref, str_ref, own_ref, kv_ref)
    for g, (top, total, o) in enumerate(got):
        acc_ref[g] = o
        top_ref[g] = widen(top, 128)
        sum_ref[g] = widen(total, 128)


def merge(got, g, acc_ref, top_ref, sum_ref):
    top, total, o = got[g]
    width = o.shape[-1]
    best = jnp.maximum(widen(top, 128), top_ref[g])
    a, b = jnp.exp(top_ref[g] - best), jnp.exp(widen(top, 128) - best)
    summed = a * sum_ref[g] + b * widen(total, 128)
    acc = repeat_lanes(a, width) * acc_ref[g] + repeat_lanes(b, width) * o
    return best, summed, acc


def next_kernel(head_dim, plan, *refs):
    pieces = refs[: len(plan)]
    wqkv_ref, qexp_ref, str_ref, own_ref = refs[len(plan) : len(plan) + 4]
    _, acc_in, top_in, sum_in, kv_ref, acc_ref, top_ref, sum_ref = refs[len(plan) + 4 :]
    got = absorb(head_dim, plan, pieces, wqkv_ref, qexp_ref, str_ref, own_ref, kv_ref)
    for g in range(len(got)):
        best, summed, acc = merge(got, g, acc_in, top_in, sum_in)
        acc_ref[g] = acc
        top_ref[g] = best
        sum_ref[g] = summed


def chosen(row, lane):
    out = jnp.broadcast_to(row[:, :1], lane.shape)
    for e in range(1, row.shape[1]):
        out = jnp.where(lane == e, row[:, e : e + 1], out)
    return out


def last_kernel(head_dim, locate, plan, col_count, list_ref, valid_ref, shift_ref, cell_ref, *refs):
    piece_refs = refs[:8]
    (
        wqkv_ref,
        qexp_ref,
        str_ref,
        own_ref,
        w1_ref,
        w2_ref,
        wout_ref,
        in_ref,
        _,
        acc_in,
        top_in,
        sum_in,
        out_ref,
        kv_ref,
        near_ref,
        pos_ref,
        bias_ref,
    ) = refs[8:]
    dim = wqkv_ref.shape[0]
    atoms = own_ref.shape[1]
    groups, rows, width = qexp_ref.shape
    per = rows // atoms
    got = absorb(head_dim, plan[7:], piece_refs[7:], wqkv_ref, qexp_ref, str_ref, own_ref, kv_ref)
    at = 0
    for piece, (_, counts) in zip(piece_refs, plan):
        for tile in piece_tiles(piece, counts):
            pos_ref[at] = tile
            at += 1
    me = lax.axis_index("rows") * col_count + lax.axis_index("cols")
    entries = list_ref.shape[1]
    listed = entries * atoms
    lane = lax.broadcasted_iota(jnp.int32, (1, listed), 1) // atoms
    a_tile = 128 // atoms
    in_tile = lax.broadcasted_iota(jnp.int32, (1, 128), 1) // atoms
    tiles = []
    for e in range(entries):
        slot, tile, spot = locate(jnp.sum(list_ref[:, e : e + 1]) ^ me)
        start = pl.multiple_of(slot * atoms, atoms)
        near_ref[e * atoms : (e + 1) * atoms, :] = kv_ref[pl.ds(start, atoms), :]
        into = e % a_tile
        moved = pltpu.roll(pos_ref[tile], (into - spot + a_tile) % a_tile * atoms, 1)
        if into == 0:
            tiles.append(moved)
        else:
            tiles[-1] = jnp.where(in_tile == into, moved, tiles[-1])
    near = jnp.concatenate(tiles, axis=1)
    square = None
    for c in range(3):
        at = near[c : c + 1] + chosen(shift_ref[c].astype(jnp.float32), lane)
        gap = (at - own_ref[0, :, c : c + 1]) * cell_ref[:, c : c + 1]
        square = gap * gap if square is None else square + gap * gap
    dist = jnp.sqrt(square + 0.25)
    nrbf = (w1_ref.shape[1] - 16) // 6
    centers = lax.broadcasted_iota(jnp.int32, (nrbf, 1), 0).astype(jnp.float32) * rbf_step
    step = 16
    ones = jnp.ones((16, step * listed), jnp.bfloat16)
    for i in range(0, atoms, step):
        gap = jnp.concatenate([dist[j : j + 1] - centers for j in range(i, i + step)], axis=1)
        radial = jnp.exp(gap * gap * (-0.5 / rbf_width**2))
        h, m, l = parts_of(radial, 3)
        stack = jnp.concatenate([h, m, h, l, h, m, ones], axis=0)
        u = mm(w1_ref[...], stack, ((1,), (0,)))
        u = u + u * jnp.tanh(u)
        h, l = parts_of(u, 2)
        pair = mm(w2_ref[...], jnp.concatenate([h, l, h], axis=0), ((1,), (0,)))
        for j in range(step):
            for g in range(groups):
                bias_ref[g, i + j] = pair[g * per : (g + 1) * per, j * listed : (j + 1) * listed]
    live = (chosen(valid_ref[...], lane) > 0)[None]
    block = lax.broadcasted_iota(jnp.int32, (1, per, width), 2) // head_dim
    keep = block == lax.broadcasted_iota(jnp.int32, (1, per, width), 1)
    pieces = []
    for g in range(groups):
        low, high = g * width, (g + 1) * width
        _, summed, far = merge(got, g, acc_in, top_in, sum_in)
        far = far / repeat_lanes(summed, width)
        far = jnp.sum(jnp.where(keep, far, 0.0), axis=1).astype(jnp.bfloat16)
        s = mm(qexp_ref[g], near_ref[:, low:high], ((1,), (1,)))
        s = s.reshape(atoms, per, listed) * head_dim ** (-0.5) + bias_ref[g]
        s = jnp.where(live, s, -1e30)
        p = jnp.exp(s - jnp.max(s, axis=-1, keepdims=True))
        summed = jnp.sum(p, axis=-1, keepdims=True)
        o = mm(
            p.astype(jnp.bfloat16).reshape(rows, listed),
            near_ref[:, dim + low : dim + high],
            ((1,), (0,)),
        )
        o = o.reshape(atoms, per, width) / summed
        close = jnp.sum(jnp.where(keep, o, 0.0), axis=1).astype(jnp.bfloat16)
        pieces.append((close.astype(jnp.float32) + far.astype(jnp.float32)).astype(jnp.bfloat16))
    combined = jnp.concatenate(pieces, axis=1)
    moved = mm(combined, wout_ref[...], ((1,), (0,)))
    out_ref[...] = (in_ref[...].astype(jnp.float32) + moved).astype(jnp.bfloat16)


def call(kernel, outs, scratch, smem, args, aliases=None, hbm=0):
    vmem = pl.BlockSpec(memory_space=pltpu.VMEM)
    first = smem + hbm
    specs = [pl.BlockSpec(memory_space=pltpu.SMEM)] * smem
    specs += [pl.BlockSpec(memory_space=pltpu.HBM)] * hbm + [vmem] * (len(args) - first)
    placed = [pltpu.with_memory_space_constraint(a, pltpu.HBM) for a in args[smem:first]]
    placed += [pltpu.with_memory_space_constraint(a, pltpu.VMEM) for a in args[first:]]
    many = isinstance(outs, list)
    return pl.pallas_call(
        kernel,
        out_shape=outs,
        in_specs=specs,
        out_specs=[vmem] * len(outs) if many else vmem,
        scratch_shapes=scratch,
        input_output_aliases=aliases or {},
        compiler_params=pltpu.CompilerParams(vmem_limit_bytes=24 << 20),
    )(*args[:smem], *placed)


def on_device_small(
    features,
    positions,
    cell_lengths,
    block_lists,
    image_offsets,
    block_valid,
    norm_gain,
    w_qkv,
    w_out,
    rbf_weight,
    rbf_offset,
    pair_weight,
    cosine_scale,
):
    atoms, dim = features.shape
    heads = pair_weight.shape[1]
    hidden = pair_weight.shape[0]
    nrbf = rbf_weight.shape[0]
    head_dim = dim // heads
    row_count = lax.axis_size("rows")
    col_count = lax.axis_size("cols")
    total = row_count * col_count
    axes = ("rows", "cols")
    col_bits = col_count.bit_length() - 1
    flip = 1 << col_bits
    across_bits = (0, col_bits + 1)
    entries = block_lists.shape[1]
    width = 256
    per = width // head_dim
    groups = heads // per
    rows = atoms * per
    f32, bf16 = jnp.float32, jnp.bfloat16
    vm = pltpu.VMEM

    def swap(array, mask):
        return lax.ppermute(array, axes, [(i, i ^ mask) for i in range(total)])

    def locate(rel):
        up = (rel >> 1) & 3
        across = (rel & 1) + 2 * ((rel >> across_bits[1]) & 1)
        turn = (rel >> col_bits) & 1
        turn = turn ^ jnp.minimum(up, 1) ^ jnp.minimum(across, 1)
        far = jnp.minimum(up, 1)
        slot = turn * 16 + across + far * (3 + 2 * across + up)
        tile = turn * 5 + far * (1 + across)
        spot = across + far * (up - 1 - across)
        return slot, tile, spot

    tied = lax.optimization_barrier
    tables = (rbf_weight, rbf_offset[None], pair_weight.T, cosine_scale[None])
    pack, *tables = call(
        pack_kernel,
        [vm((atoms, dim + 128), bf16)] + [vm(table.shape, f32) for table in tables],
        [
            vm((atoms, dim), bf16),
            vm((1, dim), f32),
            vm(positions.shape, f32),
            vm((128, atoms), f32),
            pltpu.SemaphoreType.DMA((7,)),
        ],
        0,
        (features, norm_gain[None], positions, *tables),
        hbm=7,
    )
    across_masks = {"e": 1 | flip, "n": (1 << across_bits[1]) | flip}
    across_masks["d"] = 1 | across_masks["n"]
    ups = [swap(pack, (d << 1) | flip) for d in (1, 2, 3)]
    owns = [swap(pack, mask) for mask in across_masks.values()]
    four, three = 4 * atoms, 3 * atoms
    ring = call(repack_kernel, vm((three + 8, dim), bf16), [], 0, (w_qkv, *ups), hbm=1)
    east, north, diag = [swap(ring, mask) for mask in across_masks.values()]
    state_shapes = [
        vm((total * atoms, 2 * dim), bf16),
        vm((groups, atoms, per, width), f32),
        vm((groups, atoms, per, 128), f32),
        vm((groups, atoms, per, 128), f32),
    ]
    half = total // 2 * atoms
    plan = [(0, (four, three))] + [(four + k * three, (three,)) for k in (1, 2, 3)]
    plan += [(half + start, counts) for start, counts in plan]

    core = call(core_kernel, vm((four + three + 16, dim), bf16), [], 0, (pack, *owns, ring))
    core2 = swap(core, flip)
    kv, acc, top, summed, qexp, w1, w2, strength, own = call(
        functools.partial(first_kernel, head_dim, plan[:1]),
        state_shapes
        + [
            vm((groups, rows, width), bf16),
            vm((hidden, 6 * nrbf + 16), bf16),
            vm((heads, 3 * hidden), bf16),
            vm((heads, 128), f32),
            vm((3, atoms, 128), f32),
        ],
        [],
        0,
        (pack, core, w_qkv, *tables),
    )
    state = (kv, acc, top, summed)
    common = (w_qkv, qexp, strength, own)

    def step(places, pieces, state):
        at = len(pieces) + len(common)
        return call(
            functools.partial(next_kernel, head_dim, [plan[k] for k in places]),
            state_shapes,
            [],
            0,
            (*pieces, *common, *state),
            {at + k: k for k in range(4)},
        )

    core2, state = tied((core2, state))
    state = step((4,), (core2,), state)
    east, north, state = tied((east, north, state))
    east2, north2 = swap(east, flip), swap(north, flip)
    state = step((1, 2), (east, north), state)
    diag, state = tied((diag, state))
    diag2 = swap(diag, flip)
    state = step((3, 5, 6), (diag, east2, north2), state)
    diag2, state = tied((diag2, state))
    updated, _ = call(
        functools.partial(last_kernel, head_dim, locate, plan, col_count),
        [jax.ShapeDtypeStruct((atoms, dim), bf16), state_shapes[0]],
        [
            vm((entries * atoms, 2 * dim), bf16),
            vm((10, 8, 128), f32),
            vm((groups, atoms, per, entries * atoms), f32),
        ],
        0,
        (
            block_lists,
            block_valid,
            image_offsets,
            cell_lengths[None],
            core,
            east,
            north,
            diag,
            core2,
            east2,
            north2,
            diag2,
            *common,
            w1,
            w2,
            w_out,
            features,
            *state,
        ),
        {4 + 8 + len(common) + 4: 1},
    )
    return updated


def solution(mesh):
    row_count, col_count = mesh.shape["rows"], mesh.shape["cols"]
    small = (row_count, col_count) == (4, 8)
    body = on_device_small if small else on_device
    return jax.shard_map(
        body,
        mesh=mesh,
        in_specs=(
            P(("rows", "cols"), None),
            P(None, ("rows", "cols")),
            P(),
            P(("rows", "cols"), None),
            P(None, ("rows", "cols"), None),
            P(("rows", "cols"), None),
            P(),
            P(),
            P(),
            P(),
            P(),
            P(),
            P(),
        ),
        out_specs=P(("rows", "cols"), None),
        check_vma=False,
    )
```

```python
import functools
import math

import jax
import jax.numpy as jnp
from jax import lax
from jax.experimental import pallas as pl
from jax.experimental.pallas import tpu as pltpu
from jax.sharding import PartitionSpec as P


rbf_step = 2.0
rbf_width = 2.0
two_pi = 2.0 * math.pi
log2_e = 1.0 / math.log(2.0)
highest = lax.Precision.HIGHEST


def with_halo(cells, sides, width):
    for axis, dim in sides:
        count = lax.axis_size(axis)
        head = lax.slice_in_dim(cells, 0, width, axis=dim)
        tail = lax.slice_in_dim(cells, cells.shape[dim] - width, cells.shape[dim], axis=dim)
        cells = jnp.concatenate(
            [
                lax.ppermute(tail, axis, [(i, (i + 1) % count) for i in range(count)]),
                cells,
                lax.ppermute(head, axis, [((i + 1) % count, i) for i in range(count)]),
            ],
            axis=dim,
        )
    return cells


def rms_rows(values, norm_gain):
    floats = values.astype(jnp.float32)
    spread = jnp.mean(floats * floats, axis=-1, keepdims=True)
    return (floats * lax.rsqrt(spread + 1e-06) * norm_gain).astype(jnp.bfloat16)


def near_attention(
    query_rows,
    own_pos,
    keys,
    key_pos,
    shifts,
    live,
    cell_lengths,
    rbf_weight,
    rbf_offset,
    pair_weight,
):
    entries, block_len = (keys.shape[0], keys.shape[1])
    model_dim = query_rows.shape[1]
    head_count = pair_weight.shape[1]
    head_dim = model_dim // head_count
    key_coords = key_pos.transpose(1, 0, 2) + shifts.astype(jnp.float32)[:, :, None]
    key_coords = key_coords.reshape(3, entries * block_len)
    displace = (key_coords[:, None, :] - own_pos[:, :, None]) * cell_lengths[:, None, None]
    distance = jnp.sqrt(jnp.sum(displace * displace, axis=0) + 0.25)
    centers = jnp.arange(rbf_weight.shape[0], dtype=jnp.float32) * rbf_step
    radial = jnp.exp(-((distance[None] - centers[:, None, None]) ** 2) * (0.5 / rbf_width**2))
    radial = radial.reshape(rbf_weight.shape[0], -1)
    hidden = jax.nn.silu(jnp.dot(rbf_weight.T, radial, precision=highest) + rbf_offset[:, None])
    pair_bias = jnp.dot(pair_weight.T, hidden, precision=highest).reshape(
        head_count, query_rows.shape[0], entries * block_len
    )
    query_heads = query_rows.reshape(-1, head_count, head_dim)
    key_heads = keys[:, :, :model_dim].reshape(entries * block_len, head_count, head_dim)
    value_heads = keys[:, :, model_dim:].reshape(entries * block_len, head_count, head_dim)
    scores = (
        jnp.einsum("ahd,khd->hak", query_heads, key_heads, preferred_element_type=jnp.float32)
        * head_dim ** (-0.5)
        + pair_bias
    )
    allowed = jnp.repeat(live > 0, block_len)
    scores = jnp.where(allowed[None, None, :], scores, -1e30)
    row_max = jnp.max(scores, axis=-1, keepdims=True)
    weights = jnp.exp(scores - row_max)
    row_sum = jnp.sum(weights, axis=-1, keepdims=True)
    prob_bf = weights.astype(jnp.bfloat16)
    attended = jnp.einsum(
        "hak,khd->ahd", prob_bf, value_heads, preferred_element_type=jnp.float32
    ) / row_sum.transpose(1, 0, 2)
    return attended.reshape(-1, model_dim).astype(jnp.bfloat16)


def on_device(
    features,
    positions,
    cell_lengths,
    block_lists,
    image_offsets,
    block_valid,
    norm_gain,
    w_qkv,
    w_out,
    rbf_weight,
    rbf_offset,
    pair_weight,
    cosine_scale,
):
    atom_count, model_dim = features.shape
    head_count = pair_weight.shape[1]
    head_dim = model_dim // head_count
    row_count = lax.axis_size("rows")
    col_count = lax.axis_size("cols")
    row_index = lax.axis_index("rows")
    col_index = lax.axis_index("cols")
    per_dev = head_count // row_count
    normed = rms_rows(features, norm_gain)
    packed = jnp.dot(normed, w_qkv, preferred_element_type=jnp.float32).astype(jnp.bfloat16)
    every_pos = lax.all_gather(positions, ("rows", "cols"), axis=1, tiled=True)
    near_rows = with_halo(normed[None, None], (("rows", 0), ("cols", 1)), 1)
    near_kv = jnp.dot(
        near_rows.reshape(9 * atom_count, model_dim),
        w_qkv[:, model_dim:],
        preferred_element_type=jnp.float32,
    )
    near_kv = near_kv.astype(jnp.bfloat16).reshape(9, atom_count, 2 * model_dim)
    listed = block_lists[0]
    list_row = listed // col_count
    list_col = listed % col_count
    slots = (list_row - row_index + 1) % row_count * 3 + (list_col - col_index + 1) % col_count
    keys = jnp.take(near_kv, slots, axis=0)
    block_pos = every_pos.reshape(3, row_count * col_count, atom_count)
    key_pos = jnp.take(block_pos, listed, axis=1).transpose(1, 0, 2)
    local_out = near_attention(
        packed[:, :model_dim],
        positions,
        keys,
        key_pos,
        image_offsets[:, 0, :],
        block_valid[0],
        cell_lengths,
        rbf_weight,
        rbf_offset,
        pair_weight,
    )
    grouped = (
        packed.reshape(atom_count, 3, head_count, head_dim)
        .transpose(1, 2, 0, 3)
        .reshape(3, head_count, atom_count * head_dim)
    )
    regrouped = lax.all_to_all(grouped, "rows", split_axis=1, concat_axis=2, tiled=True)
    query_count = row_count * atom_count
    queries = regrouped[0].reshape(per_dev, query_count, head_dim)
    key_vals = regrouped[1:]
    cycle_pos = (
        every_pos.reshape(3, row_count, col_count, atom_count).transpose(0, 2, 1, 3).reshape(3, -1)
    )
    query_pos = lax.dynamic_slice_in_dim(cycle_pos, col_index * query_count, query_count, 1)
    cycle_feats = jnp.concatenate(
        [jnp.cos(two_pi * cycle_pos), jnp.sin(two_pi * cycle_pos)], axis=0
    )
    query_feats = jnp.concatenate(
        [jnp.cos(two_pi * query_pos), jnp.sin(two_pi * query_pos)], axis=0
    )
    strengths = lax.dynamic_slice_in_dim(cosine_scale, row_index * per_dev, per_dev)
    scale = head_dim ** (-0.5)

    def update(state, kv_block, key_start, block_len):
        run_max, run_sum, accum = state
        scores = (
            jnp.einsum("hqd,hkd->hqk", queries, kv_block[0], preferred_element_type=jnp.float32)
            * scale
        )
        coords = lax.dynamic_slice_in_dim(cycle_feats, key_start, block_len, 1)
        cos_bias = jnp.dot(query_feats.T, coords, precision=highest)
        scores = scores + strengths[:, None, None] * cos_bias[None]
        new_max = jnp.maximum(run_max, jnp.max(scores, axis=-1))
        keep_part = jnp.exp(run_max - new_max)
        weights = jnp.exp(scores - new_max[:, :, None])
        run_sum = run_sum * keep_part + jnp.sum(weights, axis=-1)
        prob_bf = weights.astype(jnp.bfloat16)
        accum = accum * keep_part[:, None, :] + jnp.einsum(
            "hqk,hkd->hdq", prob_bf, kv_block[1], preferred_element_type=jnp.float32
        )
        return (new_max, run_sum, accum)

    initial = (
        jnp.full((per_dev, query_count), -1e30, jnp.float32),
        jnp.zeros((per_dev, query_count), jnp.float32),
        jnp.zeros((per_dev, head_dim, query_count), jnp.float32),
    )
    piece = lax.all_gather(key_vals, "cols", axis=2, tiled=True)
    key_total = piece.shape[2] // head_dim
    if key_total > 1024 and key_total % 1024 == 0:
        block_len = 1024
    else:
        block_len = key_total
    block_count = key_total // block_len
    kv_blocks = piece.reshape(2, per_dev, block_count, block_len, head_dim).transpose(2, 0, 1, 3, 4)
    block_starts = jnp.arange(block_count, dtype=jnp.int32) * block_len

    def one_block(state, block_in):
        kv_block, key_start = block_in
        return (update(state, kv_block, key_start, block_len), None)

    state, _ = lax.scan(one_block, initial, (kv_blocks, block_starts))
    _, run_sum, accum = state
    head_out = (
        (accum / run_sum[:, None, :])
        .transpose(0, 2, 1)
        .astype(jnp.bfloat16)
        .reshape(per_dev, query_count * head_dim)
    )
    returned = lax.all_to_all(head_out, "rows", split_axis=1, concat_axis=0, tiled=True)
    global_out = (
        returned.reshape(head_count, atom_count, head_dim)
        .transpose(1, 0, 2)
        .reshape(atom_count, model_dim)
    )
    combined = (local_out.astype(jnp.float32) + global_out.astype(jnp.float32)).astype(jnp.bfloat16)
    updated = features.astype(jnp.float32) + jnp.dot(
        combined, w_out, preferred_element_type=jnp.float32
    )
    return updated.astype(jnp.bfloat16)


def mm(a, b, dims):
    return lax.dot_general(a, b, (dims, ((), ())), preferred_element_type=jnp.float32)


def parts_of(value, count):
    out = []
    for _ in range(count):
        part = value.astype(jnp.bfloat16)
        out.append(part)
        value = value - part.astype(jnp.float32)
    return out


def unit(rows, cols, dtype):
    r = lax.broadcasted_iota(jnp.int32, (rows, cols), 0)
    c = lax.broadcasted_iota(jnp.int32, (rows, cols), 1)
    return (r == c).astype(dtype)


def to_column(row):
    count = row.shape[1]
    r = lax.broadcasted_iota(jnp.int32, (count, count), 0)
    c = lax.broadcasted_iota(jnp.int32, (count, count), 1)
    return jnp.sum(jnp.where(r == c, jnp.broadcast_to(row, (count, count)), 0.0), axis=1, keepdims=True)


def fetch(pairs, sems):
    copies = [pltpu.make_async_copy(src, dst, sems.at[k]) for k, (src, dst) in enumerate(pairs)]
    for copy in copies:
        copy.start()
    return copies


def settle(copies):
    for copy in copies:
        copy.wait()


def pack_kernel(*refs):
    sources, out_ref, tables = refs[:7], refs[7], refs[8:12]
    feat_ref, gain_ref, pos_ref, tmp_ref, sems = refs[12:]
    copies = fetch(list(zip(sources, (feat_ref, gain_ref, pos_ref, *tables))), sems)
    settle(copies[:3])
    atoms, _ = feat_ref.shape
    floats = feat_ref[...].astype(jnp.float32)
    spread = jnp.mean(floats * floats, axis=-1, keepdims=True)
    normed = floats * lax.rsqrt(spread + 1e-06) * gain_ref[...]
    out_ref[:atoms, :] = normed.astype(jnp.bfloat16)
    tmp_ref[...] = jnp.zeros(tmp_ref.shape, jnp.float32)
    for p, part in enumerate(parts_of(pos_ref[...], 3)):
        tmp_ref[:3, p * 128 : p * 128 + atoms] = part.astype(jnp.float32)
    out_ref[atoms:, :] = tmp_ref[...].astype(jnp.bfloat16)
    settle(copies[3:])


def prepare(
    head_dim,
    wqkv_ref,
    rw_ref,
    ro_ref,
    pw_ref,
    cs_ref,
    pack_ref,
    qexp_ref,
    w1_ref,
    w2_ref,
    str_ref,
    own_ref,
):
    atoms = own_ref.shape[1]
    dim = wqkv_ref.shape[0]
    groups, rows, width = qexp_ref.shape
    per = rows // atoms
    tile = pack_ref[atoms:, :].astype(jnp.float32)
    tile = jnp.concatenate([tile[:, p * 128 : p * 128 + atoms] for p in range(3)], axis=0)
    pos = mm(unit(atoms, atoms, jnp.bfloat16), tile.astype(jnp.bfloat16), ((1,), (1,)))
    pos = jnp.concatenate([pos, jnp.zeros((atoms, 128 - 24), jnp.float32)], axis=1)
    pos = pos + pltpu.roll(pos, 120, 1) + pltpu.roll(pos, 112, 1)
    own_ref[0] = pos
    own_ref[1] = jnp.cos(two_pi * pos)
    own_ref[2] = jnp.sin(two_pi * pos)
    h, m, l = parts_of(0.5 * rw_ref[...], 3)
    hidden = rw_ref.shape[1]
    row = lax.broadcasted_iota(jnp.int32, (16, hidden), 0)
    tail = jnp.zeros((16, hidden), jnp.float32)
    for k, part in enumerate(parts_of(0.5 * ro_ref[...], 3)):
        tail = jnp.where(row == k, part.astype(jnp.float32), tail)
    stack = jnp.concatenate([h, h, m, h, l, m, tail.astype(jnp.bfloat16)], axis=0)
    w1_ref[...] = mm(unit(hidden, hidden, jnp.bfloat16), stack, ((1,), (1,))).astype(jnp.bfloat16)
    h, l = parts_of(log2_e * pw_ref[...], 2)
    w2_ref[...] = jnp.concatenate([h, h, l], axis=1)
    str_ref[...] = jnp.broadcast_to(to_column(log2_e * cs_ref[...]), str_ref.shape)
    q = mm(pack_ref[:atoms, :], wqkv_ref[:, :dim], ((1,), (0,)))
    q = q.astype(jnp.bfloat16).astype(jnp.float32)
    lane = lax.broadcasted_iota(jnp.int32, (per, width), 1) // head_dim
    sub = lax.broadcasted_iota(jnp.int32, (per, width), 0)
    keep = (lane == sub)[None]
    for g in range(groups):
        part = q[:, g * width : (g + 1) * width]
        spread = jnp.broadcast_to(part[:, None, :], (atoms, per, width))
        spread = jnp.where(keep, spread, 0.0).reshape(rows, width)
        qexp_ref[g] = spread.astype(jnp.bfloat16)


def position_tile(blocks, atoms, dim):
    tiles = [block[atoms:, :].astype(jnp.float32) for block in blocks]
    pad = 128 - atoms * len(blocks)
    out = []
    for p in range(3):
        part = [tile[:, p * 128 : p * 128 + atoms] for tile in tiles]
        if pad:
            part.append(jnp.zeros((8, pad), jnp.float32))
        out += part
    out.append(jnp.zeros((8, dim - 3 * 128), jnp.float32))
    return jnp.concatenate(out, axis=1).astype(jnp.bfloat16)


def repack_kernel(_, *refs):
    blocks, out_ref = refs[:-1], refs[-1]
    atoms = blocks[0].shape[0] - 8
    dim = out_ref.shape[1]
    for k, block in enumerate(blocks):
        out_ref[k * atoms : (k + 1) * atoms, :] = block[:atoms, :]
    out_ref[len(blocks) * atoms :, :] = position_tile(blocks, atoms, dim)


def piece_tiles(piece, counts):
    total = sum(counts)
    out = []
    for k in range(len(counts)):
        tail = piece[total + 8 * k : total + 8 * (k + 1), :].astype(jnp.float32)
        out.append(tail[:, :128] + tail[:, 128:256] + tail[:, 256:384])
    return out


def attend(qexp, keys, vals, scale, bias3):
    rows = qexp.shape[0]
    count = keys.shape[0]
    atoms, per, _ = bias3.shape
    s = mm(qexp, keys, ((1,), (1,))).reshape(atoms, per, count) * scale + bias3
    top = jnp.max(s, axis=-1, keepdims=True)
    p = jnp.exp2(s - top)
    total = jnp.sum(p, axis=-1, keepdims=True)
    o = mm(p.astype(jnp.bfloat16).reshape(rows, count), vals, ((1,), (0,)))
    return top, total, o.reshape(atoms, per, vals.shape[1])


def absorb(head_dim, plan, pieces, wqkv_ref, qexp_ref, str_ref, own_ref, kv_ref):
    dim = wqkv_ref.shape[0]
    atoms = own_ref.shape[1]
    groups, rows, width = qexp_ref.shape
    per = rows // atoms
    rows_in = jnp.concatenate(
        [piece[: sum(counts), :] for piece, (_, counts) in zip(pieces, plan)], axis=0
    )
    kv = mm(rows_in, wqkv_ref[:, dim:], ((1,), (0,))).astype(jnp.bfloat16)
    at = 0
    tiles = []
    for piece, (start, counts) in zip(pieces, plan):
        kv_ref[start : start + sum(counts), :] = kv[at : at + sum(counts)]
        at += sum(counts)
        tiles += [t[:, :n] for t, n in zip(piece_tiles(piece, counts), counts)]
    pos8 = jnp.concatenate(tiles, axis=1)
    cos_k, sin_k = jnp.cos(two_pi * pos8), jnp.sin(two_pi * pos8)
    waves = None
    for c in range(3):
        term = own_ref[1, :, c : c + 1] * cos_k[c : c + 1] + own_ref[2, :, c : c + 1] * sin_k[c : c + 1]
        waves = term if waves is None else waves + term
    out = []
    for g in range(groups):
        low, high = g * width, (g + 1) * width
        bias3 = str_ref[g * per : (g + 1) * per, :1][None] * waves[:, None, :]
        out.append(
            attend(
                qexp_ref[g],
                kv[:, low:high],
                kv[:, dim + low : dim + high],
                log2_e * head_dim ** (-0.5),
                bias3,
            )
        )
    return out


def widen(column, lanes):
    return jnp.broadcast_to(column, column.shape[:-1] + (lanes,))


def repeat_lanes(array, lanes):
    return jnp.concatenate([array] * (lanes // array.shape[-1]), axis=-1)


def core_kernel(*refs):
    blocks, ring_ref, core_ref = refs[:4], refs[4], refs[5]
    atoms = blocks[0].shape[0] - 8
    dim = core_ref.shape[1]
    four, three = 4 * atoms, 3 * atoms
    for k, block in enumerate(blocks):
        core_ref[k * atoms : (k + 1) * atoms, :] = block[:atoms, :]
    core_ref[four : four + three, :] = ring_ref[:three, :]
    core_ref[four + three : four + three + 8, :] = position_tile(blocks, atoms, dim)
    core_ref[four + three + 8 :, :] = ring_ref[three:, :]


def first_kernel(head_dim, plan, *refs):
    pack_ref, core_ref, wqkv_ref, tables = refs[0], refs[1], refs[2], refs[3:7]
    kv_ref, acc_ref, top_ref, sum_ref, qexp_ref, w1_ref, w2_ref, str_ref, own_ref = refs[7:]
    prepare(head_dim, wqkv_ref, *tables, pack_ref, qexp_ref, w1_ref, w2_ref, str_ref, own_ref)
    got = absorb(head_dim, plan, (core_ref,), wqkv_ref, qexp_ref, str_ref, own_ref, kv_ref)
    for g, (top, total, o) in enumerate(got):
        acc_ref[g] = o
        top_ref[g] = widen(top, 128)
        sum_ref[g] = widen(total, 128)


def merge(got, g, acc_ref, top_ref, sum_ref):
    top, total, o = got[g]
    width = o.shape[-1]
    best = jnp.maximum(widen(top, 128), top_ref[g])
    a, b = jnp.exp2(top_ref[g] - best), jnp.exp2(widen(top, 128) - best)
    summed = a * sum_ref[g] + b * widen(total, 128)
    acc = repeat_lanes(a, width) * acc_ref[g] + repeat_lanes(b, width) * o
    return best, summed, acc


def next_kernel(head_dim, plan, *refs):
    pieces = refs[: len(plan)]
    wqkv_ref, qexp_ref, str_ref, own_ref = refs[len(plan) : len(plan) + 4]
    _, acc_in, top_in, sum_in, kv_ref, acc_ref, top_ref, sum_ref = refs[len(plan) + 4 :]
    got = absorb(head_dim, plan, pieces, wqkv_ref, qexp_ref, str_ref, own_ref, kv_ref)
    for g in range(len(got)):
        best, summed, acc = merge(got, g, acc_in, top_in, sum_in)
        acc_ref[g] = acc
        top_ref[g] = best
        sum_ref[g] = summed


def chosen(row, lane):
    out = jnp.broadcast_to(row[:, :1], lane.shape)
    for e in range(1, row.shape[1]):
        out = jnp.where(lane == e, row[:, e : e + 1], out)
    return out


def last_kernel(head_dim, locate, plan, col_count, list_ref, valid_ref, shift_ref, cell_ref, *refs):
    piece_refs = refs[:8]
    (
        wqkv_ref,
        qexp_ref,
        str_ref,
        own_ref,
        w1_ref,
        w2_ref,
        wout_ref,
        in_ref,
        _,
        acc_in,
        top_in,
        sum_in,
        out_ref,
        kv_ref,
        near_ref,
        pos_ref,
        bias_ref,
    ) = refs[8:]
    dim = wqkv_ref.shape[0]
    atoms = own_ref.shape[1]
    groups, rows, width = qexp_ref.shape
    per = rows // atoms
    got = absorb(head_dim, plan[7:], piece_refs[7:], wqkv_ref, qexp_ref, str_ref, own_ref, kv_ref)
    at = 0
    for piece, (_, counts) in zip(piece_refs, plan):
        for tile in piece_tiles(piece, counts):
            pos_ref[at] = tile
            at += 1
    me = lax.axis_index("rows") * col_count + lax.axis_index("cols")
    entries = list_ref.shape[1]
    listed = entries * atoms
    lane = lax.broadcasted_iota(jnp.int32, (1, listed), 1) // atoms
    a_tile = 128 // atoms
    in_tile = lax.broadcasted_iota(jnp.int32, (1, 128), 1) // atoms
    tiles = []
    for e in range(entries):
        slot, tile, spot = locate(jnp.sum(list_ref[:, e : e + 1]) ^ me)
        start = pl.multiple_of(slot * atoms, atoms)
        near_ref[e * atoms : (e + 1) * atoms, :] = kv_ref[pl.ds(start, atoms), :]
        into = e % a_tile
        moved = pltpu.roll(pos_ref[tile], (into - spot + a_tile) % a_tile * atoms, 1)
        if into == 0:
            tiles.append(moved)
        else:
            tiles[-1] = jnp.where(in_tile == into, moved, tiles[-1])
    near = jnp.concatenate(tiles, axis=1)
    square = None
    for c in range(3):
        at = near[c : c + 1] + chosen(shift_ref[c].astype(jnp.float32), lane)
        gap = (at - own_ref[0, :, c : c + 1]) * cell_ref[:, c : c + 1]
        square = gap * gap if square is None else square + gap * gap
    dist = jnp.sqrt(square + 0.25)
    nrbf = (w1_ref.shape[1] - 16) // 6
    centers = lax.broadcasted_iota(jnp.int32, (nrbf, 1), 0).astype(jnp.float32) * rbf_step
    step = 16
    ones = jnp.ones((16, step * listed), jnp.bfloat16)
    for i in range(0, atoms, step):
        gap = jnp.concatenate([dist[j : j + 1] - centers for j in range(i, i + step)], axis=1)
        radial = jnp.exp(gap * gap * (-0.5 / rbf_width**2))
        h, m, l = parts_of(radial, 3)
        stack = jnp.concatenate([h, m, h, l, h, m, ones], axis=0)
        u = mm(w1_ref[...], stack, ((1,), (0,)))
        u = u + u * jnp.tanh(u)
        h, l = parts_of(u, 2)
        pair = mm(w2_ref[...], jnp.concatenate([h, l, h], axis=0), ((1,), (0,)))
        for j in range(step):
            for g in range(groups):
                bias_ref[g, i + j] = pair[g * per : (g + 1) * per, j * listed : (j + 1) * listed]
    live = (chosen(valid_ref[...], lane) > 0)[None]
    block = lax.broadcasted_iota(jnp.int32, (1, per, width), 2) // head_dim
    keep = block == lax.broadcasted_iota(jnp.int32, (1, per, width), 1)
    pieces = []
    for g in range(groups):
        low, high = g * width, (g + 1) * width
        _, summed, far = merge(got, g, acc_in, top_in, sum_in)
        far = far * repeat_lanes(1.0 / summed, width)
        far = jnp.sum(jnp.where(keep, far, 0.0), axis=1).astype(jnp.bfloat16)
        s = mm(qexp_ref[g], near_ref[:, low:high], ((1,), (1,)))
        s = s.reshape(atoms, per, listed) * (log2_e * head_dim ** (-0.5)) + bias_ref[g]
        s = jnp.where(live, s, -1e30)
        p = jnp.exp2(s - jnp.max(s, axis=-1, keepdims=True))
        summed = jnp.sum(p, axis=-1, keepdims=True)
        o = mm(
            p.astype(jnp.bfloat16).reshape(rows, listed),
            near_ref[:, dim + low : dim + high],
            ((1,), (0,)),
        )
        o = o.reshape(atoms, per, width) * (1.0 / summed)
        close = jnp.sum(jnp.where(keep, o, 0.0), axis=1).astype(jnp.bfloat16)
        pieces.append((close.astype(jnp.float32) + far.astype(jnp.float32)).astype(jnp.bfloat16))
    combined = jnp.concatenate(pieces, axis=1)
    moved = mm(combined, wout_ref[...], ((1,), (0,)))
    out_ref[...] = (in_ref[...].astype(jnp.float32) + moved).astype(jnp.bfloat16)


def call(kernel, outs, scratch, smem, args, aliases=None, hbm=0):
    vmem = pl.BlockSpec(memory_space=pltpu.VMEM)
    first = smem + hbm
    specs = [pl.BlockSpec(memory_space=pltpu.SMEM)] * smem
    specs += [pl.BlockSpec(memory_space=pltpu.HBM)] * hbm + [vmem] * (len(args) - first)
    placed = [pltpu.with_memory_space_constraint(a, pltpu.HBM) for a in args[smem:first]]
    placed += [pltpu.with_memory_space_constraint(a, pltpu.VMEM) for a in args[first:]]
    many = isinstance(outs, list)
    return pl.pallas_call(
        kernel,
        out_shape=outs,
        in_specs=specs,
        out_specs=[vmem] * len(outs) if many else vmem,
        scratch_shapes=scratch,
        input_output_aliases=aliases or {},
        compiler_params=pltpu.CompilerParams(vmem_limit_bytes=24 << 20),
    )(*args[:smem], *placed)


def on_device_small(
    features,
    positions,
    cell_lengths,
    block_lists,
    image_offsets,
    block_valid,
    norm_gain,
    w_qkv,
    w_out,
    rbf_weight,
    rbf_offset,
    pair_weight,
    cosine_scale,
):
    atoms, dim = features.shape
    heads = pair_weight.shape[1]
    hidden = pair_weight.shape[0]
    nrbf = rbf_weight.shape[0]
    head_dim = dim // heads
    row_count = lax.axis_size("rows")
    col_count = lax.axis_size("cols")
    total = row_count * col_count
    axes = ("rows", "cols")
    col_bits = col_count.bit_length() - 1
    flip = 1 << col_bits
    across_bits = (0, col_bits + 1)
    entries = block_lists.shape[1]
    width = 256
    per = width // head_dim
    groups = heads // per
    rows = atoms * per
    f32, bf16 = jnp.float32, jnp.bfloat16
    vm = pltpu.VMEM

    def swap(array, mask):
        return lax.ppermute(array, axes, [(i, i ^ mask) for i in range(total)])

    def locate(rel):
        up = (rel >> 1) & 3
        across = (rel & 1) + 2 * ((rel >> across_bits[1]) & 1)
        turn = (rel >> col_bits) & 1
        turn = turn ^ jnp.minimum(up, 1) ^ jnp.minimum(across, 1)
        far = jnp.minimum(up, 1)
        slot = turn * 16 + across + far * (3 + 2 * across + up)
        tile = turn * 5 + far * (1 + across)
        spot = across + far * (up - 1 - across)
        return slot, tile, spot

    tied = lax.optimization_barrier
    tables = (rbf_weight, rbf_offset[None], pair_weight.T, cosine_scale[None])
    pack, *tables = call(
        pack_kernel,
        [vm((atoms + 8, dim), bf16)] + [vm(table.shape, f32) for table in tables],
        [
            vm((atoms, dim), bf16),
            vm((1, dim), f32),
            vm(positions.shape, f32),
            vm((8, dim), f32),
            pltpu.SemaphoreType.DMA((7,)),
        ],
        0,
        (features, norm_gain[None], positions, *tables),
        hbm=7,
    )
    across_masks = {"e": 1 | flip, "n": (1 << across_bits[1]) | flip}
    across_masks["d"] = 1 | across_masks["n"]
    ups = [swap(pack, (d << 1) | flip) for d in (1, 2, 3)]
    owns = [swap(pack, mask) for mask in across_masks.values()]
    four, three = 4 * atoms, 3 * atoms
    ring = call(repack_kernel, vm((three + 8, dim), bf16), [], 0, (w_qkv, *ups), hbm=1)
    east, north, diag = [swap(ring, mask) for mask in across_masks.values()]
    state_shapes = [
        vm((total * atoms, 2 * dim), bf16),
        vm((groups, atoms, per, width), f32),
        vm((groups, atoms, per, 128), f32),
        vm((groups, atoms, per, 128), f32),
    ]
    half = total // 2 * atoms
    plan = [(0, (four, three))] + [(four + k * three, (three,)) for k in (1, 2, 3)]
    plan += [(half + start, counts) for start, counts in plan]

    core = call(core_kernel, vm((four + three + 16, dim), bf16), [], 0, (pack, *owns, ring))
    core2 = swap(core, flip)
    kv, acc, top, summed, qexp, w1, w2, strength, own = call(
        functools.partial(first_kernel, head_dim, plan[:1]),
        state_shapes
        + [
            vm((groups, rows, width), bf16),
            vm((hidden, 6 * nrbf + 16), bf16),
            vm((heads, 3 * hidden), bf16),
            vm((heads, 128), f32),
            vm((3, atoms, 128), f32),
        ],
        [],
        0,
        (pack, core, w_qkv, *tables),
    )
    state = (kv, acc, top, summed)
    common = (w_qkv, qexp, strength, own)

    def step(places, pieces, state):
        at = len(pieces) + len(common)
        return call(
            functools.partial(next_kernel, head_dim, [plan[k] for k in places]),
            state_shapes,
            [],
            0,
            (*pieces, *common, *state),
            {at + k: k for k in range(4)},
        )

    core2, state = tied((core2, state))
    state = step((4,), (core2,), state)
    east, north, state = tied((east, north, state))
    east2, north2 = swap(east, flip), swap(north, flip)
    state = step((1, 2), (east, north), state)
    diag, state = tied((diag, state))
    diag2 = swap(diag, flip)
    state = step((3, 5, 6), (diag, east2, north2), state)
    diag2, state = tied((diag2, state))
    updated, _ = call(
        functools.partial(last_kernel, head_dim, locate, plan, col_count),
        [jax.ShapeDtypeStruct((atoms, dim), bf16), state_shapes[0]],
        [
            vm((entries * atoms, 2 * dim), bf16),
            vm((10, 8, 128), f32),
            vm((groups, atoms, per, entries * atoms), f32),
        ],
        0,
        (
            block_lists,
            block_valid,
            image_offsets,
            cell_lengths[None],
            core,
            east,
            north,
            diag,
            core2,
            east2,
            north2,
            diag2,
            *common,
            w1,
            w2,
            w_out,
            features,
            *state,
        ),
        {4 + 8 + len(common) + 4: 1},
    )
    return updated


def solution(mesh):
    row_count, col_count = mesh.shape["rows"], mesh.shape["cols"]
    small = (row_count, col_count) == (4, 8)
    body = on_device_small if small else on_device
    return jax.shard_map(
        body,
        mesh=mesh,
        in_specs=(
            P(("rows", "cols"), None),
            P(None, ("rows", "cols")),
            P(),
            P(("rows", "cols"), None),
            P(None, ("rows", "cols"), None),
            P(("rows", "cols"), None),
            P(),
            P(),
            P(),
            P(),
            P(),
            P(),
            P(),
        ),
        out_specs=P(("rows", "cols"), None),
        check_vma=False,
    )
```

```python
import functools
import math

import jax
import jax.numpy as jnp
from jax import lax
from jax.experimental import pallas as pl
from jax.experimental.pallas import tpu as pltpu
from jax.sharding import PartitionSpec as P


rbf_step = 2.0
rbf_width = 2.0
two_pi = 2.0 * math.pi
highest = lax.Precision.HIGHEST


def with_halo(cells, sides, width):
    for axis, dim in sides:
        count = lax.axis_size(axis)
        head = lax.slice_in_dim(cells, 0, width, axis=dim)
        tail = lax.slice_in_dim(cells, cells.shape[dim] - width, cells.shape[dim], axis=dim)
        cells = jnp.concatenate(
            [
                lax.ppermute(tail, axis, [(i, (i + 1) % count) for i in range(count)]),
                cells,
                lax.ppermute(head, axis, [((i + 1) % count, i) for i in range(count)]),
            ],
            axis=dim,
        )
    return cells


def rms_rows(values, norm_gain):
    floats = values.astype(jnp.float32)
    spread = jnp.mean(floats * floats, axis=-1, keepdims=True)
    return (floats * lax.rsqrt(spread + 1e-06) * norm_gain).astype(jnp.bfloat16)


def near_attention(
    query_rows,
    own_pos,
    keys,
    key_pos,
    shifts,
    live,
    cell_lengths,
    rbf_weight,
    rbf_offset,
    pair_weight,
):
    entries, block_len = (keys.shape[0], keys.shape[1])
    model_dim = query_rows.shape[1]
    head_count = pair_weight.shape[1]
    head_dim = model_dim // head_count
    key_coords = key_pos.transpose(1, 0, 2) + shifts.astype(jnp.float32)[:, :, None]
    key_coords = key_coords.reshape(3, entries * block_len)
    displace = (key_coords[:, None, :] - own_pos[:, :, None]) * cell_lengths[:, None, None]
    distance = jnp.sqrt(jnp.sum(displace * displace, axis=0) + 0.25)
    centers = jnp.arange(rbf_weight.shape[0], dtype=jnp.float32) * rbf_step
    radial = jnp.exp(-((distance[None] - centers[:, None, None]) ** 2) * (0.5 / rbf_width**2))
    radial = radial.reshape(rbf_weight.shape[0], -1)
    hidden = jax.nn.silu(jnp.dot(rbf_weight.T, radial, precision=highest) + rbf_offset[:, None])
    pair_bias = jnp.dot(pair_weight.T, hidden, precision=highest).reshape(
        head_count, query_rows.shape[0], entries * block_len
    )
    query_heads = query_rows.reshape(-1, head_count, head_dim)
    key_heads = keys[:, :, :model_dim].reshape(entries * block_len, head_count, head_dim)
    value_heads = keys[:, :, model_dim:].reshape(entries * block_len, head_count, head_dim)
    scores = (
        jnp.einsum("ahd,khd->hak", query_heads, key_heads, preferred_element_type=jnp.float32)
        * head_dim ** (-0.5)
        + pair_bias
    )
    allowed = jnp.repeat(live > 0, block_len)
    scores = jnp.where(allowed[None, None, :], scores, -1e30)
    row_max = jnp.max(scores, axis=-1, keepdims=True)
    weights = jnp.exp(scores - row_max)
    row_sum = jnp.sum(weights, axis=-1, keepdims=True)
    prob_bf = weights.astype(jnp.bfloat16)
    attended = jnp.einsum(
        "hak,khd->ahd", prob_bf, value_heads, preferred_element_type=jnp.float32
    ) / row_sum.transpose(1, 0, 2)
    return attended.reshape(-1, model_dim).astype(jnp.bfloat16)


def on_device(
    features,
    positions,
    cell_lengths,
    block_lists,
    image_offsets,
    block_valid,
    norm_gain,
    w_qkv,
    w_out,
    rbf_weight,
    rbf_offset,
    pair_weight,
    cosine_scale,
):
    atom_count, model_dim = features.shape
    head_count = pair_weight.shape[1]
    head_dim = model_dim // head_count
    row_count = lax.axis_size("rows")
    col_count = lax.axis_size("cols")
    row_index = lax.axis_index("rows")
    col_index = lax.axis_index("cols")
    per_dev = head_count // row_count
    normed = rms_rows(features, norm_gain)
    packed = jnp.dot(normed, w_qkv, preferred_element_type=jnp.float32).astype(jnp.bfloat16)
    every_pos = lax.all_gather(positions, ("rows", "cols"), axis=1, tiled=True)
    near_rows = with_halo(normed[None, None], (("rows", 0), ("cols", 1)), 1)
    near_kv = jnp.dot(
        near_rows.reshape(9 * atom_count, model_dim),
        w_qkv[:, model_dim:],
        preferred_element_type=jnp.float32,
    )
    near_kv = near_kv.astype(jnp.bfloat16).reshape(9, atom_count, 2 * model_dim)
    listed = block_lists[0]
    list_row = listed // col_count
    list_col = listed % col_count
    slots = (list_row - row_index + 1) % row_count * 3 + (list_col - col_index + 1) % col_count
    keys = jnp.take(near_kv, slots, axis=0)
    block_pos = every_pos.reshape(3, row_count * col_count, atom_count)
    key_pos = jnp.take(block_pos, listed, axis=1).transpose(1, 0, 2)
    local_out = near_attention(
        packed[:, :model_dim],
        positions,
        keys,
        key_pos,
        image_offsets[:, 0, :],
        block_valid[0],
        cell_lengths,
        rbf_weight,
        rbf_offset,
        pair_weight,
    )
    grouped = (
        packed.reshape(atom_count, 3, head_count, head_dim)
        .transpose(1, 2, 0, 3)
        .reshape(3, head_count, atom_count * head_dim)
    )
    regrouped = lax.all_to_all(grouped, "rows", split_axis=1, concat_axis=2, tiled=True)
    query_count = row_count * atom_count
    queries = regrouped[0].reshape(per_dev, query_count, head_dim)
    key_vals = regrouped[1:]
    cycle_pos = (
        every_pos.reshape(3, row_count, col_count, atom_count).transpose(0, 2, 1, 3).reshape(3, -1)
    )
    query_pos = lax.dynamic_slice_in_dim(cycle_pos, col_index * query_count, query_count, 1)
    cycle_feats = jnp.concatenate(
        [jnp.cos(two_pi * cycle_pos), jnp.sin(two_pi * cycle_pos)], axis=0
    )
    query_feats = jnp.concatenate(
        [jnp.cos(two_pi * query_pos), jnp.sin(two_pi * query_pos)], axis=0
    )
    strengths = lax.dynamic_slice_in_dim(cosine_scale, row_index * per_dev, per_dev)
    scale = head_dim ** (-0.5)

    def update(state, kv_block, key_start, block_len):
        run_max, run_sum, accum = state
        scores = (
            jnp.einsum("hqd,hkd->hqk", queries, kv_block[0], preferred_element_type=jnp.float32)
            * scale
        )
        coords = lax.dynamic_slice_in_dim(cycle_feats, key_start, block_len, 1)
        cos_bias = jnp.dot(query_feats.T, coords, precision=highest)
        scores = scores + strengths[:, None, None] * cos_bias[None]
        new_max = jnp.maximum(run_max, jnp.max(scores, axis=-1))
        keep_part = jnp.exp(run_max - new_max)
        weights = jnp.exp(scores - new_max[:, :, None])
        run_sum = run_sum * keep_part + jnp.sum(weights, axis=-1)
        prob_bf = weights.astype(jnp.bfloat16)
        accum = accum * keep_part[:, None, :] + jnp.einsum(
            "hqk,hkd->hdq", prob_bf, kv_block[1], preferred_element_type=jnp.float32
        )
        return (new_max, run_sum, accum)

    initial = (
        jnp.full((per_dev, query_count), -1e30, jnp.float32),
        jnp.zeros((per_dev, query_count), jnp.float32),
        jnp.zeros((per_dev, head_dim, query_count), jnp.float32),
    )
    piece = lax.all_gather(key_vals, "cols", axis=2, tiled=True)
    key_total = piece.shape[2] // head_dim
    if key_total > 1024 and key_total % 1024 == 0:
        block_len = 1024
    else:
        block_len = key_total
    block_count = key_total // block_len
    kv_blocks = piece.reshape(2, per_dev, block_count, block_len, head_dim).transpose(2, 0, 1, 3, 4)
    block_starts = jnp.arange(block_count, dtype=jnp.int32) * block_len

    def one_block(state, block_in):
        kv_block, key_start = block_in
        return (update(state, kv_block, key_start, block_len), None)

    state, _ = lax.scan(one_block, initial, (kv_blocks, block_starts))
    _, run_sum, accum = state
    head_out = (
        (accum / run_sum[:, None, :])
        .transpose(0, 2, 1)
        .astype(jnp.bfloat16)
        .reshape(per_dev, query_count * head_dim)
    )
    returned = lax.all_to_all(head_out, "rows", split_axis=1, concat_axis=0, tiled=True)
    global_out = (
        returned.reshape(head_count, atom_count, head_dim)
        .transpose(1, 0, 2)
        .reshape(atom_count, model_dim)
    )
    combined = (local_out.astype(jnp.float32) + global_out.astype(jnp.float32)).astype(jnp.bfloat16)
    updated = features.astype(jnp.float32) + jnp.dot(
        combined, w_out, preferred_element_type=jnp.float32
    )
    return updated.astype(jnp.bfloat16)


def mm(a, b, dims):
    return lax.dot_general(a, b, (dims, ((), ())), preferred_element_type=jnp.float32)


def parts_of(value, count):
    out = []
    for _ in range(count):
        part = value.astype(jnp.bfloat16)
        out.append(part)
        value = value - part.astype(jnp.float32)
    return out


def unit(rows, cols, dtype):
    r = lax.broadcasted_iota(jnp.int32, (rows, cols), 0)
    c = lax.broadcasted_iota(jnp.int32, (rows, cols), 1)
    return (r == c).astype(dtype)


def to_column(row):
    count = row.shape[1]
    r = lax.broadcasted_iota(jnp.int32, (count, count), 0)
    c = lax.broadcasted_iota(jnp.int32, (count, count), 1)
    return jnp.sum(jnp.where(r == c, jnp.broadcast_to(row, (count, count)), 0.0), axis=1, keepdims=True)


def fetch(pairs, sems):
    copies = [pltpu.make_async_copy(src, dst, sems.at[k]) for k, (src, dst) in enumerate(pairs)]
    for copy in copies:
        copy.start()
    return copies


def settle(copies):
    for copy in copies:
        copy.wait()


def pack_kernel(*refs):
    sources, out_ref, tables = refs[:7], refs[7], refs[8:12]
    feat_ref, gain_ref, pos_ref, tmp_ref, sems = refs[12:]
    copies = fetch(list(zip(sources, (feat_ref, gain_ref, pos_ref, *tables))), sems)
    settle(copies[:3])
    atoms, _ = feat_ref.shape
    floats = feat_ref[...].astype(jnp.float32)
    spread = jnp.mean(floats * floats, axis=-1, keepdims=True)
    normed = floats * lax.rsqrt(spread + 1e-06) * gain_ref[...]
    out_ref[:atoms, :] = normed.astype(jnp.bfloat16)
    tmp_ref[...] = jnp.zeros(tmp_ref.shape, jnp.float32)
    for p, part in enumerate(parts_of(pos_ref[...], 3)):
        tmp_ref[:3, p * 128 : p * 128 + atoms] = part.astype(jnp.float32)
    out_ref[atoms:, :] = tmp_ref[...].astype(jnp.bfloat16)
    settle(copies[3:])


def prepare(
    head_dim,
    wqkv_ref,
    rw_ref,
    ro_ref,
    pw_ref,
    cs_ref,
    pack_ref,
    qexp_ref,
    w1_ref,
    w2_ref,
    str_ref,
    own_ref,
):
    atoms = own_ref.shape[1]
    dim = wqkv_ref.shape[0]
    groups, rows, width = qexp_ref.shape
    per = rows // atoms
    tile = pack_ref[atoms:, :].astype(jnp.float32)
    tile = jnp.concatenate([tile[:, p * 128 : p * 128 + atoms] for p in range(3)], axis=0)
    pos = mm(unit(atoms, atoms, jnp.bfloat16), tile.astype(jnp.bfloat16), ((1,), (1,)))
    pos = jnp.concatenate([pos, jnp.zeros((atoms, 128 - 24), jnp.float32)], axis=1)
    pos = pos + pltpu.roll(pos, 120, 1) + pltpu.roll(pos, 112, 1)
    own_ref[0] = pos
    own_ref[1] = jnp.cos(two_pi * pos)
    own_ref[2] = jnp.sin(two_pi * pos)
    h, m, l = parts_of(0.5 * rw_ref[...], 3)
    hidden = rw_ref.shape[1]
    row = lax.broadcasted_iota(jnp.int32, (16, hidden), 0)
    tail = jnp.zeros((16, hidden), jnp.float32)
    for k, part in enumerate(parts_of(0.5 * ro_ref[...], 3)):
        tail = jnp.where(row == k, part.astype(jnp.float32), tail)
    stack = jnp.concatenate([h, h, m, h, l, m, tail.astype(jnp.bfloat16)], axis=0)
    w1_ref[...] = mm(unit(hidden, hidden, jnp.bfloat16), stack, ((1,), (1,))).astype(jnp.bfloat16)
    h, l = parts_of(pw_ref[...], 2)
    w2_ref[...] = jnp.concatenate([h, h, l], axis=1)
    str_ref[...] = jnp.broadcast_to(to_column(cs_ref[...]), str_ref.shape)
    q = mm(pack_ref[:atoms, :], wqkv_ref[:, :dim], ((1,), (0,)))
    q = q.astype(jnp.bfloat16).astype(jnp.float32)
    lane = lax.broadcasted_iota(jnp.int32, (per, width), 1) // head_dim
    sub = lax.broadcasted_iota(jnp.int32, (per, width), 0)
    keep = (lane == sub)[None]
    for g in range(groups):
        part = q[:, g * width : (g + 1) * width]
        spread = jnp.broadcast_to(part[:, None, :], (atoms, per, width))
        spread = jnp.where(keep, spread, 0.0).reshape(rows, width)
        qexp_ref[g] = spread.astype(jnp.bfloat16)


def position_tile(blocks, atoms, dim):
    tiles = [block[atoms:, :].astype(jnp.float32) for block in blocks]
    pad = 128 - atoms * len(blocks)
    out = []
    for p in range(3):
        part = [tile[:, p * 128 : p * 128 + atoms] for tile in tiles]
        if pad:
            part.append(jnp.zeros((8, pad), jnp.float32))
        out += part
    out.append(jnp.zeros((8, dim - 3 * 128), jnp.float32))
    return jnp.concatenate(out, axis=1).astype(jnp.bfloat16)


def repack_kernel(_, *refs):
    blocks, out_ref = refs[:-1], refs[-1]
    atoms = blocks[0].shape[0] - 8
    dim = out_ref.shape[1]
    for k, block in enumerate(blocks):
        out_ref[k * atoms : (k + 1) * atoms, :] = block[:atoms, :]
    out_ref[len(blocks) * atoms :, :] = position_tile(blocks, atoms, dim)


def piece_tiles(piece, counts):
    total = sum(counts)
    out = []
    for k in range(len(counts)):
        tail = piece[total + 8 * k : total + 8 * (k + 1), :].astype(jnp.float32)
        out.append(tail[:, :128] + tail[:, 128:256] + tail[:, 256:384])
    return out


def attend(qexps, keys, vals, scale, biases):
    rows = qexps[0].shape[0]
    count = keys[0].shape[0]
    atoms, per, _ = biases[0].shape
    scores = [mm(q, k, ((1,), (1,))) for q, k in zip(qexps, keys)]
    tops, sums, probs = [], [], []
    for s, bias3 in zip(scores, biases):
        s = s.reshape(atoms, per, count) * scale + bias3
        tops.append(jnp.max(s, axis=-1, keepdims=True))
        p = jnp.exp(s - tops[-1])
        sums.append(jnp.sum(p, axis=-1, keepdims=True))
        probs.append(p.astype(jnp.bfloat16).reshape(rows, count))
    outs = [mm(p, v, ((1,), (0,))) for p, v in zip(probs, vals)]
    return [(t, n, o.reshape(atoms, per, o.shape[-1])) for t, n, o in zip(tops, sums, outs)]


def absorb(head_dim, plan, pieces, wqkv_ref, qexp_ref, str_ref, own_ref, kv_ref):
    dim = wqkv_ref.shape[0]
    atoms = own_ref.shape[1]
    groups, rows, width = qexp_ref.shape
    per = rows // atoms
    rows_in = jnp.concatenate(
        [piece[: sum(counts), :] for piece, (_, counts) in zip(pieces, plan)], axis=0
    )
    kv = mm(rows_in, wqkv_ref[:, dim:], ((1,), (0,))).astype(jnp.bfloat16)
    at = 0
    tiles = []
    for piece, (start, counts) in zip(pieces, plan):
        kv_ref[start : start + sum(counts), :] = kv[at : at + sum(counts)]
        at += sum(counts)
        tiles += [t[:, :n] for t, n in zip(piece_tiles(piece, counts), counts)]
    pos8 = jnp.concatenate(tiles, axis=1)
    cos_k, sin_k = jnp.cos(two_pi * pos8), jnp.sin(two_pi * pos8)
    waves = None
    for c in range(3):
        term = own_ref[1, :, c : c + 1] * cos_k[c : c + 1] + own_ref[2, :, c : c + 1] * sin_k[c : c + 1]
        waves = term if waves is None else waves + term
    spans = [(g * width, (g + 1) * width) for g in range(groups)]
    return attend(
        [qexp_ref[g] for g in range(groups)],
        [kv[:, low:high] for low, high in spans],
        [kv[:, dim + low : dim + high] for low, high in spans],
        head_dim ** (-0.5),
        [
            str_ref[g * per : (g + 1) * per, :1][None] * waves[:, None, :]
            for g in range(groups)
        ],
    )


def widen(column, lanes):
    return jnp.broadcast_to(column, column.shape[:-1] + (lanes,))


def repeat_lanes(array, lanes):
    return jnp.concatenate([array] * (lanes // array.shape[-1]), axis=-1)


def core_kernel(*refs):
    blocks, ring_ref, core_ref = refs[:4], refs[4], refs[5]
    atoms = blocks[0].shape[0] - 8
    dim = core_ref.shape[1]
    four, three = 4 * atoms, 3 * atoms
    for k, block in enumerate(blocks):
        core_ref[k * atoms : (k + 1) * atoms, :] = block[:atoms, :]
    core_ref[four : four + three, :] = ring_ref[:three, :]
    core_ref[four + three : four + three + 8, :] = position_tile(blocks, atoms, dim)
    core_ref[four + three + 8 :, :] = ring_ref[three:, :]


def first_kernel(head_dim, plan, *refs):
    pack_ref, core_ref, wqkv_ref, tables = refs[0], refs[1], refs[2], refs[3:7]
    kv_ref, acc_ref, top_ref, sum_ref, qexp_ref, w1_ref, w2_ref, str_ref, own_ref = refs[7:]
    prepare(head_dim, wqkv_ref, *tables, pack_ref, qexp_ref, w1_ref, w2_ref, str_ref, own_ref)
    got = absorb(head_dim, plan, (core_ref,), wqkv_ref, qexp_ref, str_ref, own_ref, kv_ref)
    for g, (top, total, o) in enumerate(got):
        acc_ref[g] = o
        top_ref[g] = widen(top, 128)
        sum_ref[g] = widen(total, 128)


def merge(got, g, acc_ref, top_ref, sum_ref):
    top, total, o = got[g]
    width = o.shape[-1]
    best = jnp.maximum(widen(top, 128), top_ref[g])
    a, b = jnp.exp(top_ref[g] - best), jnp.exp(widen(top, 128) - best)
    summed = a * sum_ref[g] + b * widen(total, 128)
    acc = repeat_lanes(a, width) * acc_ref[g] + repeat_lanes(b, width) * o
    return best, summed, acc


def next_kernel(head_dim, plan, *refs):
    pieces = refs[: len(plan)]
    wqkv_ref, qexp_ref, str_ref, own_ref = refs[len(plan) : len(plan) + 4]
    _, acc_in, top_in, sum_in, kv_ref, acc_ref, top_ref, sum_ref = refs[len(plan) + 4 :]
    got = absorb(head_dim, plan, pieces, wqkv_ref, qexp_ref, str_ref, own_ref, kv_ref)
    for g in range(len(got)):
        best, summed, acc = merge(got, g, acc_in, top_in, sum_in)
        acc_ref[g] = acc
        top_ref[g] = best
        sum_ref[g] = summed


def chosen(row, lane):
    out = jnp.broadcast_to(row[:, :1], lane.shape)
    for e in range(1, row.shape[1]):
        out = jnp.where(lane == e, row[:, e : e + 1], out)
    return out


def last_kernel(head_dim, locate, plan, col_count, list_ref, valid_ref, shift_ref, cell_ref, *refs):
    piece_refs = refs[:8]
    (
        wqkv_ref,
        qexp_ref,
        str_ref,
        own_ref,
        w1_ref,
        w2_ref,
        wout_ref,
        in_ref,
        _,
        acc_in,
        top_in,
        sum_in,
        out_ref,
        kv_ref,
        near_ref,
        pos_ref,
        bias_ref,
    ) = refs[8:]
    dim = wqkv_ref.shape[0]
    atoms = own_ref.shape[1]
    groups, rows, width = qexp_ref.shape
    per = rows // atoms
    got = absorb(head_dim, plan[7:], piece_refs[7:], wqkv_ref, qexp_ref, str_ref, own_ref, kv_ref)
    at = 0
    for piece, (_, counts) in zip(piece_refs, plan):
        for tile in piece_tiles(piece, counts):
            pos_ref[at] = tile
            at += 1
    me = lax.axis_index("rows") * col_count + lax.axis_index("cols")
    entries = list_ref.shape[1]
    listed = entries * atoms
    lane = lax.broadcasted_iota(jnp.int32, (1, listed), 1) // atoms
    a_tile = 128 // atoms
    in_tile = lax.broadcasted_iota(jnp.int32, (1, 128), 1) // atoms
    tiles = []
    for e in range(entries):
        slot, tile, spot = locate(jnp.sum(list_ref[:, e : e + 1]) ^ me)
        start = pl.multiple_of(slot * atoms, atoms)
        near_ref[e * atoms : (e + 1) * atoms, :] = kv_ref[pl.ds(start, atoms), :]
        into = e % a_tile
        moved = pltpu.roll(pos_ref[tile], (into - spot + a_tile) % a_tile * atoms, 1)
        if into == 0:
            tiles.append(moved)
        else:
            tiles[-1] = jnp.where(in_tile == into, moved, tiles[-1])
    near = jnp.concatenate(tiles, axis=1)
    square = None
    for c in range(3):
        at = near[c : c + 1] + chosen(shift_ref[c].astype(jnp.float32), lane)
        gap = (at - own_ref[0, :, c : c + 1]) * cell_ref[:, c : c + 1]
        square = gap * gap if square is None else square + gap * gap
    dist = jnp.sqrt(square + 0.25)
    nrbf = (w1_ref.shape[1] - 16) // 6
    centers = lax.broadcasted_iota(jnp.int32, (nrbf, 1), 0).astype(jnp.float32) * rbf_step
    step = 16
    ones = jnp.ones((16, step * listed), jnp.bfloat16)
    for i in range(0, atoms, step):
        gap = jnp.concatenate([dist[j : j + 1] - centers for j in range(i, i + step)], axis=1)
        radial = jnp.exp(gap * gap * (-0.5 / rbf_width**2))
        h, m, l = parts_of(radial, 3)
        stack = jnp.concatenate([h, m, h, l, h, m, ones], axis=0)
        u = mm(w1_ref[...], stack, ((1,), (0,)))
        u = u + u * jnp.tanh(u)
        h, l = parts_of(u, 2)
        pair = mm(w2_ref[...], jnp.concatenate([h, l, h], axis=0), ((1,), (0,)))
        for j in range(step):
            for g in range(groups):
                bias_ref[g, i + j] = pair[g * per : (g + 1) * per, j * listed : (j + 1) * listed]
    live = (chosen(valid_ref[...], lane) > 0)[None]
    block = lax.broadcasted_iota(jnp.int32, (1, per, width), 2) // head_dim
    keep = block == lax.broadcasted_iota(jnp.int32, (1, per, width), 1)
    spans = [(g * width, (g + 1) * width) for g in range(groups)]
    scores = [mm(qexp_ref[g], near_ref[:, low:high], ((1,), (1,))) for g, (low, high) in enumerate(spans)]
    fars = []
    for g in range(groups):
        _, summed, far = merge(got, g, acc_in, top_in, sum_in)
        far = far * repeat_lanes(1.0 / summed, width)
        fars.append(jnp.sum(jnp.where(keep, far, 0.0), axis=1).astype(jnp.bfloat16))
    probs, sums = [], []
    for g in range(groups):
        s = scores[g].reshape(atoms, per, listed) * head_dim ** (-0.5) + bias_ref[g]
        s = jnp.where(live, s, -1e30)
        p = jnp.exp(s - jnp.max(s, axis=-1, keepdims=True))
        sums.append(1.0 / jnp.sum(p, axis=-1, keepdims=True))
        probs.append(p.astype(jnp.bfloat16).reshape(rows, listed))
    outs = [mm(probs[g], near_ref[:, dim + low : dim + high], ((1,), (0,))) for g, (low, high) in enumerate(spans)]
    pieces = []
    for g in range(groups):
        o = outs[g].reshape(atoms, per, width) * sums[g]
        close = jnp.sum(jnp.where(keep, o, 0.0), axis=1).astype(jnp.bfloat16)
        pieces.append((close.astype(jnp.float32) + fars[g].astype(jnp.float32)).astype(jnp.bfloat16))
    combined = jnp.concatenate(pieces, axis=1)
    moved = mm(combined, wout_ref[...], ((1,), (0,)))
    out_ref[...] = (in_ref[...].astype(jnp.float32) + moved).astype(jnp.bfloat16)


def call(kernel, outs, scratch, smem, args, aliases=None, hbm=0):
    vmem = pl.BlockSpec(memory_space=pltpu.VMEM)
    first = smem + hbm
    specs = [pl.BlockSpec(memory_space=pltpu.SMEM)] * smem
    specs += [pl.BlockSpec(memory_space=pltpu.HBM)] * hbm + [vmem] * (len(args) - first)
    placed = [pltpu.with_memory_space_constraint(a, pltpu.HBM) for a in args[smem:first]]
    placed += [pltpu.with_memory_space_constraint(a, pltpu.VMEM) for a in args[first:]]
    many = isinstance(outs, list)
    return pl.pallas_call(
        kernel,
        out_shape=outs,
        in_specs=specs,
        out_specs=[vmem] * len(outs) if many else vmem,
        scratch_shapes=scratch,
        input_output_aliases=aliases or {},
        compiler_params=pltpu.CompilerParams(vmem_limit_bytes=24 << 20),
    )(*args[:smem], *placed)


def on_device_small(
    features,
    positions,
    cell_lengths,
    block_lists,
    image_offsets,
    block_valid,
    norm_gain,
    w_qkv,
    w_out,
    rbf_weight,
    rbf_offset,
    pair_weight,
    cosine_scale,
):
    atoms, dim = features.shape
    heads = pair_weight.shape[1]
    hidden = pair_weight.shape[0]
    nrbf = rbf_weight.shape[0]
    head_dim = dim // heads
    row_count = lax.axis_size("rows")
    col_count = lax.axis_size("cols")
    total = row_count * col_count
    axes = ("rows", "cols")
    col_bits = col_count.bit_length() - 1
    flip = 1 << col_bits
    across_bits = (0, col_bits + 1)
    entries = block_lists.shape[1]
    width = 256
    per = width // head_dim
    groups = heads // per
    rows = atoms * per
    f32, bf16 = jnp.float32, jnp.bfloat16
    vm = pltpu.VMEM

    def swap(array, mask):
        return lax.ppermute(array, axes, [(i, i ^ mask) for i in range(total)])

    def locate(rel):
        up = (rel >> 1) & 3
        across = (rel & 1) + 2 * ((rel >> across_bits[1]) & 1)
        turn = (rel >> col_bits) & 1
        turn = turn ^ jnp.minimum(up, 1) ^ jnp.minimum(across, 1)
        far = jnp.minimum(up, 1)
        slot = turn * 16 + across + far * (3 + 2 * across + up)
        tile = turn * 5 + far * (1 + across)
        spot = across + far * (up - 1 - across)
        return slot, tile, spot

    tied = lax.optimization_barrier
    tables = (rbf_weight, rbf_offset[None], pair_weight.T, cosine_scale[None])
    pack, *tables = call(
        pack_kernel,
        [vm((atoms + 8, dim), bf16)] + [vm(table.shape, f32) for table in tables],
        [
            vm((atoms, dim), bf16),
            vm((1, dim), f32),
            vm(positions.shape, f32),
            vm((8, dim), f32),
            pltpu.SemaphoreType.DMA((7,)),
        ],
        0,
        (features, norm_gain[None], positions, *tables),
        hbm=7,
    )
    across_masks = {"e": 1 | flip, "n": (1 << across_bits[1]) | flip}
    across_masks["d"] = 1 | across_masks["n"]
    ups = [swap(pack, (d << 1) | flip) for d in (1, 2, 3)]
    owns = [swap(pack, mask) for mask in across_masks.values()]
    four, three = 4 * atoms, 3 * atoms
    ring = call(repack_kernel, vm((three + 8, dim), bf16), [], 0, (w_qkv, *ups), hbm=1)
    east, north, diag = [swap(ring, mask) for mask in across_masks.values()]
    state_shapes = [
        vm((total * atoms, 2 * dim), bf16),
        vm((groups, atoms, per, width), f32),
        vm((groups, atoms, per, 128), f32),
        vm((groups, atoms, per, 128), f32),
    ]
    half = total // 2 * atoms
    plan = [(0, (four, three))] + [(four + k * three, (three,)) for k in (1, 2, 3)]
    plan += [(half + start, counts) for start, counts in plan]

    core = call(core_kernel, vm((four + three + 16, dim), bf16), [], 0, (pack, *owns, ring))
    core2 = swap(core, flip)
    kv, acc, top, summed, qexp, w1, w2, strength, own = call(
        functools.partial(first_kernel, head_dim, plan[:1]),
        state_shapes
        + [
            vm((groups, rows, width), bf16),
            vm((hidden, 6 * nrbf + 16), bf16),
            vm((heads, 3 * hidden), bf16),
            vm((heads, 128), f32),
            vm((3, atoms, 128), f32),
        ],
        [],
        0,
        (pack, core, w_qkv, *tables),
    )
    state = (kv, acc, top, summed)
    common = (w_qkv, qexp, strength, own)

    def step(places, pieces, state):
        at = len(pieces) + len(common)
        return call(
            functools.partial(next_kernel, head_dim, [plan[k] for k in places]),
            state_shapes,
            [],
            0,
            (*pieces, *common, *state),
            {at + k: k for k in range(4)},
        )

    core2, state = tied((core2, state))
    state = step((4,), (core2,), state)
    east, north, state = tied((east, north, state))
    east2, north2 = swap(east, flip), swap(north, flip)
    state = step((1, 2), (east, north), state)
    diag, state = tied((diag, state))
    diag2 = swap(diag, flip)
    state = step((3, 5, 6), (diag, east2, north2), state)
    diag2, state = tied((diag2, state))
    updated, _ = call(
        functools.partial(last_kernel, head_dim, locate, plan, col_count),
        [jax.ShapeDtypeStruct((atoms, dim), bf16), state_shapes[0]],
        [
            vm((entries * atoms, 2 * dim), bf16),
            vm((10, 8, 128), f32),
            vm((groups, atoms, per, entries * atoms), f32),
        ],
        0,
        (
            block_lists,
            block_valid,
            image_offsets,
            cell_lengths[None],
            core,
            east,
            north,
            diag,
            core2,
            east2,
            north2,
            diag2,
            *common,
            w1,
            w2,
            w_out,
            features,
            *state,
        ),
        {4 + 8 + len(common) + 4: 1},
    )
    return updated


def solution(mesh):
    row_count, col_count = mesh.shape["rows"], mesh.shape["cols"]
    small = (row_count, col_count) == (4, 8)
    body = on_device_small if small else on_device
    return jax.shard_map(
        body,
        mesh=mesh,
        in_specs=(
            P(("rows", "cols"), None),
            P(None, ("rows", "cols")),
            P(),
            P(("rows", "cols"), None),
            P(None, ("rows", "cols"), None),
            P(("rows", "cols"), None),
            P(),
            P(),
            P(),
            P(),
            P(),
            P(),
            P(),
        ),
        out_specs=P(("rows", "cols"), None),
        check_vma=False,
    )
```

```python
import functools
import math

import jax
import jax.numpy as jnp
from jax import lax
from jax.experimental import pallas as pl
from jax.experimental.pallas import tpu as pltpu
from jax.sharding import PartitionSpec as P


rbf_step = 2.0
rbf_width = 2.0
two_pi = 2.0 * math.pi
highest = lax.Precision.HIGHEST


def with_halo(cells, sides, width):
    for axis, dim in sides:
        count = lax.axis_size(axis)
        head = lax.slice_in_dim(cells, 0, width, axis=dim)
        tail = lax.slice_in_dim(cells, cells.shape[dim] - width, cells.shape[dim], axis=dim)
        cells = jnp.concatenate(
            [
                lax.ppermute(tail, axis, [(i, (i + 1) % count) for i in range(count)]),
                cells,
                lax.ppermute(head, axis, [((i + 1) % count, i) for i in range(count)]),
            ],
            axis=dim,
        )
    return cells


def rms_rows(values, norm_gain):
    floats = values.astype(jnp.float32)
    spread = jnp.mean(floats * floats, axis=-1, keepdims=True)
    return (floats * lax.rsqrt(spread + 1e-06) * norm_gain).astype(jnp.bfloat16)


def near_attention(
    query_rows,
    own_pos,
    keys,
    key_pos,
    shifts,
    live,
    cell_lengths,
    rbf_weight,
    rbf_offset,
    pair_weight,
):
    entries, block_len = (keys.shape[0], keys.shape[1])
    model_dim = query_rows.shape[1]
    head_count = pair_weight.shape[1]
    head_dim = model_dim // head_count
    key_coords = key_pos.transpose(1, 0, 2) + shifts.astype(jnp.float32)[:, :, None]
    key_coords = key_coords.reshape(3, entries * block_len)
    displace = (key_coords[:, None, :] - own_pos[:, :, None]) * cell_lengths[:, None, None]
    distance = jnp.sqrt(jnp.sum(displace * displace, axis=0) + 0.25)
    centers = jnp.arange(rbf_weight.shape[0], dtype=jnp.float32) * rbf_step
    radial = jnp.exp(-((distance[None] - centers[:, None, None]) ** 2) * (0.5 / rbf_width**2))
    radial = radial.reshape(rbf_weight.shape[0], -1)
    hidden = jax.nn.silu(jnp.dot(rbf_weight.T, radial, precision=highest) + rbf_offset[:, None])
    pair_bias = jnp.dot(pair_weight.T, hidden, precision=highest).reshape(
        head_count, query_rows.shape[0], entries * block_len
    )
    query_heads = query_rows.reshape(-1, head_count, head_dim)
    key_heads = keys[:, :, :model_dim].reshape(entries * block_len, head_count, head_dim)
    value_heads = keys[:, :, model_dim:].reshape(entries * block_len, head_count, head_dim)
    scores = (
        jnp.einsum("ahd,khd->hak", query_heads, key_heads, preferred_element_type=jnp.float32)
        * head_dim ** (-0.5)
        + pair_bias
    )
    allowed = jnp.repeat(live > 0, block_len)
    scores = jnp.where(allowed[None, None, :], scores, -1e30)
    row_max = jnp.max(scores, axis=-1, keepdims=True)
    weights = jnp.exp(scores - row_max)
    row_sum = jnp.sum(weights, axis=-1, keepdims=True)
    prob_bf = weights.astype(jnp.bfloat16)
    attended = jnp.einsum(
        "hak,khd->ahd", prob_bf, value_heads, preferred_element_type=jnp.float32
    ) / row_sum.transpose(1, 0, 2)
    return attended.reshape(-1, model_dim).astype(jnp.bfloat16)


def on_device(
    features,
    positions,
    cell_lengths,
    block_lists,
    image_offsets,
    block_valid,
    norm_gain,
    w_qkv,
    w_out,
    rbf_weight,
    rbf_offset,
    pair_weight,
    cosine_scale,
):
    atom_count, model_dim = features.shape
    head_count = pair_weight.shape[1]
    head_dim = model_dim // head_count
    row_count = lax.axis_size("rows")
    col_count = lax.axis_size("cols")
    row_index = lax.axis_index("rows")
    col_index = lax.axis_index("cols")
    per_dev = head_count // row_count
    normed = rms_rows(features, norm_gain)
    packed = jnp.dot(normed, w_qkv, preferred_element_type=jnp.float32).astype(jnp.bfloat16)
    every_pos = lax.all_gather(positions, ("rows", "cols"), axis=1, tiled=True)
    near_rows = with_halo(normed[None, None], (("rows", 0), ("cols", 1)), 1)
    near_kv = jnp.dot(
        near_rows.reshape(9 * atom_count, model_dim),
        w_qkv[:, model_dim:],
        preferred_element_type=jnp.float32,
    )
    near_kv = near_kv.astype(jnp.bfloat16).reshape(9, atom_count, 2 * model_dim)
    listed = block_lists[0]
    list_row = listed // col_count
    list_col = listed % col_count
    slots = (list_row - row_index + 1) % row_count * 3 + (list_col - col_index + 1) % col_count
    keys = jnp.take(near_kv, slots, axis=0)
    block_pos = every_pos.reshape(3, row_count * col_count, atom_count)
    key_pos = jnp.take(block_pos, listed, axis=1).transpose(1, 0, 2)
    local_out = near_attention(
        packed[:, :model_dim],
        positions,
        keys,
        key_pos,
        image_offsets[:, 0, :],
        block_valid[0],
        cell_lengths,
        rbf_weight,
        rbf_offset,
        pair_weight,
    )
    grouped = (
        packed.reshape(atom_count, 3, head_count, head_dim)
        .transpose(1, 2, 0, 3)
        .reshape(3, head_count, atom_count * head_dim)
    )
    regrouped = lax.all_to_all(grouped, "rows", split_axis=1, concat_axis=2, tiled=True)
    query_count = row_count * atom_count
    queries = regrouped[0].reshape(per_dev, query_count, head_dim)
    key_vals = regrouped[1:]
    cycle_pos = (
        every_pos.reshape(3, row_count, col_count, atom_count).transpose(0, 2, 1, 3).reshape(3, -1)
    )
    query_pos = lax.dynamic_slice_in_dim(cycle_pos, col_index * query_count, query_count, 1)
    cycle_feats = jnp.concatenate(
        [jnp.cos(two_pi * cycle_pos), jnp.sin(two_pi * cycle_pos)], axis=0
    )
    query_feats = jnp.concatenate(
        [jnp.cos(two_pi * query_pos), jnp.sin(two_pi * query_pos)], axis=0
    )
    strengths = lax.dynamic_slice_in_dim(cosine_scale, row_index * per_dev, per_dev)
    scale = head_dim ** (-0.5)

    def update(state, kv_block, key_start, block_len):
        run_max, run_sum, accum = state
        scores = (
            jnp.einsum("hqd,hkd->hqk", queries, kv_block[0], preferred_element_type=jnp.float32)
            * scale
        )
        coords = lax.dynamic_slice_in_dim(cycle_feats, key_start, block_len, 1)
        cos_bias = jnp.dot(query_feats.T, coords, precision=highest)
        scores = scores + strengths[:, None, None] * cos_bias[None]
        new_max = jnp.maximum(run_max, jnp.max(scores, axis=-1))
        keep_part = jnp.exp(run_max - new_max)
        weights = jnp.exp(scores - new_max[:, :, None])
        run_sum = run_sum * keep_part + jnp.sum(weights, axis=-1)
        prob_bf = weights.astype(jnp.bfloat16)
        accum = accum * keep_part[:, None, :] + jnp.einsum(
            "hqk,hkd->hdq", prob_bf, kv_block[1], preferred_element_type=jnp.float32
        )
        return (new_max, run_sum, accum)

    initial = (
        jnp.full((per_dev, query_count), -1e30, jnp.float32),
        jnp.zeros((per_dev, query_count), jnp.float32),
        jnp.zeros((per_dev, head_dim, query_count), jnp.float32),
    )
    piece = lax.all_gather(key_vals, "cols", axis=2, tiled=True)
    key_total = piece.shape[2] // head_dim
    if key_total > 1024 and key_total % 1024 == 0:
        block_len = 1024
    else:
        block_len = key_total
    block_count = key_total // block_len
    kv_blocks = piece.reshape(2, per_dev, block_count, block_len, head_dim).transpose(2, 0, 1, 3, 4)
    block_starts = jnp.arange(block_count, dtype=jnp.int32) * block_len

    def one_block(state, block_in):
        kv_block, key_start = block_in
        return (update(state, kv_block, key_start, block_len), None)

    state, _ = lax.scan(one_block, initial, (kv_blocks, block_starts))
    _, run_sum, accum = state
    head_out = (
        (accum / run_sum[:, None, :])
        .transpose(0, 2, 1)
        .astype(jnp.bfloat16)
        .reshape(per_dev, query_count * head_dim)
    )
    returned = lax.all_to_all(head_out, "rows", split_axis=1, concat_axis=0, tiled=True)
    global_out = (
        returned.reshape(head_count, atom_count, head_dim)
        .transpose(1, 0, 2)
        .reshape(atom_count, model_dim)
    )
    combined = (local_out.astype(jnp.float32) + global_out.astype(jnp.float32)).astype(jnp.bfloat16)
    updated = features.astype(jnp.float32) + jnp.dot(
        combined, w_out, preferred_element_type=jnp.float32
    )
    return updated.astype(jnp.bfloat16)


def mm(a, b, dims):
    return lax.dot_general(a, b, (dims, ((), ())), preferred_element_type=jnp.float32)


def parts_of(value, count):
    out = []
    for _ in range(count):
        part = value.astype(jnp.bfloat16)
        out.append(part)
        value = value - part.astype(jnp.float32)
    return out


def unit(rows, cols, dtype):
    r = lax.broadcasted_iota(jnp.int32, (rows, cols), 0)
    c = lax.broadcasted_iota(jnp.int32, (rows, cols), 1)
    return (r == c).astype(dtype)


def to_column(row):
    count = row.shape[1]
    r = lax.broadcasted_iota(jnp.int32, (count, count), 0)
    c = lax.broadcasted_iota(jnp.int32, (count, count), 1)
    return jnp.sum(jnp.where(r == c, jnp.broadcast_to(row, (count, count)), 0.0), axis=1, keepdims=True)


def fetch(pairs, sems):
    copies = [pltpu.make_async_copy(src, dst, sems.at[k]) for k, (src, dst) in enumerate(pairs)]
    for copy in copies:
        copy.start()
    return copies


def settle(copies):
    for copy in copies:
        copy.wait()


def pack_kernel(*refs):
    sources, out_ref, tables = refs[:11], refs[11], refs[12:20]
    feat_ref, gain_ref, pos_ref, tmp_ref, sems = refs[20:]
    copies = fetch(list(zip(sources, (feat_ref, gain_ref, pos_ref, *tables))), sems)
    settle(copies[:3])
    atoms, _ = feat_ref.shape
    floats = feat_ref[...].astype(jnp.float32)
    spread = jnp.mean(floats * floats, axis=-1, keepdims=True)
    normed = floats * lax.rsqrt(spread + 1e-06) * gain_ref[...]
    out_ref[:atoms, :] = normed.astype(jnp.bfloat16)
    tmp_ref[...] = jnp.zeros(tmp_ref.shape, jnp.float32)
    for p, part in enumerate(parts_of(pos_ref[...], 3)):
        tmp_ref[:3, p * 128 : p * 128 + atoms] = part.astype(jnp.float32)
    out_ref[atoms:, :] = tmp_ref[...].astype(jnp.bfloat16)
    settle(copies[3:])


def prepare(
    head_dim,
    wqkv_ref,
    rw_ref,
    ro_ref,
    pw_ref,
    cs_ref,
    pack_ref,
    qexp_ref,
    w1_ref,
    w2_ref,
    str_ref,
    own_ref,
):
    atoms = own_ref.shape[1]
    dim = wqkv_ref.shape[0]
    groups, rows, width = qexp_ref.shape
    per = rows // atoms
    tile = pack_ref[atoms:, :].astype(jnp.float32)
    tile = jnp.concatenate([tile[:, p * 128 : p * 128 + atoms] for p in range(3)], axis=0)
    pos = mm(unit(atoms, atoms, jnp.bfloat16), tile.astype(jnp.bfloat16), ((1,), (1,)))
    pos = jnp.concatenate([pos, jnp.zeros((atoms, 128 - 24), jnp.float32)], axis=1)
    pos = pos + pltpu.roll(pos, 120, 1) + pltpu.roll(pos, 112, 1)
    own_ref[0] = pos
    own_ref[1] = jnp.cos(two_pi * pos)
    own_ref[2] = jnp.sin(two_pi * pos)
    h, m, l = parts_of(0.5 * rw_ref[...], 3)
    hidden = rw_ref.shape[1]
    row = lax.broadcasted_iota(jnp.int32, (16, hidden), 0)
    tail = jnp.zeros((16, hidden), jnp.float32)
    for k, part in enumerate(parts_of(0.5 * ro_ref[...], 3)):
        tail = jnp.where(row == k, part.astype(jnp.float32), tail)
    stack = jnp.concatenate([h, h, m, h, l, m, tail.astype(jnp.bfloat16)], axis=0)
    w1_ref[...] = mm(unit(hidden, hidden, jnp.bfloat16), stack, ((1,), (1,))).astype(jnp.bfloat16)
    h, l = parts_of(pw_ref[...], 2)
    w2_ref[...] = jnp.concatenate([h, h, l], axis=1)
    str_ref[...] = jnp.broadcast_to(to_column(cs_ref[...]), str_ref.shape)
    q = mm(pack_ref[:atoms, :], wqkv_ref[:, :dim], ((1,), (0,)))
    q = q.astype(jnp.bfloat16).astype(jnp.float32)
    lane = lax.broadcasted_iota(jnp.int32, (per, width), 1) // head_dim
    sub = lax.broadcasted_iota(jnp.int32, (per, width), 0)
    keep = (lane == sub)[None]
    for g in range(groups):
        part = q[:, g * width : (g + 1) * width]
        spread = jnp.broadcast_to(part[:, None, :], (atoms, per, width))
        spread = jnp.where(keep, spread, 0.0).reshape(rows, width)
        qexp_ref[g] = spread.astype(jnp.bfloat16)


def position_tile(blocks, atoms, dim):
    tiles = [block[atoms:, :].astype(jnp.float32) for block in blocks]
    pad = 128 - atoms * len(blocks)
    out = []
    for p in range(3):
        part = [tile[:, p * 128 : p * 128 + atoms] for tile in tiles]
        if pad:
            part.append(jnp.zeros((8, pad), jnp.float32))
        out += part
    out.append(jnp.zeros((8, dim - 3 * 128), jnp.float32))
    return jnp.concatenate(out, axis=1).astype(jnp.bfloat16)


def repack_kernel(_, *refs):
    blocks, out_ref = refs[:-1], refs[-1]
    atoms = blocks[0].shape[0] - 8
    dim = out_ref.shape[1]
    for k, block in enumerate(blocks):
        out_ref[k * atoms : (k + 1) * atoms, :] = block[:atoms, :]
    out_ref[len(blocks) * atoms :, :] = position_tile(blocks, atoms, dim)


def piece_tiles(piece, counts):
    total = sum(counts)
    out = []
    for k in range(len(counts)):
        tail = piece[total + 8 * k : total + 8 * (k + 1), :].astype(jnp.float32)
        out.append(tail[:, :128] + tail[:, 128:256] + tail[:, 256:384])
    return out


def attend(qexps, keys, vals, scale, biases):
    rows = qexps[0].shape[0]
    count = keys[0].shape[0]
    atoms, per, _ = biases[0].shape
    scores = [mm(q, k, ((1,), (1,))) for q, k in zip(qexps, keys)]
    tops, sums, probs = [], [], []
    for s, bias3 in zip(scores, biases):
        s = s.reshape(atoms, per, count) * scale + bias3
        tops.append(jnp.max(s, axis=-1, keepdims=True))
        p = jnp.exp(s - tops[-1])
        sums.append(jnp.sum(p, axis=-1, keepdims=True))
        probs.append(p.astype(jnp.bfloat16).reshape(rows, count))
    outs = [mm(p, v, ((1,), (0,))) for p, v in zip(probs, vals)]
    return [(t, n, o.reshape(atoms, per, o.shape[-1])) for t, n, o in zip(tops, sums, outs)]


def absorb(head_dim, plan, pieces, wqkv_ref, qexp_ref, str_ref, own_ref, kv_ref):
    dim = wqkv_ref.shape[0]
    atoms = own_ref.shape[1]
    groups, rows, width = qexp_ref.shape
    per = rows // atoms
    rows_in = jnp.concatenate(
        [piece[: sum(counts), :] for piece, (_, counts) in zip(pieces, plan)], axis=0
    )
    kv = mm(rows_in, wqkv_ref[:, dim:], ((1,), (0,))).astype(jnp.bfloat16)
    at = 0
    tiles = []
    for piece, (start, counts) in zip(pieces, plan):
        kv_ref[start : start + sum(counts), :] = kv[at : at + sum(counts)]
        at += sum(counts)
        tiles += [t[:, :n] for t, n in zip(piece_tiles(piece, counts), counts)]
    pos8 = jnp.concatenate(tiles, axis=1)
    cos_k, sin_k = jnp.cos(two_pi * pos8), jnp.sin(two_pi * pos8)
    waves = None
    for c in range(3):
        term = own_ref[1, :, c : c + 1] * cos_k[c : c + 1] + own_ref[2, :, c : c + 1] * sin_k[c : c + 1]
        waves = term if waves is None else waves + term
    spans = [(g * width, (g + 1) * width) for g in range(groups)]
    return attend(
        [qexp_ref[g] for g in range(groups)],
        [kv[:, low:high] for low, high in spans],
        [kv[:, dim + low : dim + high] for low, high in spans],
        head_dim ** (-0.5),
        [
            str_ref[g * per : (g + 1) * per, :1][None] * waves[:, None, :]
            for g in range(groups)
        ],
    )


def widen(column, lanes):
    return jnp.broadcast_to(column, column.shape[:-1] + (lanes,))


def repeat_lanes(array, lanes):
    return jnp.concatenate([array] * (lanes // array.shape[-1]), axis=-1)


def core_kernel(*refs):
    blocks, ring_ref, core_ref = refs[:4], refs[4], refs[5]
    atoms = blocks[0].shape[0] - 8
    dim = core_ref.shape[1]
    four, three = 4 * atoms, 3 * atoms
    for k, block in enumerate(blocks):
        core_ref[k * atoms : (k + 1) * atoms, :] = block[:atoms, :]
    core_ref[four : four + three, :] = ring_ref[:three, :]
    core_ref[four + three : four + three + 8, :] = position_tile(blocks, atoms, dim)
    core_ref[four + three + 8 :, :] = ring_ref[three:, :]


def first_kernel(head_dim, plan, *refs):
    pack_ref, core_ref, wqkv_ref, tables = refs[0], refs[1], refs[2], refs[3:7]
    kv_ref, acc_ref, top_ref, sum_ref, qexp_ref, w1_ref, w2_ref, str_ref, own_ref = refs[7:]
    prepare(head_dim, wqkv_ref, *tables, pack_ref, qexp_ref, w1_ref, w2_ref, str_ref, own_ref)
    got = absorb(head_dim, plan, (core_ref,), wqkv_ref, qexp_ref, str_ref, own_ref, kv_ref)
    for g, (top, total, o) in enumerate(got):
        acc_ref[g] = o
        top_ref[g] = widen(top, 128)
        sum_ref[g] = widen(total, 128)


def merge(got, g, acc_ref, top_ref, sum_ref):
    top, total, o = got[g]
    width = o.shape[-1]
    best = jnp.maximum(widen(top, 128), top_ref[g])
    a, b = jnp.exp(top_ref[g] - best), jnp.exp(widen(top, 128) - best)
    summed = a * sum_ref[g] + b * widen(total, 128)
    acc = repeat_lanes(a, width) * acc_ref[g] + repeat_lanes(b, width) * o
    return best, summed, acc


def next_kernel(head_dim, plan, *refs):
    pieces = refs[: len(plan)]
    wqkv_ref, qexp_ref, str_ref, own_ref = refs[len(plan) : len(plan) + 4]
    _, acc_in, top_in, sum_in, kv_ref, acc_ref, top_ref, sum_ref = refs[len(plan) + 4 :]
    got = absorb(head_dim, plan, pieces, wqkv_ref, qexp_ref, str_ref, own_ref, kv_ref)
    for g in range(len(got)):
        best, summed, acc = merge(got, g, acc_in, top_in, sum_in)
        acc_ref[g] = acc
        top_ref[g] = best
        sum_ref[g] = summed


def chosen(row, lane):
    out = jnp.broadcast_to(row[:, :1], lane.shape)
    for e in range(1, row.shape[1]):
        out = jnp.where(lane == e, row[:, e : e + 1], out)
    return out


def pair_distance(near, shifts, own_ref, cell_ref):
    square = None
    for c in range(3):
        gap = (near[c : c + 1] + shifts[c] - own_ref[0, :, c : c + 1]) * cell_ref[:, c : c + 1]
        square = gap * gap if square is None else square + gap * gap
    return jnp.sqrt(square + 0.25)


def pair_stage(dist, w1_ref, w2_ref, bias_ref, step):
    atoms, listed = dist.shape
    groups, _, per, _ = bias_ref.shape
    nrbf = (w1_ref.shape[1] - 16) // 6
    centers = lax.broadcasted_iota(jnp.int32, (nrbf, 1), 0).astype(jnp.float32) * rbf_step
    ones = jnp.ones((16, step * listed), jnp.bfloat16)
    for i in range(0, atoms, step):
        gap = jnp.concatenate([dist[j : j + 1] - centers for j in range(i, i + step)], axis=1)
        radial = jnp.exp(gap * gap * (-0.5 / rbf_width**2))
        h, m, l = parts_of(radial, 3)
        stack = jnp.concatenate([h, m, h, l, h, m, ones], axis=0)
        u = mm(w1_ref[...], stack, ((1,), (0,)))
        u = u + u * jnp.tanh(u)
        h, l = parts_of(u, 2)
        pair = mm(w2_ref[...], jnp.concatenate([h, l, h], axis=0), ((1,), (0,)))
        for j in range(step):
            for g in range(groups):
                bias_ref[g, i + j] = pair[g * per : (g + 1) * per, j * listed : (j + 1) * listed]


def turned_tile(pos_ref, tile, spot, into, atoms):
    return pltpu.roll(pos_ref[tile], (into - spot + 128 // atoms) % (128 // atoms) * atoms, 1)


def mid_kernel(head_dim, locate, plans, col_count, list_ref, shift_ref, cell_ref, *refs):
    w1_ref, w2_ref, core_ref = refs[:3]
    core2_ref, own_ref = refs[3], refs[7]
    *rest, bias_ref, pos_ref = refs[3:]
    atoms = own_ref.shape[1]
    pos_ref[0] = piece_tiles(core_ref, plans[0][1])[0]
    pos_ref[1] = piece_tiles(core2_ref, plans[1][1])[0]
    me = lax.axis_index("rows") * col_count + lax.axis_index("cols")
    entries = list_ref.shape[1]
    in_tile = lax.broadcasted_iota(jnp.int32, (1, 128), 1) // atoms
    tiles = []
    for e in range(entries):
        _, _, spot, turn, _ = locate(jnp.sum(list_ref[:, e : e + 1]) ^ me)
        into = e % (128 // atoms)
        moved = turned_tile(pos_ref, turn, spot, into, atoms)
        if into == 0:
            tiles.append(moved)
        else:
            tiles[-1] = jnp.where(in_tile == into, moved, tiles[-1])
    lane = lax.broadcasted_iota(jnp.int32, (1, entries * atoms), 1) // atoms
    shifts = [chosen(shift_ref[c].astype(jnp.float32), lane) for c in range(3)]
    dist = pair_distance(jnp.concatenate(tiles, axis=1), shifts, own_ref, cell_ref)
    pair_stage(dist, w1_ref, w2_ref, bias_ref, 16)
    next_kernel(head_dim, plans[1:], *rest)


def last_kernel(head_dim, locate, plan, col_count, list_ref, valid_ref, shift_ref, cell_ref, *refs):
    piece_refs = refs[:8]
    (
        wqkv_ref,
        qexp_ref,
        str_ref,
        own_ref,
        w1_ref,
        w2_ref,
        wout_ref,
        in_ref,
        early_ref,
        _,
        acc_in,
        top_in,
        sum_in,
        out_ref,
        kv_ref,
        near_ref,
        pos_ref,
        bias_ref,
    ) = refs[8:]
    dim = wqkv_ref.shape[0]
    atoms = own_ref.shape[1]
    groups, rows, width = qexp_ref.shape
    per = rows // atoms
    got = absorb(head_dim, plan[7:], piece_refs[7:], wqkv_ref, qexp_ref, str_ref, own_ref, kv_ref)
    at = 0
    for piece, (_, counts) in zip(piece_refs, plan):
        for tile in piece_tiles(piece, counts):
            pos_ref[at] = tile
            at += 1
    me = lax.axis_index("rows") * col_count + lax.axis_index("cols")
    entries = list_ref.shape[1]
    listed = entries * atoms
    late_count = 128 // atoms
    lane = lax.broadcasted_iota(jnp.int32, (1, listed), 1) // atoms
    in_tile = lax.broadcasted_iota(jnp.int32, (1, 128), 1) // atoms
    seen = jnp.int32(0)
    late = [[jnp.int32(0), jnp.int32(0), jnp.int32(0), jnp.int32(-1)] for _ in range(late_count)]
    early_live = jnp.zeros((1, listed), jnp.int32)
    for e in range(entries):
        slot, tile, spot, _, far = locate(jnp.sum(list_ref[:, e : e + 1]) ^ me)
        start = pl.multiple_of(slot * atoms, atoms)
        near_ref[e * atoms : (e + 1) * atoms, :] = kv_ref[pl.ds(start, atoms), :]
        early_live = jnp.where(lane == e, 1 - far, early_live)
        for k in range(late_count):
            hit = (far == 1) & (seen == k)
            found = (slot, tile, spot, jnp.int32(e))
            late[k] = [jnp.where(hit, new, old) for new, old in zip(found, late[k])]
        seen = seen + far
    near = None
    which = jnp.full((1, 128), -1, jnp.int32)
    for k, (slot, tile, spot, entry) in enumerate(late):
        start = pl.multiple_of(slot * atoms, atoms)
        near_ref[listed + k * atoms : listed + (k + 1) * atoms, :] = kv_ref[pl.ds(start, atoms), :]
        moved = turned_tile(pos_ref, tile, spot, k, atoms)
        near = moved if near is None else jnp.where(in_tile == k, moved, near)
        which = jnp.where(in_tile == k, entry, which)

    def late_row(row):
        out = jnp.zeros((1, 128), row.dtype)
        for e in range(entries):
            out = jnp.where(which == e, row[:, e : e + 1], out)
        return out

    shifts = [late_row(shift_ref[c].astype(jnp.float32)) for c in range(3)]
    pair_stage(pair_distance(near, shifts, own_ref, cell_ref), w1_ref, w2_ref, bias_ref, atoms)
    live = jnp.concatenate(
        [chosen(valid_ref[...], lane) * early_live, late_row(valid_ref[...])], axis=1
    )
    live = (live > 0)[None]
    listed = listed + 128
    block = lax.broadcasted_iota(jnp.int32, (1, per, width), 2) // head_dim
    keep = block == lax.broadcasted_iota(jnp.int32, (1, per, width), 1)
    spans = [(g * width, (g + 1) * width) for g in range(groups)]
    scores = [mm(qexp_ref[g], near_ref[:, low:high], ((1,), (1,))) for g, (low, high) in enumerate(spans)]
    fars = []
    for g in range(groups):
        _, summed, far = merge(got, g, acc_in, top_in, sum_in)
        far = far * repeat_lanes(1.0 / summed, width)
        fars.append(jnp.sum(jnp.where(keep, far, 0.0), axis=1).astype(jnp.bfloat16))
    probs, sums = [], []
    for g in range(groups):
        s = scores[g].reshape(atoms, per, listed) * head_dim ** (-0.5) + jnp.concatenate(
            [early_ref[g], bias_ref[g]], axis=-1
        )
        s = jnp.where(live, s, -1e30)
        p = jnp.exp(s - jnp.max(s, axis=-1, keepdims=True))
        sums.append(1.0 / jnp.sum(p, axis=-1, keepdims=True))
        probs.append(p.astype(jnp.bfloat16).reshape(rows, listed))
    outs = [mm(probs[g], near_ref[:, dim + low : dim + high], ((1,), (0,))) for g, (low, high) in enumerate(spans)]
    pieces = []
    for g in range(groups):
        o = outs[g].reshape(atoms, per, width) * sums[g]
        close = jnp.sum(jnp.where(keep, o, 0.0), axis=1).astype(jnp.bfloat16)
        pieces.append((close.astype(jnp.float32) + fars[g].astype(jnp.float32)).astype(jnp.bfloat16))
    combined = jnp.concatenate(pieces, axis=1)
    moved = mm(combined, wout_ref[...], ((1,), (0,)))
    out_ref[...] = (in_ref[...].astype(jnp.float32) + moved).astype(jnp.bfloat16)


def call(kernel, outs, scratch, smem, args, aliases=None, hbm=0):
    vmem = pl.BlockSpec(memory_space=pltpu.VMEM)
    first = smem + hbm
    specs = [pl.BlockSpec(memory_space=pltpu.SMEM)] * smem
    specs += [pl.BlockSpec(memory_space=pltpu.HBM)] * hbm + [vmem] * (len(args) - first)
    placed = [pltpu.with_memory_space_constraint(a, pltpu.HBM) for a in args[smem:first]]
    placed += [pltpu.with_memory_space_constraint(a, pltpu.VMEM) for a in args[first:]]
    many = isinstance(outs, list)
    return pl.pallas_call(
        kernel,
        out_shape=outs,
        in_specs=specs,
        out_specs=[vmem] * len(outs) if many else vmem,
        scratch_shapes=scratch,
        input_output_aliases=aliases or {},
        compiler_params=pltpu.CompilerParams(vmem_limit_bytes=24 << 20),
    )(*args[:smem], *placed)


def on_device_small(
    features,
    positions,
    cell_lengths,
    block_lists,
    image_offsets,
    block_valid,
    norm_gain,
    w_qkv,
    w_out,
    rbf_weight,
    rbf_offset,
    pair_weight,
    cosine_scale,
):
    atoms, dim = features.shape
    heads = pair_weight.shape[1]
    hidden = pair_weight.shape[0]
    nrbf = rbf_weight.shape[0]
    head_dim = dim // heads
    row_count = lax.axis_size("rows")
    col_count = lax.axis_size("cols")
    total = row_count * col_count
    axes = ("rows", "cols")
    col_bits = col_count.bit_length() - 1
    flip = 1 << col_bits
    across_bits = (0, col_bits + 1)
    entries = block_lists.shape[1]
    width = 256
    per = width // head_dim
    groups = heads // per
    rows = atoms * per
    f32, bf16 = jnp.float32, jnp.bfloat16
    vm = pltpu.VMEM

    def swap(array, mask):
        return lax.ppermute(array, axes, [(i, i ^ mask) for i in range(total)])

    def locate(rel):
        up = (rel >> 1) & 3
        across = (rel & 1) + 2 * ((rel >> across_bits[1]) & 1)
        turn = (rel >> col_bits) & 1
        turn = turn ^ jnp.minimum(up, 1) ^ jnp.minimum(across, 1)
        far = jnp.minimum(up, 1)
        slot = turn * 16 + across + far * (3 + 2 * across + up)
        tile = turn * 5 + far * (1 + across)
        spot = across + far * (up - 1 - across)
        return slot, tile, spot, turn, far

    tied = lax.optimization_barrier
    tables = (rbf_weight, rbf_offset[None], pair_weight.T, cosine_scale[None])
    tables += (block_lists, block_valid, image_offsets, cell_lengths[None])
    pack, *tables = call(
        pack_kernel,
        [vm((atoms + 8, dim), bf16)] + [vm(table.shape, table.dtype) for table in tables],
        [
            vm((atoms, dim), bf16),
            vm((1, dim), f32),
            vm(positions.shape, f32),
            vm((8, dim), f32),
            pltpu.SemaphoreType.DMA((11,)),
        ],
        0,
        (features, norm_gain[None], positions, *tables),
        hbm=11,
    )
    across_masks = {"e": 1 | flip, "n": (1 << across_bits[1]) | flip}
    across_masks["d"] = 1 | across_masks["n"]
    ups = [swap(pack, (d << 1) | flip) for d in (1, 2, 3)]
    owns = [swap(pack, mask) for mask in across_masks.values()]
    four, three = 4 * atoms, 3 * atoms
    ring = call(repack_kernel, vm((three + 8, dim), bf16), [], 0, (w_qkv, *ups), hbm=1)
    east, north, diag = [swap(ring, mask) for mask in across_masks.values()]
    state_shapes = [
        vm((total * atoms, 2 * dim), bf16),
        vm((groups, atoms, per, width), f32),
        vm((groups, atoms, per, 128), f32),
        vm((groups, atoms, per, 128), f32),
    ]
    half = total // 2 * atoms
    plan = [(0, (four, three))] + [(four + k * three, (three,)) for k in (1, 2, 3)]
    plan += [(half + start, counts) for start, counts in plan]

    core = call(core_kernel, vm((four + three + 16, dim), bf16), [], 0, (pack, *owns, ring))
    core2 = swap(core, flip)
    kv, acc, top, summed, qexp, w1, w2, strength, own = call(
        functools.partial(first_kernel, head_dim, plan[:1]),
        state_shapes
        + [
            vm((groups, rows, width), bf16),
            vm((hidden, 6 * nrbf + 16), bf16),
            vm((heads, 3 * hidden), bf16),
            vm((heads, 128), f32),
            vm((3, atoms, 128), f32),
        ],
        [],
        0,
        (pack, core, w_qkv, *tables[:4]),
    )
    state = (kv, acc, top, summed)
    common = (w_qkv, qexp, strength, own)

    def step(places, pieces, state):
        at = len(pieces) + len(common)
        return call(
            functools.partial(next_kernel, head_dim, [plan[k] for k in places]),
            state_shapes,
            [],
            0,
            (*pieces, *common, *state),
            {at + k: k for k in range(4)},
        )

    core2, state = tied((core2, state))
    lists, valid, offsets, cells = tables[4:]
    *state, early = call(
        functools.partial(mid_kernel, head_dim, locate, [plan[0], plan[4]], col_count),
        state_shapes + [vm((groups, atoms, per, entries * atoms), f32)],
        [vm((2, 8, 128), f32)],
        0,
        (lists, offsets, cells, w1, w2, core, core2, *common, *state),
        {3 + 4 + len(common) + k: k for k in range(4)},
    )
    east, north, state = tied((east, north, state))
    east2, north2 = swap(east, flip), swap(north, flip)
    state = step((1, 2), (east, north), state)
    diag, state = tied((diag, state))
    diag2 = swap(diag, flip)
    state = step((3, 5, 6), (diag, east2, north2), state)
    diag2, state = tied((diag2, state))
    updated, _ = call(
        functools.partial(last_kernel, head_dim, locate, plan, col_count),
        [jax.ShapeDtypeStruct((atoms, dim), bf16), state_shapes[0]],
        [
            vm((entries * atoms + 128, 2 * dim), bf16),
            vm((10, 8, 128), f32),
            vm((groups, atoms, per, 128), f32),
        ],
        0,
        (
            lists,
            valid,
            offsets,
            cells,
            core,
            east,
            north,
            diag,
            core2,
            east2,
            north2,
            diag2,
            *common,
            w1,
            w2,
            w_out,
            features,
            early,
            *state,
        ),
        {4 + 8 + len(common) + 5: 1},
    )
    return updated


def solution(mesh):
    row_count, col_count = mesh.shape["rows"], mesh.shape["cols"]
    small = (row_count, col_count) == (4, 8)
    body = on_device_small if small else on_device
    return jax.shard_map(
        body,
        mesh=mesh,
        in_specs=(
            P(("rows", "cols"), None),
            P(None, ("rows", "cols")),
            P(),
            P(("rows", "cols"), None),
            P(None, ("rows", "cols"), None),
            P(("rows", "cols"), None),
            P(),
            P(),
            P(),
            P(),
            P(),
            P(),
            P(),
        ),
        out_specs=P(("rows", "cols"), None),
        check_vma=False,
    )
```
